256 devices in a mesh: req: 8 (over y, core), blk: 32 (over z, x).
Axes of the slice: x: 4, y: 4, z: 8, core: 2. Of those that a mesh axis runs over, the one named last changes fastest.
Arguments:
- hidden: bfloat16 [320, 2048], P('req'), may hold values from -6 to 6
- attn_gain: bfloat16 [2048], replicated, may hold values from 0.099609375 to 1.8984375
- ffn_gain: bfloat16 [2048], replicated, may hold values from 0.099609375 to 1.8984375
- shared_weight: bfloat16 [2048, 2048], P(None, 'blk'), may hold values from -0.125 to 0.125
- w_dt: bfloat16 [2048, 48], replicated, may hold values from -0.125 to 0.125
- dt_bias: float32 [48], replicated, may hold values from -4 to 0.5
- a_log: float32 [48], replicated, may hold values from -2 to 2.5
- d_skip: float32 [48], replicated, may hold values from 0.5 to 2
- w_inner_x: bfloat16 [2048, 3072], P(None, 'blk'), may hold values from -0.125 to 0.125
- w_inner_z: bfloat16 [2048, 3072], P(None, 'blk'), may hold values from -0.125 to 0.125
- w_attn_out: bfloat16 [1024, 2048], P('blk'), may hold values from -0.1875 to 0.1875
- w_ssm_out: bfloat16 [3072, 2048], P('blk'), may hold values from -0.21875 to 0.21875
- w_gate: bfloat16 [2048, 4096], P(None, 'blk'), may hold values from -0.125 to 0.125
- w_up: bfloat16 [2048, 4096], P(None, 'blk'), may hold values from -0.125 to 0.125
- w_down: bfloat16 [4096, 2048], P('blk'), may hold values from -0.1875 to 0.1875
- key_value_cache: bfloat16 [64, 16384, 512], P('req', 'blk'), may hold values from -400 to 400
- cache_len: int32 [64], P('req'), may hold values from 1 to 16384, as said below
- accepted: int32 [64], P('req'), may hold values from 1 to 5
- parked: float32 [64, 3072, 256], P('req', 'blk'), may hold values from -6 to 6
- source_slot: int32 [64], replicated, may hold values from 0 to 63, as said below
Outputs:
- hidden_out: bfloat16 [320, 2048], P('req', 'blk')
- new_kv: bfloat16 [64, 5, 512], P('req')
- ssm_states: float32 [64, 3072, 256], P('req', 'blk')
The draws below stay inside these ranges and needn't reach their ends.
Inputs may be any that keep to these rules, and one draw needn't show every extreme that they name: `cache_len`: some request has exactly 16384 earlier positions. `source_slot`: every slot is used by exactly one request; the first 2 requests of each index of req continue their own slots; the other 6 continue slots on other indices of req, exactly 2 from each of three distinct other indices.
All inputs are finite; a program needn't handle non-finite values.
Results may differ from the reference program's by a relative error of at most 0.019.
Values may be sent and summed in bfloat16 or wider, within the bound.
A program may use at most 64 MiB of HBM per device.

```python
import jax
import jax.numpy as jnp
from jax import lax

MODEL_WIDTH = 2048
QUERY_HEADS = 8
KEY_VALUE_HEADS = 2
HEAD_SIZE = 128
H = 48
P_SIZE = 64
STATE_SIZE = 256
FF = 4096
VERIFY_POSITIONS = 5
REQ_DEV = 8
REQS = 64
CACHE_POSITIONS = 16384


def draw_key_value_cache(key, part):
    total_width = 2 * KEY_VALUE_HEADS * HEAD_SIZE
    key_columns = jnp.arange(total_width) < KEY_VALUE_HEADS * HEAD_SIZE
    noise_base = jax.random.normal(jax.random.fold_in(key, 11), (REQS, CACHE_POSITIONS, total_width), jnp.float32)
    common_dir = jax.random.normal(jax.random.fold_in(key, 15), (REQS, 1, total_width), jnp.float32)
    fraction = jnp.arange(CACHE_POSITIONS).astype(jnp.float32) / max(CACHE_POSITIONS - 1, 1)
    ramp = 1.0 + 5.0 * fraction
    value_part = (common_dir + noise_base) * ramp[None, :, None]
    noise_base = jnp.where(key_columns[None, None, :], noise_base, value_part)
    return jnp.clip(noise_base, -400.0, 400.0).astype(jnp.bfloat16)


def draw_cache_len(key, part):
    lengths = jax.random.randint(jax.random.fold_in(key, 21), (REQS,), 1, CACHE_POSITIONS + 1)
    chosen = jax.random.randint(jax.random.fold_in(key, 22), (), 0, REQS)
    return jnp.where(jnp.arange(REQS) == chosen, CACHE_POSITIONS, lengths).astype(jnp.int32)


def draw_source_slot(key, part):
    groups = REQS // REQ_DEV
    shifts = jax.random.permutation(jax.random.fold_in(key, 31), groups - 1) + 1
    group_id = jnp.arange(REQS) // REQ_DEV
    inner_id = jnp.arange(REQS) % REQ_DEV
    column = jnp.clip((inner_id - 2) // 2, 0, 2)
    shifts_used = shifts[column]
    remote = (group_id + shifts_used) % groups * REQ_DEV + inner_id
    return jnp.where(inner_id < 2, jnp.arange(REQS), remote).astype(jnp.int32)


def with_ends(result, stream_key, smallest, largest):
    longest = result.shape.index(max(result.shape))
    spots = []
    for shift in (0, 1):
        where = [jax.random.randint(jax.random.fold_in(stream_key, axis), (), 0, length) for axis, length in enumerate(result.shape)]
        where[longest] = (where[longest] + shift) % result.shape[longest]
        spots.append(tuple(where))
    return result.at[spots[0]].set(smallest).at[spots[1]].set(largest)


def raised(array, own_key, source, target, parts, factor):
    def block_of(dim):
        return (jnp.arange(array.shape[dim]) // (array.shape[dim] // parts)).reshape((-1,) + (1,) * (array.ndim - 1 - dim))

    first = jax.random.permutation(own_key, parts)[block_of(target)]
    other_side = (block_of(target) + parts // 2) % parts
    return jnp.where((block_of(source) == first) | (block_of(source) == other_side), factor * array, array)


def level_of(key, dims, cuts, smallest, high):
    gain, own = 1.0, jax.random.fold_in(key, 6)
    for dim, blocks in cuts:
        steps = jnp.exp(jax.random.uniform(jax.random.fold_in(own, dim), (blocks,), jnp.float32, smallest / len(cuts), high / len(cuts)))
        gain = gain * jnp.repeat(steps, dims[dim] // blocks).reshape([-1 if axis == dim else 1 for axis in range(len(dims))])
    return gain


def normal_values(own_key, shape, scale, bound, shards=(), kind=jnp.bfloat16):
    drawn = jax.random.normal(own_key, shape, jnp.float32) * scale
    if len(shards) > 0:
        drawn = level_of(own_key, shape, shards, -0.22, 0.18) * drawn
    return jnp.clip(drawn, min=-bound, max=bound).astype(kind)


def heavy_noise(own_key, dims, width, limit, pieces, heavy, held_as=jnp.bfloat16):
    array = width * jax.random.normal(own_key, dims, jnp.float32)
    if pieces:
        array = array * level_of(own_key, dims, pieces, -0.22, 0.18)
    return jnp.clip(raised(array, jax.random.fold_in(own_key, 3), *heavy), -limit, limit).astype(held_as)


def setup_inputs(seed: int = 0) -> dict:
    arg_keys = jax.random.split(jax.random.key(seed), 21)
    return {
        "hidden": normal_values(arg_keys[0], (REQS * VERIFY_POSITIONS, MODEL_WIDTH), 1.0, 6.0, ((0, 8),)),
        "attn_gain": jnp.clip(1.0 + 0.18 * jax.random.normal(arg_keys[1], (MODEL_WIDTH,), jnp.float32), 0.099609375, 1.8984375).astype(jnp.bfloat16),
        "ffn_gain": jnp.clip(1.0 + 0.18 * jax.random.normal(arg_keys[2], (MODEL_WIDTH,), jnp.float32), 0.099609375, 1.8984375).astype(jnp.bfloat16),
        "shared_weight": normal_values(arg_keys[3], (MODEL_WIDTH, (QUERY_HEADS + 2 * KEY_VALUE_HEADS) * HEAD_SIZE + 2 * STATE_SIZE), MODEL_WIDTH ** -0.5, 0.125, ((1, 32),)),
        "w_dt": normal_values(arg_keys[4], (MODEL_WIDTH, H), MODEL_WIDTH ** -0.5, 0.125),
        "dt_bias": jnp.clip(jax.random.uniform(arg_keys[5], (H,), jnp.float32, -4.0, 0.5), -4.0, 0.5),
        "a_log": jnp.clip(jax.random.uniform(arg_keys[6], (H,), jnp.float32, -2.0, 2.5), -2.0, 2.5),
        "d_skip": jnp.clip(jax.random.uniform(arg_keys[7], (H,), jnp.float32, 0.5, 2.0), 0.5, 2.0),
        "w_inner_x": normal_values(arg_keys[8], (MODEL_WIDTH, H * P_SIZE), MODEL_WIDTH ** -0.5, 0.125, ((1, 32),)),
        "w_inner_z": normal_values(arg_keys[9], (MODEL_WIDTH, H * P_SIZE), MODEL_WIDTH ** -0.5, 0.125, ((1, 32),)),
        "w_attn_out": normal_values(arg_keys[10], (QUERY_HEADS * HEAD_SIZE, MODEL_WIDTH), (QUERY_HEADS * HEAD_SIZE) ** -0.5, 0.1875, ((0, 32),)),
        "w_ssm_out": heavy_noise(arg_keys[11], (H * P_SIZE, MODEL_WIDTH), (H * P_SIZE) ** -0.5, 0.21875, ((0, 32),), (0, 1, 32, 2.75)),
        "w_gate": normal_values(arg_keys[12], (MODEL_WIDTH, FF), MODEL_WIDTH ** -0.5, 0.125, ((1, 32),)),
        "w_up": normal_values(arg_keys[13], (MODEL_WIDTH, FF), MODEL_WIDTH ** -0.5, 0.125, ((1, 32),)),
        "w_down": heavy_noise(arg_keys[14], (FF, MODEL_WIDTH), FF ** -0.5, 0.1875, ((0, 32),), (0, 1, 32, 2.75)),
        "key_value_cache": draw_key_value_cache(jax.random.fold_in(arg_keys[20], 71), 0),
        "cache_len": draw_cache_len(jax.random.fold_in(arg_keys[20], 71), 0),
        "accepted": with_ends(jax.random.randint(arg_keys[17], (REQS,), 1, VERIFY_POSITIONS + 1), jax.random.fold_in(arg_keys[17], 1), 1, VERIFY_POSITIONS).astype(jnp.int32),
        "parked": normal_values(arg_keys[18], (REQS, H * P_SIZE, STATE_SIZE), 1.0, 6.0, ((0, 8), (1, 32)), jnp.float32),
        "source_slot": draw_source_slot(jax.random.fold_in(arg_keys[20], 71), 0),
    }


EPSILON = 1e-05
ROPE_THETA = 100000000000.0
NEGATIVE = -1e+30

def rounded_values(values):
    return lax.optimization_barrier(values.astype(jnp.bfloat16))

def rms_norm(values, gain_vec):
    float_numbers = values.astype(jnp.float32)
    scaling = lax.rsqrt(lax.optimization_barrier(jnp.mean(float_numbers * float_numbers, axis=-1, keepdims=True)) + EPSILON)
    return (float_numbers * scaling * gain_vec.astype(jnp.float32)).astype(jnp.bfloat16)

def apply_rotary(values, token_positions):
    half_width = values.shape[-1] // 2
    frequency = ROPE_THETA ** (-(jnp.arange(half_width).astype(jnp.float32) * 2.0 / values.shape[-1]))
    angles = token_positions.astype(jnp.float32)[..., None, None] * frequency
    cosine = jnp.cos(angles)
    sine_part = jnp.sin(angles)
    lower_half = values[..., :half_width]
    upper_half = values[..., half_width:]
    return jnp.concatenate([lower_half * cosine - upper_half * sine_part, upper_half * cosine + lower_half * sine_part], axis=-1)

def split_projection(shared_projection, cache_len, item_count):
    query_width = QUERY_HEADS * HEAD_SIZE
    key_value_width = KEY_VALUE_HEADS * HEAD_SIZE
    token_positions = cache_len[:, None] + jnp.arange(VERIFY_POSITIONS, dtype=jnp.int32)[None, :]
    float_numbers = shared_projection.astype(jnp.float32)
    query_rows = rounded_values(apply_rotary(float_numbers[:, :query_width].reshape(item_count, VERIFY_POSITIONS, QUERY_HEADS, HEAD_SIZE), token_positions))
    drafted_keys = rounded_values(apply_rotary(float_numbers[:, query_width:query_width + key_value_width].reshape(item_count, VERIFY_POSITIONS, KEY_VALUE_HEADS, HEAD_SIZE), token_positions))
    drafted_values = shared_projection[:, query_width + key_value_width:query_width + 2 * key_value_width].reshape(item_count, VERIFY_POSITIONS, KEY_VALUE_HEADS, HEAD_SIZE)
    b_start = query_width + 2 * key_value_width
    b_rows = float_numbers[:, b_start:b_start + STATE_SIZE].reshape(item_count, VERIFY_POSITIONS, STATE_SIZE)
    c_rows = float_numbers[:, b_start + STATE_SIZE:b_start + 2 * STATE_SIZE].reshape(item_count, VERIFY_POSITIONS, STATE_SIZE)
    return (query_rows, drafted_keys, drafted_values, b_rows, c_rows)

def attend_request(packed):
    query_rows, drafted_keys, drafted_values, earlier_rows, length = packed
    key_value_width = KEY_VALUE_HEADS * HEAD_SIZE
    joined_keys = jnp.concatenate([earlier_rows[:, :key_value_width].reshape(CACHE_POSITIONS, KEY_VALUE_HEADS, HEAD_SIZE), drafted_keys], axis=0).astype(jnp.float32)
    joined_values = jnp.concatenate([earlier_rows[:, key_value_width:].reshape(CACHE_POSITIONS, KEY_VALUE_HEADS, HEAD_SIZE), drafted_values], axis=0).astype(jnp.float32)
    query_groups = query_rows.astype(jnp.float32).reshape(VERIFY_POSITIONS, KEY_VALUE_HEADS, QUERY_HEADS // KEY_VALUE_HEADS, HEAD_SIZE)
    scores = jnp.einsum('tkgd,skd->tkgs', query_groups, joined_keys) * HEAD_SIZE ** (-0.5)
    columns = jnp.arange(CACHE_POSITIONS + VERIFY_POSITIONS)
    rows_t = jnp.arange(VERIFY_POSITIONS)
    usable = jnp.where(columns[None, :] < CACHE_POSITIONS, columns[None, :] < length, columns[None, :] - CACHE_POSITIONS <= rows_t[:, None])
    usable = usable[:, None, None, :]
    peak = lax.optimization_barrier(jnp.max(jnp.where(usable, scores, NEGATIVE), axis=-1, keepdims=True))
    weights = jnp.where(usable, jnp.exp(scores - peak), 0.0)
    totals = lax.optimization_barrier(jnp.sum(weights, axis=-1))
    mixture = jnp.einsum('tkgs,skd->tkgd', rounded_values(weights).astype(jnp.float32), joined_values)
    return (mixture / totals[..., None]).astype(jnp.bfloat16).reshape(VERIFY_POSITIONS, QUERY_HEADS * HEAD_SIZE)

def reference(hidden, attn_gain, ffn_gain, shared_weight, w_dt, dt_bias, a_log, d_skip, w_inner_x, w_inner_z, w_attn_out, w_ssm_out, w_gate, w_up, w_down, key_value_cache, cache_len, accepted, parked, source_slot):
    item_count = cache_len.shape[0]
    normed = rms_norm(hidden, attn_gain)
    shared_projection = jnp.dot(normed, shared_weight, preferred_element_type=jnp.float32).astype(jnp.bfloat16)
    query_rows, drafted_keys, drafted_values, b_rows, c_rows = split_projection(shared_projection, cache_len, item_count)
    attended = lax.map(attend_request, (query_rows, drafted_keys, drafted_values, key_value_cache, cache_len)).reshape(item_count * VERIFY_POSITIONS, QUERY_HEADS * HEAD_SIZE)
    step_size = jax.nn.softplus(jnp.dot(normed, w_dt, preferred_element_type=jnp.float32) + dt_bias)
    inner_x = jnp.dot(normed, w_inner_x, preferred_element_type=jnp.float32)
    inner_z = jnp.dot(normed, w_inner_z, preferred_element_type=jnp.float32)
    rate_c = jnp.repeat(-jnp.exp(a_log), P_SIZE)
    skip_c = jnp.repeat(d_skip, P_SIZE)
    step_c = jnp.repeat(step_size, P_SIZE, axis=1)
    starts = jnp.take(parked, source_slot, axis=0)

    def scan_request(packed):
        carried, step_rows, input_rows, b_part, c_part, keep_count = packed
        kept_state = jnp.zeros_like(carried)
        outputs = []
        for step in range(VERIFY_POSITIONS):
            carried = jnp.exp(step_rows[step] * rate_c)[:, None] * carried + (step_rows[step] * input_rows[step])[:, None] * b_part[step][None, :]
            outputs.append(lax.optimization_barrier(jnp.sum(carried * c_part[step][None, :], axis=-1)) + skip_c * input_rows[step])
            kept_state = jnp.where(keep_count == step + 1, carried, kept_state)
        return (jnp.stack(outputs), kept_state)
    outputs, ssm_states = lax.map(scan_request, (starts, step_c.reshape(item_count, VERIFY_POSITIONS, -1), inner_x.reshape(item_count, VERIFY_POSITIONS, -1), b_rows, c_rows, accepted))
    gated = (outputs.reshape(item_count * VERIFY_POSITIONS, -1) * jax.nn.silu(inner_z)).astype(jnp.bfloat16)
    mixer = jnp.dot(attended, w_attn_out, preferred_element_type=jnp.float32) + jnp.dot(gated, w_ssm_out, preferred_element_type=jnp.float32)
    resid = (hidden.astype(jnp.float32) + mixer).astype(jnp.bfloat16)
    normed_ff = rms_norm(resid, ffn_gain)
    gate_val = jnp.dot(normed_ff, w_gate, preferred_element_type=jnp.float32)
    up_val = jnp.dot(normed_ff, w_up, preferred_element_type=jnp.float32)
    inner_ff = (jax.nn.silu(gate_val) * up_val).astype(jnp.bfloat16)
    hidden_out = (resid.astype(jnp.float32) + jnp.dot(inner_ff, w_down, preferred_element_type=jnp.float32)).astype(jnp.bfloat16)
    newest_rows = jnp.concatenate([drafted_keys.reshape(item_count, VERIFY_POSITIONS, KEY_VALUE_HEADS * HEAD_SIZE), drafted_values.reshape(item_count, VERIFY_POSITIONS, KEY_VALUE_HEADS * HEAD_SIZE)], axis=-1)
    keep_rows = jnp.arange(VERIFY_POSITIONS, dtype=jnp.int32)[None, :] < accepted[:, None]
    new_kv = jnp.where(keep_rows[:, :, None], newest_rows, jnp.zeros_like(newest_rows))
    return (hidden_out, new_kv, ssm_states)
```

```python
import math

import jax
import jax.numpy as jnp
import numpy as np
from jax import lax
from jax.experimental import pallas as pl
from jax.experimental.pallas import tpu as pltpu
from jax.sharding import PartitionSpec as P

HEADS = 8
HEAD_SIZE = 128
T = 5
R = 8
ROWS = R * T
BLK = 32
REQ = 8
WIDTH = 2048
STRIPS = WIDTH // 128
EXTENT = 512
FRESH = 16
CH = 96
STATE = 256
EPSILON = 1e-05
ROPE_THETA = 100000000000.0
NEGATIVE = -1e30
MESH = pl.DeviceIdType.MESH
F32 = jnp.float32
BF16 = jnp.bfloat16

NT = (((1,), (1,)), ((), ()))


def iota(shape, dim):
    return lax.broadcasted_iota(jnp.int32, shape, dim)


def widen(values):
    return values.astype(F32)


def pack_pair(strip):
    lane = iota((24, 128), 1)
    top = strip[0:24]
    low = jnp.concatenate([strip[24:40], jnp.zeros((8, 128), F32)], axis=0)
    first = jnp.where(lane < 64, top, pltpu.roll(low, 64, 1))
    second = jnp.where(lane < 64, pltpu.roll(top, 64, 1), low)
    return first, second


def unpack_pair(first, second):
    lane = iota((24, 128), 1)
    top = jnp.where(lane < 64, first, pltpu.roll(second, 64, 1))
    low = jnp.where(lane < 64, pltpu.roll(first, 64, 1), second)
    return jnp.concatenate([top, low[0:16]], axis=0)


def kernel(
    hidden,
    attn_gain,
    ffn_gain,
    w_shared,
    w_dt,
    w_x,
    w_z,
    w_attn,
    w_ssm,
    w_gate,
    w_up,
    w_down,
    cache,
    parked,
    freq,
    dt_bias,
    a_log,
    d_skip,
    cache_len,
    accepted,
    slots,
    out_hidden,
    out_kv,
    out_state,
    hid_v,
    ag_v,
    fg_v,
    fr_v,
    wsh_v,
    wdt_v,
    wx_v,
    wz_v,
    wmix_v,
    wg_v,
    wu_v,
    wd_v,
    kv_v,
    pk_v,
    hp_v,
    pj_v,
    q_v,
    nk_v,
    b_v,
    c_v,
    o_v,
    l_v,
    g_v,
    wst_v,
    sv_v,
    nkv_v,
    out_v,
    st_send,
    st_recv,
    at_send,
    at_recv,
    mx_send,
    mx_recv,
    rs_v,
    dn_send,
    dn_recv,
    in_sem,
    kv_sem,
    out_sem,
    st_ss,
    st_rs,
    pj_ss,
    pj_rs,
    at_ss,
    at_rs,
    mx_ss,
    mx_rs,
    rs_ss,
    rs_rs,
    dn_ss,
    dn_rs,
):
    g = lax.axis_index("req")
    me = lax.axis_index("blk")
    core = lax.rem(g, 2)

    def owner_of(e):
        return 2 * e + lax.rem(lax.div(e, 2) + core, 2)

    my_e = lax.div(me, 2)
    parity = lax.rem(me, 2)
    is_owner = owner_of(my_e) == me

    def load(i, src, dst):
        copy = pltpu.make_async_copy(src, dst, in_sem.at[i])
        copy.start()
        return copy

    c_hid = load(0, hidden, hid_v)
    c_ag = load(1, attn_gain, ag_v)
    c_wsh = load(2, w_shared, wsh_v)

    barrier = pltpu.get_barrier_semaphore()

    def greet_blk(k, carry):
        pl.semaphore_signal(
            barrier, inc=1, device_id=(g, lax.rem(me + k, BLK)), device_id_type=MESH
        )
        return carry

    lax.fori_loop(1, BLK, greet_blk, 0)

    def greet_req(k, carry):
        pl.semaphore_signal(
            barrier, inc=1, device_id=(lax.rem(g + k, REQ), me), device_id_type=MESH
        )
        return carry

    lax.fori_loop(1, REQ, greet_req, 0)

    c_pk = load(3, parked, pk_v)
    c_wx = load(4, w_x, wx_v.at[pl.ds(0, CH)])
    c_wz = load(5, w_z, wz_v.at[pl.ds(0, CH)])
    c_wdt = load(6, w_dt, wdt_v.at[pl.ds(0, 48)])
    c_fr = load(7, freq, fr_v)
    c_kv = []
    for r in range(R):
        copy = pltpu.make_async_copy(cache.at[r], kv_v.at[r, pl.ds(0, EXTENT)], kv_sem.at[r])
        copy.start()
        c_kv.append(copy)
    c_ws = load(8, w_ssm, wmix_v.at[pl.ds(0, CH)])
    c_wa = load(9, w_attn, wmix_v.at[pl.ds(CH, 32)])
    c_fg = load(10, ffn_gain, fg_v)
    c_wg = load(11, w_gate, wg_v)
    c_wu = load(12, w_up, wu_v)
    c_wd = load(13, w_down, wd_v)

    c_hid.wait()
    c_ag.wait()
    row = iota((ROWS, ROWS), 0)
    col = iota((ROWS, ROWS), 1)
    place = (col == (row & 7) * T + (row >> 3)).astype(F32).astype(BF16)
    hid = jnp.dot(place, hid_v[...], preferred_element_type=F32)
    scaling = lax.rsqrt(jnp.sum(hid * hid, axis=1, keepdims=True) * (1.0 / WIDTH) + EPSILON)
    normed = (hid * scaling * widen(ag_v[...])).astype(BF16)
    c_wsh.wait()
    part = lax.dot_general(normed, wsh_v[...], NT, preferred_element_type=F32)
    twice = jnp.concatenate([part, part], axis=1)
    low = jnp.concatenate([twice[24:40], jnp.zeros((8, 128), F32)], axis=0)
    pj_v[me] = jnp.where(iota((24, 128), 1) < 64, twice[0:24], low).astype(BF16)

    pl.semaphore_wait(barrier, BLK - 1 + REQ - 1)

    def blk_copy(src, dst, send, recv, target):
        return pltpu.make_async_remote_copy(
            src_ref=src,
            dst_ref=dst,
            send_sem=send,
            recv_sem=recv,
            device_id=(g, target),
            device_id_type=MESH,
        )

    def pj_copy(k):
        target = lax.rem(me + k, BLK)
        return blk_copy(pj_v.at[me], pj_v.at[me], pj_ss.at[k], pj_rs.at[me], target)

    def pj_send(k, carry):
        pj_copy(k).start()
        return carry

    lax.fori_loop(1, BLK, pj_send, 0)

    c_pk.wait()

    def st_copy(k):
        target = lax.rem(g + k, REQ)
        return pltpu.make_async_remote_copy(
            src_ref=st_send.at[k],
            dst_ref=st_recv.at[g],
            send_sem=st_ss.at[k],
            recv_sem=st_rs.at[g],
            device_id=(target, me),
            device_id_type=MESH,
        )

    def st_push(k, carry):
        target = lax.rem(g + k, REQ)
        found = jnp.int32(0)
        picks = [jnp.int32(0), jnp.int32(0)]
        for i in range(2, R):
            slot = slots[target * R + i]
            mine = (slot >> 3) == g
            picks[0] = jnp.where(mine & (found == 0), slot & 7, picks[0])
            picks[1] = jnp.where(mine & (found == 1), slot & 7, picks[1])
            found = found + mine.astype(jnp.int32)
        for c in range(2):
            st_send[k, c] = pk_v[picks[c]].astype(BF16)
        st_copy(k).start()
        return carry

    lax.fori_loop(1, REQ, st_push, 0)

    hid_strips = [hid[:, 128 * e : 128 * (e + 1)] for e in range(STRIPS)]
    for e in range(STRIPS):
        hp_v[e] = hid_strips[e]
    wx_v[CH:128] = jnp.zeros((128 - CH, WIDTH), BF16)
    wz_v[CH:128] = jnp.zeros((128 - CH, WIDTH), BF16)
    wdt_v[48:128] = jnp.zeros((80, WIDTH), BF16)
    c_wx.wait()
    inner_x = lax.dot_general(normed, wx_v[...], NT, preferred_element_type=F32)
    c_wz.wait()
    inner_z = lax.dot_general(normed, wz_v[...], NT, preferred_element_type=F32)
    c_wdt.wait()
    dt = lax.dot_general(normed, wdt_v[...], NT, preferred_element_type=F32)

    head0 = lax.div(me * CH, 64)
    cut = 64 - lax.rem(me * CH, 64)
    lane1 = iota((1, 128), 1)
    lane = iota((ROWS, 128), 1)

    def by_head(ref):
        return jnp.where(lane1 < cut, ref[head0], ref[head0 + 1])

    dt0 = jnp.sum(jnp.where(lane == head0, dt, 0.0), axis=1, keepdims=True)
    dt1 = jnp.sum(jnp.where(lane == head0 + 1, dt, 0.0), axis=1, keepdims=True)
    raw = jnp.where(lane < cut, dt0, dt1) + by_head(dt_bias)
    steps = jnp.maximum(raw, 0.0) + jnp.log1p(jnp.exp(-jnp.abs(raw)))
    rate = -jnp.exp(by_head(a_log))
    skip = by_head(d_skip)

    c_fr.wait()
    sub24 = iota((24, 128), 0)
    lane24 = iota((24, 128), 1)
    base = jnp.zeros((24, 128), jnp.int32)
    for r in range(R):
        base = jnp.where((sub24 & 7) == r, cache_len[r], base)
    spot = base + (sub24 >> 3) + jnp.where(lane24 < 64, 0, 3)
    angle = spot.astype(F32) * fr_v[...]
    cosine = jnp.cos(angle)
    sine = jnp.sin(angle)

    nk_v[:, 40:128, :] = jnp.zeros((4, 88, 128), F32)
    b_v[:, 40:64, :] = jnp.zeros((2, 24, 128), F32)
    c_v[:, 40:64, :] = jnp.zeros((2, 24, 128), F32)

    def pj_wait(k, carry):
        source = lax.rem(me + BLK - k, BLK)
        blk_copy(
            pj_v.at[source], pj_v.at[source], pj_ss.at[k], pj_rs.at[source], source
        ).wait_recv()
        return carry

    lax.fori_loop(1, BLK, pj_wait, 0)

    def rotated(i):
        first = widen(pj_v[i])
        second = widen(pj_v[i + 1])
        return unpack_pair(
            first * cosine - second * sine, second * cosine + first * sine
        )

    def plain(i):
        return unpack_pair(widen(pj_v[i]), widen(pj_v[i + 1]))

    for h in range(HEADS):
        rows = rotated(2 * h)
        for t in range(T):
            q_v[pl.ds(t * 8 + h, R, stride=ROWS), :] = rows[8 * t : 8 * t + 8]
    for j in range(2):
        nk_v[j, 0:ROWS, :] = rotated(16 + 2 * j)
        nk_v[2 + j, 0:ROWS, :] = plain(20 + 2 * j)
        b_v[j, 0:ROWS, :] = plain(24 + 2 * j)
        c_v[j, 0:ROWS, :] = plain(28 + 2 * j)

    acc_col = jnp.zeros((8, 128), jnp.int32)
    sub8 = iota((8, 128), 0)
    for r in range(R):
        acc_col = jnp.where(sub8 == r, accepted[r], acc_col)
    for t in range(T):
        for j in range(4):
            rows = nk_v[j, 8 * t : 8 * t + 8, :]
            nkv_v[t, :, 128 * j : 128 * (j + 1)] = jnp.where(acc_col > t, rows, 0.0).astype(BF16)
    kv_out = pltpu.make_async_copy(nkv_v, out_kv, out_sem.at[0])
    kv_out.start()

    sub40 = iota((ROWS, 128), 0)
    group0 = (sub40 & 7) < 4
    spots = iota((ROWS, EXTENT + FRESH), 1)
    times = iota((ROWS, EXTENT + FRESH), 0) >> 3
    fresh_ok = (spots >= EXTENT) & (spots - EXTENT <= times) & (me == 0)
    for r in range(R):
        c_kv[r].wait()
        fresh = [nk_v[j, pl.ds(r, FRESH, stride=8), :] for j in range(4)]
        kv_v[r, EXTENT : EXTENT + FRESH, :] = jnp.concatenate(fresh, axis=1).astype(BF16)
        query = q_v[ROWS * r : ROWS * (r + 1), :]
        both = jnp.concatenate(
            [jnp.where(group0, query, 0.0), jnp.where(group0, 0.0, query)], axis=1
        ).astype(BF16)
        scores = lax.dot_general(
            both, kv_v[r, :, 0:256], NT, preferred_element_type=F32
        ) * (HEAD_SIZE**-0.5)
        usable = ((spots < EXTENT) & (spots + me * EXTENT < cache_len[r])) | fresh_ok
        peak = jnp.max(jnp.where(usable, scores, NEGATIVE), axis=1, keepdims=True)
        weights = jnp.where(usable, jnp.exp(scores - peak), 0.0)
        total = jnp.sum(weights, axis=1, keepdims=True)
        mixed = jnp.dot(weights.astype(BF16), kv_v[r, :, 256:512], preferred_element_type=F32)
        mixed = jnp.where(group0, mixed[:, 0:128], mixed[:, 128:256])
        some = total > 0.0
        o_v[ROWS * r : ROWS * (r + 1), :] = mixed / jnp.where(some, total, 1.0)
        level = jnp.where(some, peak + jnp.log(jnp.where(some, total, 1.0)), NEGATIVE)
        l_v[ROWS * r : ROWS * (r + 1), :] = jnp.broadcast_to(level, (ROWS, 128))

    lane8 = iota((8, 128), 1)
    for h in range(HEADS):
        outs = [o_v[pl.ds(t * 8 + h, R, stride=ROWS), :] for t in range(T)]
        stats = jnp.zeros((8, 128), F32)
        for t in range(T):
            level = l_v[pl.ds(t * 8 + h, R, stride=ROWS), :]
            high = widen(level.astype(BF16))
            middle = widen((level - high).astype(BF16))
            rest = level - high - middle
            stats = jnp.where(lane8 == 32 + t, high, stats)
            stats = jnp.where(lane8 == 40 + t, middle, stats)
            stats = jnp.where(lane8 == 48 + t, rest, stats)
        for q in range(4):
            first = outs[0] if q == 0 else pltpu.roll(outs[0], 128 - 32 * q, 1)
            for j in range(1, 4):
                shift = (32 * (j - q)) % 128
                moved = pltpu.roll(outs[j], shift, 1) if shift else outs[j]
                first = jnp.where(lane8 >= 32 * j, moved, first)
            last = pltpu.roll(outs[4], 128 - 32 * q, 1) if q else outs[4]
            second = jnp.where(lane8 < 32, last, stats)
            at_send[4 * h + q] = jnp.concatenate([first, second], axis=0).astype(BF16)

    def at_copy(k):
        target = lax.rem(me + k, BLK)
        return blk_copy(at_send.at[target], at_recv.at[me], at_ss.at[k], at_rs.at[me], target)

    def at_push(k, carry):
        at_copy(k).start()
        return carry

    lax.fori_loop(1, BLK, at_push, 0)
    at_recv[me] = at_send[me]

    def st_wait(k, carry):
        source = lax.rem(g + REQ - k, REQ)
        pltpu.make_async_remote_copy(
            src_ref=st_send.at[k],
            dst_ref=st_recv.at[source],
            send_sem=st_ss.at[k],
            recv_sem=st_rs.at[source],
            device_id=(source, me),
            device_id_type=MESH,
        ).wait_recv()
        return carry

    lax.fori_loop(1, REQ, st_wait, 0)

    step_t = [steps[8 * t : 8 * t + 8] for t in range(T)]
    x_t = [inner_x[8 * t : 8 * t + 8] for t in range(T)]
    dx_t = [step_t[t] * x_t[t] for t in range(T)]
    run_t = [step_t[0]]
    for t in range(1, T):
        run_t.append(run_t[-1] + step_t[t])
    at_accept = jnp.zeros((8, 128), F32)
    for t in range(T):
        at_accept = jnp.where(acc_col == t + 1, run_t[t], at_accept)
    wst_v[...] = jnp.zeros((128, 128), F32)
    for u in range(T):
        past = jnp.where(acc_col > u, rate * (at_accept - run_t[u]), NEGATIVE)
        weight = jnp.exp(past) * dx_t[u]
        wst_v[8 * u : 8 * u + 8, :] = weight
        wst_v[64 + 8 * u : 72 + 8 * u, :] = weight - widen(weight.astype(BF16))
    wst_v[40:48, :] = jnp.exp(rate * at_accept)
    turned = wst_v[...].T
    turned_low = turned[0:CH].astype(BF16)

    b_rows = jnp.concatenate([b_v[0], b_v[1]], axis=1)
    sub64 = iota((64, STATE), 0) & 7
    owners = []
    for r in range(2, R):
        slot = slots[g * R + r]
        own = slot >> 3
        rank = jnp.int32(0)
        for other in owners:
            rank = rank + (other == own).astype(jnp.int32)
        owners.append(own)
    for r in range(R):
        if r < 2:
            start = pk_v[slots[g * R + r] & 7]
        else:
            own = owners[r - 2]
            rank = jnp.int32(0)
            for other in owners[: r - 2]:
                rank = rank + (other == own).astype(jnp.int32)
            start = widen(st_recv[own, jnp.minimum(rank, 1)])
        c_rows = jnp.concatenate(
            [c_v[0, pl.ds(r, 8, stride=8), :], c_v[1, pl.ds(r, 8, stride=8), :]], axis=1
        )
        g_v[8 * r : 8 * r + 8, 0:CH] = lax.dot_general(
            c_rows.astype(BF16), start.astype(BF16), NT, preferred_element_type=F32
        )
        b_mine = jnp.where(sub64 == r, b_rows, 0.0)
        b_twice = jnp.concatenate([b_mine, b_mine], axis=0).astype(BF16)
        grown = jnp.dot(turned_low, b_twice, preferred_element_type=F32)
        sv_v[r] = turned[0:CH, 40 + r : 41 + r] * start + grown
    state_out = pltpu.make_async_copy(sv_v, out_state, out_sem.at[1])
    state_out.start()

    gated_t = []
    for t in range(T):
        y = jnp.exp(rate * run_t[t]) * g_v[pl.ds(t, R, stride=8), :] + skip * x_t[t]
        for u in range(t + 1):
            match = jnp.zeros((8, 1), F32)
            for j in range(2):
                match = match + jnp.sum(
                    c_v[j, 8 * t : 8 * t + 8, :] * b_v[j, 8 * u : 8 * u + 8, :],
                    axis=1,
                    keepdims=True,
                )
            kept = dx_t[u] if u == t else jnp.exp(rate * (run_t[t] - run_t[u])) * dx_t[u]
            y = y + match * kept
        z = inner_z[8 * t : 8 * t + 8]
        gated_t.append(y * (z * (1.0 / (1.0 + jnp.exp(-z)))))

    def at_wait(k, carry):
        source = lax.rem(me + BLK - k, BLK)
        blk_copy(
            at_send.at[source], at_recv.at[source], at_ss.at[k], at_rs.at[source], source
        ).wait_recv()
        return carry

    lax.fori_loop(1, BLK, at_wait, 0)
    parts = widen(at_recv[...])
    stats = parts[:, 8:16, :].reshape(BLK * 8, 128).astype(BF16)
    from_lane = iota((128, 256), 0)
    to_time = iota((128, 256), 1) >> 5
    to_time = jnp.minimum(to_time, 4)
    spread = (
        (from_lane == 32 + to_time) | (from_lane == 40 + to_time) | (from_lane == 48 + to_time)
    )
    level = jnp.dot(
        stats, spread.astype(F32).astype(BF16), preferred_element_type=F32
    ).reshape(BLK, 8, 256)
    top = jnp.max(level, axis=0, keepdims=True)
    share = jnp.exp(level - top)
    values = jnp.concatenate([parts[:, 0:8, :], parts[:, 8:16, :]], axis=2)
    merged = jnp.sum(share * values, axis=0) / jnp.sum(share, axis=0)
    mix_t = []
    for t in range(T):
        piece = merged[:, 0:128] if t < 4 else merged[:, 128:256]
        shift = (96 - 32 * t) % 128 if t < 4 else 96
        moved = pltpu.roll(piece, shift, 1) if shift else piece
        mix_t.append(jnp.where(lane8 < CH, gated_t[t], moved))
    mix_in = jnp.concatenate(mix_t, axis=0).astype(BF16)

    c_ws.wait()
    c_wa.wait()
    for e in range(STRIPS):
        mx_send[e] = jnp.dot(
            mix_in, wmix_v[:, 128 * e : 128 * (e + 1)], preferred_element_type=F32
        ).astype(BF16)

    def mx_copy(k):
        e = lax.rem(my_e + k, STRIPS)
        return blk_copy(
            mx_send.at[e], mx_recv.at[me], mx_ss.at[k], mx_rs.at[me], owner_of(e)
        )

    def mx_push(k, carry):
        mx_copy(k).start()
        return carry

    lax.fori_loop(1, STRIPS, mx_push, 0)

    @pl.when(jnp.logical_not(is_owner))
    def _():
        mx_copy(0).start()

    def rs_copy(k):
        return blk_copy(
            rs_v.at[my_e], rs_v.at[my_e], rs_ss.at[k], rs_rs.at[my_e], lax.rem(me + k, BLK)
        )

    @pl.when(is_owner)
    def _():
        def mx_wait(k, carry):
            source = lax.rem(me + BLK - k, BLK)
            blk_copy(
                mx_send.at[0], mx_recv.at[source], mx_ss.at[0], mx_rs.at[source], source
            ).wait_recv()
            return carry

        mx_recv[me] = mx_send[my_e]
        lax.fori_loop(1, BLK, mx_wait, 0)
        total = jnp.sum(widen(mx_recv[...]), axis=0)
        rs_v[my_e] = (hp_v[my_e] + total).astype(BF16)

        def rs_push(k, carry):
            rs_copy(k).start()
            return carry

        lax.fori_loop(1, BLK, rs_push, 0)

    c_fg.wait()
    c_wg.wait()
    c_wu.wait()
    c_wd.wait()

    def rs_wait(e, carry):
        @pl.when(owner_of(e) != me)
        def _():
            blk_copy(
                rs_v.at[e], rs_v.at[e], rs_ss.at[0], rs_rs.at[e], owner_of(e)
            ).wait_recv()

        return carry

    lax.fori_loop(0, STRIPS, rs_wait, 0)

    resid = [widen(rs_v[e]) for e in range(STRIPS)]
    squares = resid[0] * resid[0]
    for e in range(1, STRIPS):
        squares = squares + resid[e] * resid[e]
    scaling2 = lax.rsqrt(jnp.sum(squares, axis=1, keepdims=True) * (1.0 / WIDTH) + EPSILON)
    normed2 = (
        jnp.concatenate(resid, axis=1) * scaling2 * widen(fg_v[...])
    ).astype(BF16)
    gate = jnp.dot(normed2, wg_v[...], preferred_element_type=F32)
    up = jnp.dot(normed2, wu_v[...], preferred_element_type=F32)
    inner = (gate * (1.0 / (1.0 + jnp.exp(-gate))) * up).astype(BF16)
    for e in range(STRIPS):
        strip = jnp.dot(inner, wd_v[:, 128 * e : 128 * (e + 1)], preferred_element_type=F32)
        first, second = pack_pair(strip)
        dn_send[2 * e] = first.astype(BF16)
        dn_send[2 * e + 1] = second.astype(BF16)

    def dn_copy(k):
        target = lax.rem(me + k, BLK)
        return blk_copy(dn_send.at[target], dn_recv.at[me], dn_ss.at[k], dn_rs.at[me], target)

    def dn_push(k, carry):
        dn_copy(k).start()
        return carry

    lax.fori_loop(1, BLK, dn_push, 0)
    dn_recv[me] = dn_send[me]
    own_even, own_odd = pack_pair(widen(rs_v[my_e]))
    own = jnp.where(parity == 0, own_even, own_odd)

    def dn_wait(k, carry):
        source = lax.rem(me + BLK - k, BLK)
        blk_copy(
            dn_send.at[source], dn_recv.at[source], dn_ss.at[k], dn_rs.at[source], source
        ).wait_recv()
        return carry

    lax.fori_loop(1, BLK, dn_wait, 0)
    done = own + jnp.sum(widen(dn_recv[...]), axis=0)
    done = jnp.concatenate([done, pltpu.roll(done, 64, 1)[0:16]], axis=0).astype(BF16)
    back = (row == (col & 7) * T + (col >> 3)).astype(F32).astype(BF16)
    out_v[...] = jnp.dot(back, done, preferred_element_type=F32)[:, 0:64].astype(BF16)
    hid_out = pltpu.make_async_copy(out_v, out_hidden, out_sem.at[2])
    hid_out.start()

    def sent(k, carry):
        pj_copy(k).wait_send()
        at_copy(k).wait_send()
        dn_copy(k).wait_send()
        return carry

    lax.fori_loop(1, BLK, sent, 0)

    def st_sent(k, carry):
        st_copy(k).wait_send()
        return carry

    lax.fori_loop(1, REQ, st_sent, 0)

    def mx_sent(k, carry):
        mx_copy(k).wait_send()
        return carry

    lax.fori_loop(1, STRIPS, mx_sent, 0)

    @pl.when(jnp.logical_not(is_owner))
    def _():
        mx_copy(0).wait_send()

    @pl.when(is_owner)
    def _():
        def rs_sent(k, carry):
            rs_copy(k).wait_send()
            return carry

        lax.fori_loop(1, BLK, rs_sent, 0)

    kv_out.wait()
    state_out.wait()
    hid_out.wait()


def body(
    hidden,
    attn_gain,
    ffn_gain,
    shared_weight,
    w_dt,
    dt_bias,
    a_log,
    d_skip,
    w_inner_x,
    w_inner_z,
    w_attn_out,
    w_ssm_out,
    w_gate,
    w_up,
    w_down,
    key_value_cache,
    cache_len,
    accepted,
    parked,
    source_slot,
):
    half = HEAD_SIZE // 2
    exponent = np.arange(128) % half * 2.0 / HEAD_SIZE
    freq = jnp.asarray(np.power(ROPE_THETA, -exponent).astype(np.float32).reshape(1, 128))
    anywhere = pl.BlockSpec(memory_space=pltpu.HBM)
    scalars = pl.BlockSpec(memory_space=pltpu.SMEM)
    vm = pltpu.VMEM
    dma = pltpu.SemaphoreType.DMA
    outs = pl.pallas_call(
        kernel,
        out_shape=(
            jax.ShapeDtypeStruct((ROWS, WIDTH // BLK), BF16),
            jax.ShapeDtypeStruct((T, R, 512), BF16),
            jax.ShapeDtypeStruct((R, CH, STATE), F32),
        ),
        in_specs=[anywhere] * 15 + [scalars] * 6,
        out_specs=(anywhere,) * 3,
        scratch_shapes=[
            vm((ROWS, WIDTH), BF16),
            vm((1, WIDTH), BF16),
            vm((1, WIDTH), BF16),
            vm((1, 128), F32),
            vm((64, WIDTH), BF16),
            vm((128, WIDTH), BF16),
            vm((128, WIDTH), BF16),
            vm((128, WIDTH), BF16),
            vm((128, WIDTH), BF16),
            vm((WIDTH, 128), BF16),
            vm((WIDTH, 128), BF16),
            vm((128, WIDTH), BF16),
            vm((R, EXTENT + FRESH, 512), BF16),
            vm((R, CH, STATE), F32),
            vm((STRIPS, ROWS, 128), F32),
            vm((BLK, 24, 128), BF16),
            vm((R * ROWS, 128), F32),
            vm((4, 128, 128), F32),
            vm((2, 64, 128), F32),
            vm((2, 64, 128), F32),
            vm((R * ROWS, 128), F32),
            vm((R * ROWS, 128), F32),
            vm((64, 128), F32),
            vm((128, 128), F32),
            vm((R, CH, STATE), F32),
            vm((T, R, 512), BF16),
            vm((ROWS, 64), BF16),
            vm((REQ, 2, CH, STATE), BF16),
            vm((REQ, 2, CH, STATE), BF16),
            vm((BLK, 16, 128), BF16),
            vm((BLK, 16, 128), BF16),
            vm((STRIPS, ROWS, 128), BF16),
            vm((BLK, ROWS, 128), BF16),
            vm((STRIPS, ROWS, 128), BF16),
            vm((BLK, 24, 128), BF16),
            vm((BLK, 24, 128), BF16),
            dma((14,)),
            dma((R,)),
            dma((3,)),
            dma((REQ,)),
            dma((REQ,)),
            dma((BLK,)),
            dma((BLK,)),
            dma((BLK,)),
            dma((BLK,)),
            dma((STRIPS,)),
            dma((BLK,)),
            dma((BLK,)),
            dma((STRIPS,)),
            dma((BLK,)),
            dma((BLK,)),
        ],
        compiler_params=pltpu.CompilerParams(
            collective_id=0, has_side_effects=True, vmem_limit_bytes=63000000
        ),
        name="layer",
    )(
        hidden,
        attn_gain.reshape(1, WIDTH),
        ffn_gain.reshape(1, WIDTH),
        shared_weight.T,
        w_dt.T,
        w_inner_x.T,
        w_inner_z.T,
        w_attn_out,
        w_ssm_out,
        w_gate,
        w_up,
        w_down,
        key_value_cache,
        parked,
        freq,
        dt_bias,
        a_log,
        d_skip,
        cache_len,
        accepted,
        source_slot,
    )
    return outs[0], outs[1].transpose(1, 0, 2), outs[2]


def solution(mesh):
    placed = (
        P("req", None),
        P(),
        P(),
        P(None, "blk"),
        P(),
        P(),
        P(),
        P(),
        P(None, "blk"),
        P(None, "blk"),
        P("blk", None),
        P("blk", None),
        P(None, "blk"),
        P(None, "blk"),
        P("blk", None),
        P("req", "blk", None),
        P("req"),
        P("req"),
        P("req", "blk", None),
        P(),
    )
    return jax.shard_map(
        body,
        mesh=mesh,
        in_specs=placed,
        out_specs=(P("req", "blk"), P("req", None, None), P("req", "blk", None)),
        check_vma=False,
    )
```

```python
import math

import jax
import jax.numpy as jnp
import numpy as np
from jax import lax
from jax.experimental import pallas as pl
from jax.experimental.pallas import tpu as pltpu
from jax.sharding import PartitionSpec as P

HEADS = 8
HEAD_SIZE = 128
T = 5
R = 8
ROWS = R * T
BLK = 32
REQ = 8
WIDTH = 2048
STRIPS = WIDTH // 128
EXTENT = 512
FRESH = 16
CH = 96
STATE = 256
EPSILON = 1e-05
ROPE_THETA = 100000000000.0
NEGATIVE = -1e30
MESH = pl.DeviceIdType.MESH
F32 = jnp.float32
BF16 = jnp.bfloat16

NT = (((1,), (1,)), ((), ()))

FAR = sorted(
    [(dz, dx) for dz in range(8) for dx in range(4) if dz or dx],
    key=lambda o: -(min(o[0], 8 - o[0]) + min(o[1], 4 - o[1])),
)
FAR_EVEN = [o for o in FAR if (o[0] + o[1]) % 2 == 0]
FAR_ODD = [o for o in FAR if (o[0] + o[1]) % 2 == 1]


def iota(shape, dim):
    return lax.broadcasted_iota(jnp.int32, shape, dim)


def widen(values):
    return values.astype(F32)


def pack_pair(strip):
    lane = iota((24, 128), 1)
    top = strip[0:24]
    low = jnp.concatenate([strip[24:40], jnp.zeros((8, 128), F32)], axis=0)
    first = jnp.where(lane < 64, top, pltpu.roll(low, 64, 1))
    second = jnp.where(lane < 64, pltpu.roll(top, 64, 1), low)
    return first, second


def unpack_pair(first, second):
    lane = iota((24, 128), 1)
    top = jnp.where(lane < 64, first, pltpu.roll(second, 64, 1))
    low = jnp.where(lane < 64, pltpu.roll(first, 64, 1), second)
    return jnp.concatenate([top, low[0:16]], axis=0)


def kernel(
    hidden,
    attn_gain,
    ffn_gain,
    w_shared,
    w_dt,
    w_x,
    w_z,
    w_attn,
    w_ssm,
    w_gate,
    w_up,
    w_down,
    cache,
    parked,
    freq,
    dt_bias,
    a_log,
    d_skip,
    cache_len,
    accepted,
    slots,
    out_hidden,
    out_kv,
    out_state,
    hid_v,
    ag_v,
    fg_v,
    fr_v,
    wsh_v,
    wdt_v,
    wx_v,
    wz_v,
    wmix_v,
    wg_v,
    wu_v,
    wd_v,
    kv_v,
    pk_v,
    hp_v,
    pj_v,
    q_v,
    nk_v,
    b_v,
    c_v,
    s_v,
    o_v,
    l_v,
    g_v,
    wst_v,
    sv_v,
    nkv_v,
    out_v,
    st_send,
    st_recv,
    at_send,
    at_recv,
    mx_send,
    mx_recv,
    rs_v,
    dn_send,
    dn_recv,
    in_sem,
    kv_sem,
    out_sem,
    st_ss,
    st_rs,
    pj_ss,
    pj_rs,
    at_ss,
    at_rs,
    mx_ss,
    mx_rs,
    rs_ss,
    rs_rs,
    dn_ss,
    dn_rs,
):
    g = lax.axis_index("req")
    me = lax.axis_index("blk")
    core = lax.rem(g, 2)

    def owner_of(e):
        return 2 * e + lax.rem(lax.div(e, 2) + core, 2)

    my_z = lax.div(me, 4)
    my_x = lax.rem(me, 4)

    def at_offset(dz, dx):
        return lax.rem(my_z + dz, 8) * 4 + lax.rem(my_x + dx, 4)

    owns = 1 - lax.rem(my_z + my_x + core, 2)
    my_e = lax.div(me, 2)
    parity = lax.rem(me, 2)
    is_owner = owns == 1

    def load(i, src, dst):
        copy = pltpu.make_async_copy(src, dst, in_sem.at[i])
        copy.start()
        return copy

    c_hid = load(0, hidden, hid_v)
    c_ag = load(1, attn_gain, ag_v)
    c_wsh = load(2, w_shared, wsh_v)

    barrier = pltpu.get_barrier_semaphore()

    for offset in FAR:
        pl.semaphore_signal(
            barrier, inc=1, device_id=(g, at_offset(*offset)), device_id_type=MESH
        )

    def greet_req(k, carry):
        pl.semaphore_signal(
            barrier, inc=1, device_id=(lax.rem(g + k, REQ), me), device_id_type=MESH
        )
        return carry

    lax.fori_loop(1, REQ, greet_req, 0)

    c_pk = load(3, parked, pk_v)
    c_wx = load(4, w_x, wx_v.at[pl.ds(0, CH)])
    c_wz = load(5, w_z, wz_v.at[pl.ds(0, CH)])
    c_wdt = load(6, w_dt, wdt_v.at[pl.ds(0, 48)])
    c_fr = load(7, freq, fr_v)
    c_kv = []
    for r in range(R):
        copy = pltpu.make_async_copy(cache.at[r], kv_v.at[r, pl.ds(0, EXTENT)], kv_sem.at[r])
        copy.start()
        c_kv.append(copy)
    c_ws = load(8, w_ssm, wmix_v.at[pl.ds(0, CH)])
    c_wa = load(9, w_attn, wmix_v.at[pl.ds(CH, 32)])
    c_fg = load(10, ffn_gain, fg_v)
    c_wg = load(11, w_gate, wg_v)
    c_wu = load(12, w_up, wu_v)
    c_wd = load(13, w_down, wd_v)

    c_hid.wait()
    c_ag.wait()
    row = iota((ROWS, ROWS), 0)
    col = iota((ROWS, ROWS), 1)
    place = (col == (row & 7) * T + (row >> 3)).astype(F32).astype(BF16)
    hid = jnp.dot(place, hid_v[...], preferred_element_type=F32)
    scaling = lax.rsqrt(jnp.sum(hid * hid, axis=1, keepdims=True) * (1.0 / WIDTH) + EPSILON)
    gain = widen(ag_v[...])
    hid_strips = [hid[:, 128 * e : 128 * (e + 1)] for e in range(STRIPS)]
    normed = jnp.concatenate(
        [(hid_strips[e] * scaling * gain[e : e + 1]).astype(BF16) for e in range(STRIPS)], axis=1
    )
    c_wsh.wait()
    part = lax.dot_general(normed, wsh_v[...], NT, preferred_element_type=F32)
    twice = jnp.concatenate([part, part], axis=1)
    low = jnp.concatenate([twice[24:40], jnp.zeros((8, 128), F32)], axis=0)
    pj_v[me] = jnp.where(iota((24, 128), 1) < 64, twice[0:24], low).astype(BF16)

    pl.semaphore_wait(barrier, BLK - 1 + REQ - 1)

    def blk_copy(src, dst, send, recv, target):
        return pltpu.make_async_remote_copy(
            src_ref=src,
            dst_ref=dst,
            send_sem=send,
            recv_sem=recv,
            device_id=(g, target),
            device_id_type=MESH,
        )

    def pj_copy(k):
        return blk_copy(
            pj_v.at[me], pj_v.at[me], pj_ss.at[k], pj_rs.at[me], at_offset(*FAR[k])
        )

    for k in range(BLK - 1):
        pj_copy(k).start()

    c_pk.wait()

    def st_copy(k):
        target = lax.rem(g + k, REQ)
        return pltpu.make_async_remote_copy(
            src_ref=st_send.at[k],
            dst_ref=st_recv.at[g],
            send_sem=st_ss.at[k],
            recv_sem=st_rs.at[g],
            device_id=(target, me),
            device_id_type=MESH,
        )

    def st_push(k, carry):
        target = lax.rem(g + k, REQ)
        found = jnp.int32(0)
        picks = [jnp.int32(0), jnp.int32(0)]
        for i in range(2, R):
            slot = slots[target * R + i]
            mine = (slot >> 3) == g
            picks[0] = jnp.where(mine & (found == 0), slot & 7, picks[0])
            picks[1] = jnp.where(mine & (found == 1), slot & 7, picks[1])
            found = found + mine.astype(jnp.int32)
        for c in range(2):
            st_send[k, c] = pk_v[picks[c]].astype(BF16)
        st_copy(k).start()
        return carry

    lax.fori_loop(1, REQ, st_push, 0)

    for e in range(STRIPS):
        hp_v[e] = hid_strips[e]
    wx_v[CH:128] = jnp.zeros((128 - CH, WIDTH), BF16)
    wz_v[CH:128] = jnp.zeros((128 - CH, WIDTH), BF16)
    wdt_v[48:128] = jnp.zeros((80, WIDTH), BF16)
    c_wx.wait()
    inner_x = lax.dot_general(normed, wx_v[...], NT, preferred_element_type=F32)
    c_wz.wait()
    inner_z = lax.dot_general(normed, wz_v[...], NT, preferred_element_type=F32)
    c_wdt.wait()
    dt = lax.dot_general(normed, wdt_v[...], NT, preferred_element_type=F32)

    head0 = lax.div(me * CH, 64)
    cut = 64 - lax.rem(me * CH, 64)
    lane1 = iota((1, 128), 1)
    lane = iota((ROWS, 128), 1)

    def by_head(ref):
        return jnp.where(lane1 < cut, ref[head0], ref[head0 + 1])

    dt0 = jnp.sum(jnp.where(lane == head0, dt, 0.0), axis=1, keepdims=True)
    dt1 = jnp.sum(jnp.where(lane == head0 + 1, dt, 0.0), axis=1, keepdims=True)
    raw = jnp.where(lane < cut, dt0, dt1) + by_head(dt_bias)
    steps = jnp.maximum(raw, 0.0) + jnp.log1p(jnp.exp(-jnp.abs(raw)))
    rate = -jnp.exp(by_head(a_log))
    skip = by_head(d_skip)

    c_fr.wait()
    sub24 = iota((24, 128), 0)
    lane24 = iota((24, 128), 1)
    base = jnp.zeros((24, 128), jnp.int32)
    for r in range(R):
        base = jnp.where((sub24 & 7) == r, cache_len[r], base)
    spot = base + (sub24 >> 3) + jnp.where(lane24 < 64, 0, 3)
    angle = spot.astype(F32) * fr_v[...]
    cosine = jnp.cos(angle)
    sine = jnp.sin(angle)

    nk_v[:, 40:128, :] = jnp.zeros((4, 88, 128), F32)
    b_v[:, 40:64, :] = jnp.zeros((2, 24, 128), F32)
    c_v[:, 40:64, :] = jnp.zeros((2, 24, 128), F32)

    def pj_wait(k, carry):
        source = lax.rem(me + BLK - k, BLK)
        blk_copy(
            pj_v.at[source], pj_v.at[source], pj_ss.at[k], pj_rs.at[source], source
        ).wait_recv()
        return carry

    lax.fori_loop(1, BLK, pj_wait, 0)

    def rotated(i):
        first = widen(pj_v[i])
        second = widen(pj_v[i + 1])
        return unpack_pair(
            first * cosine - second * sine, second * cosine + first * sine
        )

    def plain(i):
        return unpack_pair(widen(pj_v[i]), widen(pj_v[i + 1]))

    for h in range(HEADS):
        rows = rotated(2 * h)
        for t in range(T):
            q_v[pl.ds(t * 8 + h, R, stride=ROWS), :] = rows[8 * t : 8 * t + 8]
    for j in range(2):
        nk_v[j, 0:ROWS, :] = rotated(16 + 2 * j)
        nk_v[2 + j, 0:ROWS, :] = plain(20 + 2 * j)
        b_v[j, 0:ROWS, :] = plain(24 + 2 * j)
        c_v[j, 0:ROWS, :] = plain(28 + 2 * j)

    acc_col = jnp.zeros((8, 128), jnp.int32)
    sub8 = iota((8, 128), 0)
    for r in range(R):
        acc_col = jnp.where(sub8 == r, accepted[r], acc_col)
    for t in range(T):
        for j in range(4):
            rows = nk_v[j, 8 * t : 8 * t + 8, :]
            nkv_v[t, :, 128 * j : 128 * (j + 1)] = jnp.where(acc_col > t, rows, 0.0).astype(BF16)
    kv_out = pltpu.make_async_copy(nkv_v, out_kv, out_sem.at[0])
    kv_out.start()

    sub40 = iota((ROWS, 128), 0)
    group0 = (sub40 & 7) < 4
    spots = iota((ROWS, EXTENT + FRESH), 1)
    times = iota((ROWS, EXTENT + FRESH), 0) >> 3
    fresh_ok = (spots >= EXTENT) & (spots - EXTENT <= times) & (me == 0)
    for r in range(R):
        fresh = [nk_v[j, pl.ds(r, FRESH, stride=8), :] for j in range(4)]
        kv_v[r, EXTENT : EXTENT + FRESH, :] = jnp.concatenate(fresh, axis=1).astype(BF16)
    for r in range(R):
        c_kv[r].wait()
        query = q_v[ROWS * r : ROWS * (r + 1), :]
        both = jnp.concatenate(
            [jnp.where(group0, query, 0.0), jnp.where(group0, 0.0, query)], axis=1
        ).astype(BF16)
        scores = lax.dot_general(
            both, kv_v[r, :, 0:256], NT, preferred_element_type=F32
        ) * (HEAD_SIZE**-0.5)
        usable = ((spots < EXTENT) & (spots + me * EXTENT < cache_len[r])) | fresh_ok
        s_v[ROWS * r : ROWS * (r + 1), :] = jnp.where(usable, scores, NEGATIVE)
    for r in range(R):
        scores = s_v[ROWS * r : ROWS * (r + 1), :]
        peak = jnp.max(scores, axis=1, keepdims=True)
        weights = jnp.exp(scores - peak)
        total = jnp.sum(weights, axis=1, keepdims=True)
        mixed = jnp.dot(weights.astype(BF16), kv_v[r, :, 256:512], preferred_element_type=F32)
        mixed = jnp.where(group0, mixed[:, 0:128], mixed[:, 128:256])
        o_v[ROWS * r : ROWS * (r + 1), :] = mixed / total
        level = jnp.where(peak > NEGATIVE, peak + jnp.log(total), NEGATIVE)
        l_v[ROWS * r : ROWS * (r + 1), :] = jnp.broadcast_to(level, (ROWS, 128))

    lane8 = iota((8, 128), 1)
    for h in range(HEADS):
        outs = [o_v[pl.ds(t * 8 + h, R, stride=ROWS), :] for t in range(T)]
        stats = jnp.zeros((8, 128), F32)
        for t in range(T):
            level = l_v[pl.ds(t * 8 + h, R, stride=ROWS), :]
            high = widen(level.astype(BF16))
            middle = widen((level - high).astype(BF16))
            rest = level - high - middle
            stats = jnp.where(lane8 == 32 + t, high, stats)
            stats = jnp.where(lane8 == 40 + t, middle, stats)
            stats = jnp.where(lane8 == 48 + t, rest, stats)
        for q in range(4):
            first = outs[0] if q == 0 else pltpu.roll(outs[0], 128 - 32 * q, 1)
            for j in range(1, 4):
                shift = (32 * (j - q)) % 128
                moved = pltpu.roll(outs[j], shift, 1) if shift else outs[j]
                first = jnp.where(lane8 >= 32 * j, moved, first)
            last = pltpu.roll(outs[4], 128 - 32 * q, 1) if q else outs[4]
            second = jnp.where(lane8 < 32, last, stats)
            at_send[4 * h + q] = jnp.concatenate([first, second], axis=0).astype(BF16)

    def at_copy(k):
        target = at_offset(*FAR[k])
        return blk_copy(at_send.at[target], at_recv.at[me], at_ss.at[k], at_rs.at[me], target)

    for k in range(BLK - 1):
        at_copy(k).start()
    at_recv[me] = at_send[me]

    def st_wait(k, carry):
        source = lax.rem(g + REQ - k, REQ)
        pltpu.make_async_remote_copy(
            src_ref=st_send.at[k],
            dst_ref=st_recv.at[source],
            send_sem=st_ss.at[k],
            recv_sem=st_rs.at[source],
            device_id=(source, me),
            device_id_type=MESH,
        ).wait_recv()
        return carry

    lax.fori_loop(1, REQ, st_wait, 0)

    step_t = [steps[8 * t : 8 * t + 8] for t in range(T)]
    x_t = [inner_x[8 * t : 8 * t + 8] for t in range(T)]
    dx_t = [step_t[t] * x_t[t] for t in range(T)]
    run_t = [step_t[0]]
    for t in range(1, T):
        run_t.append(run_t[-1] + step_t[t])
    at_accept = jnp.zeros((8, 128), F32)
    for t in range(T):
        at_accept = jnp.where(acc_col == t + 1, run_t[t], at_accept)
    wst_v[...] = jnp.zeros((128, 128), F32)
    for u in range(T):
        past = jnp.where(acc_col > u, rate * (at_accept - run_t[u]), NEGATIVE)
        weight = jnp.exp(past) * dx_t[u]
        wst_v[8 * u : 8 * u + 8, :] = weight
        wst_v[64 + 8 * u : 72 + 8 * u, :] = weight - widen(weight.astype(BF16))
    wst_v[40:48, :] = jnp.exp(rate * at_accept)
    turned = wst_v[...].T
    turned_low = turned[0:CH].astype(BF16)

    b_rows = jnp.concatenate([b_v[0], b_v[1]], axis=1)
    sub64 = iota((64, STATE), 0) & 7
    owners = []
    for r in range(2, R):
        slot = slots[g * R + r]
        own = slot >> 3
        rank = jnp.int32(0)
        for other in owners:
            rank = rank + (other == own).astype(jnp.int32)
        owners.append(own)
    for r in range(R):
        if r < 2:
            start = pk_v[slots[g * R + r] & 7]
        else:
            own = owners[r - 2]
            rank = jnp.int32(0)
            for other in owners[: r - 2]:
                rank = rank + (other == own).astype(jnp.int32)
            start = widen(st_recv[own, jnp.minimum(rank, 1)])
        c_rows = jnp.concatenate(
            [c_v[0, pl.ds(r, 8, stride=8), :], c_v[1, pl.ds(r, 8, stride=8), :]], axis=1
        )
        g_v[8 * r : 8 * r + 8, 0:CH] = lax.dot_general(
            c_rows.astype(BF16), start.astype(BF16), NT, preferred_element_type=F32
        )
        b_mine = jnp.where(sub64 == r, b_rows, 0.0)
        b_twice = jnp.concatenate([b_mine, b_mine], axis=0).astype(BF16)
        grown = jnp.dot(turned_low, b_twice, preferred_element_type=F32)
        sv_v[r] = turned[0:CH, 40 + r : 41 + r] * start + grown
    state_out = pltpu.make_async_copy(sv_v, out_state, out_sem.at[1])
    state_out.start()

    gated_t = []
    for t in range(T):
        y = jnp.exp(rate * run_t[t]) * g_v[pl.ds(t, R, stride=8), :] + skip * x_t[t]
        for u in range(t + 1):
            match = jnp.zeros((8, 1), F32)
            for j in range(2):
                match = match + jnp.sum(
                    c_v[j, 8 * t : 8 * t + 8, :] * b_v[j, 8 * u : 8 * u + 8, :],
                    axis=1,
                    keepdims=True,
                )
            kept = dx_t[u] if u == t else jnp.exp(rate * (run_t[t] - run_t[u])) * dx_t[u]
            y = y + match * kept
        z = inner_z[8 * t : 8 * t + 8]
        gated_t.append(y * (z * (1.0 / (1.0 + jnp.exp(-z)))))

    def at_wait(k, carry):
        source = lax.rem(me + BLK - k, BLK)
        blk_copy(
            at_send.at[source], at_recv.at[source], at_ss.at[k], at_rs.at[source], source
        ).wait_recv()
        return carry

    lax.fori_loop(1, BLK, at_wait, 0)
    parts = widen(at_recv[...])
    stats = parts[:, 8:16, :].reshape(BLK * 8, 128).astype(BF16)
    from_lane = iota((128, 256), 0)
    to_time = iota((128, 256), 1) >> 5
    to_time = jnp.minimum(to_time, 4)
    spread = (
        (from_lane == 32 + to_time) | (from_lane == 40 + to_time) | (from_lane == 48 + to_time)
    )
    level = jnp.dot(
        stats, spread.astype(F32).astype(BF16), preferred_element_type=F32
    ).reshape(BLK, 8, 256)
    top = jnp.max(level, axis=0, keepdims=True)
    share = jnp.exp(level - top)
    values = jnp.concatenate([parts[:, 0:8, :], parts[:, 8:16, :]], axis=2)
    merged = jnp.sum(share * values, axis=0) / jnp.sum(share, axis=0)
    mix_t = []
    for t in range(T):
        piece = merged[:, 0:128] if t < 4 else merged[:, 128:256]
        shift = (96 - 32 * t) % 128 if t < 4 else 96
        moved = pltpu.roll(piece, shift, 1) if shift else piece
        mix_t.append(jnp.where(lane8 < CH, gated_t[t], moved))
    mix_in = jnp.concatenate(mix_t, axis=0).astype(BF16)

    c_ws.wait()
    c_wa.wait()
    for e in range(STRIPS):
        mx_send[e] = jnp.dot(
            mix_in, wmix_v[:, 128 * e : 128 * (e + 1)], preferred_element_type=F32
        ).astype(BF16)

    def mx_copy(k):
        odd = FAR_ODD[k]
        even = FAR_EVEN[k] if k < STRIPS - 1 else odd
        target = at_offset(
            odd[0] + owns * (even[0] - odd[0]), odd[1] + owns * (even[1] - odd[1])
        )
        return blk_copy(
            mx_send.at[lax.div(target, 2)], mx_recv.at[me], mx_ss.at[k], mx_rs.at[me], target
        )

    for k in range(STRIPS - 1):
        mx_copy(k).start()

    @pl.when(jnp.logical_not(is_owner))
    def _():
        mx_copy(STRIPS - 1).start()

    def rs_copy(k):
        return blk_copy(
            rs_v.at[my_e], rs_v.at[my_e], rs_ss.at[k], rs_rs.at[my_e], at_offset(*FAR[k])
        )

    @pl.when(is_owner)
    def _():
        def mx_wait(k, carry):
            source = lax.rem(me + BLK - k, BLK)
            blk_copy(
                mx_send.at[0], mx_recv.at[source], mx_ss.at[0], mx_rs.at[source], source
            ).wait_recv()
            return carry

        mx_recv[me] = mx_send[my_e]
        lax.fori_loop(1, BLK, mx_wait, 0)
        total = jnp.sum(widen(mx_recv[...]), axis=0)
        rs_v[my_e] = (hp_v[my_e] + total).astype(BF16)

        for k in range(BLK - 1):
            rs_copy(k).start()

    c_fg.wait()
    c_wg.wait()
    c_wu.wait()
    c_wd.wait()

    def rs_wait(e, carry):
        @pl.when(owner_of(e) != me)
        def _():
            blk_copy(
                rs_v.at[e], rs_v.at[e], rs_ss.at[0], rs_rs.at[e], owner_of(e)
            ).wait_recv()

        return carry

    lax.fori_loop(0, STRIPS, rs_wait, 0)

    resid = [widen(rs_v[e]) for e in range(STRIPS)]
    squares = resid[0] * resid[0]
    for e in range(1, STRIPS):
        squares = squares + resid[e] * resid[e]
    scaling2 = lax.rsqrt(jnp.sum(squares, axis=1, keepdims=True) * (1.0 / WIDTH) + EPSILON)
    gain2 = widen(fg_v[...])
    normed2 = jnp.concatenate(
        [(resid[e] * scaling2 * gain2[e : e + 1]).astype(BF16) for e in range(STRIPS)], axis=1
    )
    gate = jnp.dot(normed2, wg_v[...], preferred_element_type=F32)
    up = jnp.dot(normed2, wu_v[...], preferred_element_type=F32)
    inner = (gate * (1.0 / (1.0 + jnp.exp(-gate))) * up).astype(BF16)
    for e in range(STRIPS):
        strip = jnp.dot(inner, wd_v[:, 128 * e : 128 * (e + 1)], preferred_element_type=F32)
        first, second = pack_pair(strip)
        dn_send[2 * e] = first.astype(BF16)
        dn_send[2 * e + 1] = second.astype(BF16)

    def dn_copy(k):
        target = at_offset(*FAR[k])
        return blk_copy(dn_send.at[target], dn_recv.at[me], dn_ss.at[k], dn_rs.at[me], target)

    for k in range(BLK - 1):
        dn_copy(k).start()
    dn_recv[me] = dn_send[me]
    own_even, own_odd = pack_pair(widen(rs_v[my_e]))
    own = jnp.where(parity == 0, own_even, own_odd)

    def dn_wait(k, carry):
        source = lax.rem(me + BLK - k, BLK)
        blk_copy(
            dn_send.at[source], dn_recv.at[source], dn_ss.at[k], dn_rs.at[source], source
        ).wait_recv()
        return carry

    lax.fori_loop(1, BLK, dn_wait, 0)
    done = own + jnp.sum(widen(dn_recv[...]), axis=0)
    done = jnp.concatenate([done, pltpu.roll(done, 64, 1)[0:16]], axis=0).astype(BF16)
    back = (row == (col & 7) * T + (col >> 3)).astype(F32).astype(BF16)
    out_v[...] = jnp.dot(back, done, preferred_element_type=F32)[:, 0:64].astype(BF16)
    hid_out = pltpu.make_async_copy(out_v, out_hidden, out_sem.at[2])
    hid_out.start()

    for k in range(BLK - 1):
        pj_copy(k).wait_send()
        at_copy(k).wait_send()
        dn_copy(k).wait_send()

    def st_sent(k, carry):
        st_copy(k).wait_send()
        return carry

    lax.fori_loop(1, REQ, st_sent, 0)
    for k in range(STRIPS - 1):
        mx_copy(k).wait_send()

    @pl.when(jnp.logical_not(is_owner))
    def _():
        mx_copy(STRIPS - 1).wait_send()

    @pl.when(is_owner)
    def _():
        for k in range(BLK - 1):
            rs_copy(k).wait_send()

    kv_out.wait()
    state_out.wait()
    hid_out.wait()


def handoff(hidden, kv, state, hidden_out, kv_out, state_out, hid_v, kv_v, st_v, in_sem, out_sem):
    steps = [(state.at[r], st_v.at[r], state_out.at[r]) for r in range(R)]
    steps += [(kv, kv_v, kv_out), (hidden, hid_v, hidden_out)]
    inward = [
        pltpu.make_async_copy(step[0], step[1], in_sem.at[i]) for i, step in enumerate(steps)
    ]
    outward = [
        pltpu.make_async_copy(step[1], step[2], out_sem.at[i]) for i, step in enumerate(steps)
    ]
    for copy in inward:
        copy.start()
    for arrive, leave in zip(inward, outward):
        arrive.wait()
        leave.start()
    for copy in outward:
        copy.wait()


def body(
    hidden,
    attn_gain,
    ffn_gain,
    shared_weight,
    w_dt,
    dt_bias,
    a_log,
    d_skip,
    w_inner_x,
    w_inner_z,
    w_attn_out,
    w_ssm_out,
    w_gate,
    w_up,
    w_down,
    key_value_cache,
    cache_len,
    accepted,
    parked,
    source_slot,
):
    half = HEAD_SIZE // 2
    exponent = np.arange(128) % half * 2.0 / HEAD_SIZE
    freq = jnp.asarray(np.power(ROPE_THETA, -exponent).astype(np.float32).reshape(1, 128))
    anywhere = pl.BlockSpec(memory_space=pltpu.HBM)
    scalars = pl.BlockSpec(memory_space=pltpu.SMEM)
    vm = pltpu.VMEM
    dma = pltpu.SemaphoreType.DMA
    shapes = (
        jax.ShapeDtypeStruct((ROWS, WIDTH // BLK), BF16),
        jax.ShapeDtypeStruct((T, R, 512), BF16),
        jax.ShapeDtypeStruct((R, CH, STATE), F32),
    )
    outs = pl.pallas_call(
        kernel,
        out_shape=shapes,
        in_specs=[anywhere] * 15 + [scalars] * 6,
        out_specs=(anywhere,) * 3,
        scratch_shapes=[
            vm((ROWS, WIDTH), BF16),
            vm((STRIPS, 128), BF16),
            vm((STRIPS, 128), BF16),
            vm((1, 128), F32),
            vm((64, WIDTH), BF16),
            vm((128, WIDTH), BF16),
            vm((128, WIDTH), BF16),
            vm((128, WIDTH), BF16),
            vm((128, WIDTH), BF16),
            vm((WIDTH, 128), BF16),
            vm((WIDTH, 128), BF16),
            vm((128, WIDTH), BF16),
            vm((R, EXTENT + FRESH, 512), BF16),
            vm((R, CH, STATE), F32),
            vm((STRIPS, ROWS, 128), F32),
            vm((BLK, 24, 128), BF16),
            vm((R * ROWS, 128), F32),
            vm((4, 128, 128), F32),
            vm((2, 64, 128), F32),
            vm((2, 64, 128), F32),
            vm((R * ROWS, EXTENT + FRESH), F32),
            vm((R * ROWS, 128), F32),
            vm((R * ROWS, 128), F32),
            vm((64, 128), F32),
            vm((128, 128), F32),
            vm((R, CH, STATE), F32),
            vm((T, R, 512), BF16),
            vm((ROWS, 64), BF16),
            vm((REQ, 2, CH, STATE), BF16),
            vm((REQ, 2, CH, STATE), BF16),
            vm((BLK, 16, 128), BF16),
            vm((BLK, 16, 128), BF16),
            vm((STRIPS, ROWS, 128), BF16),
            vm((BLK, ROWS, 128), BF16),
            vm((STRIPS, ROWS, 128), BF16),
            vm((BLK, 24, 128), BF16),
            vm((BLK, 24, 128), BF16),
            dma((14,)),
            dma((R,)),
            dma((3,)),
            dma((REQ,)),
            dma((REQ,)),
            dma((BLK,)),
            dma((BLK,)),
            dma((BLK,)),
            dma((BLK,)),
            dma((STRIPS,)),
            dma((BLK,)),
            dma((BLK,)),
            dma((STRIPS,)),
            dma((BLK,)),
            dma((BLK,)),
        ],
        compiler_params=pltpu.CompilerParams(
            collective_id=0, has_side_effects=True, vmem_limit_bytes=63000000
        ),
        name="layer",
    )(
        hidden,
        attn_gain.reshape(STRIPS, 128),
        ffn_gain.reshape(STRIPS, 128),
        shared_weight.T,
        w_dt.T,
        w_inner_x.T,
        w_inner_z.T,
        w_attn_out,
        w_ssm_out,
        w_gate,
        w_up,
        w_down,
        key_value_cache,
        parked,
        freq,
        dt_bias,
        a_log,
        d_skip,
        cache_len,
        accepted,
        source_slot,
    )
    outs = pl.pallas_call(
        handoff,
        out_shape=shapes,
        in_specs=[anywhere] * 3,
        out_specs=(anywhere,) * 3,
        scratch_shapes=[
            vm((ROWS, WIDTH // BLK), BF16),
            vm((T, R, 512), BF16),
            vm((R, CH, STATE), F32),
            dma((2 + R,)),
            dma((2 + R,)),
        ],
        compiler_params=pltpu.CompilerParams(vmem_limit_bytes=63000000),
        name="handoff",
    )(*outs)
    return outs[0], outs[1].transpose(1, 0, 2), outs[2]


def solution(mesh):
    placed = (
        P("req", None),
        P(),
        P(),
        P(None, "blk"),
        P(),
        P(),
        P(),
        P(),
        P(None, "blk"),
        P(None, "blk"),
        P("blk", None),
        P("blk", None),
        P(None, "blk"),
        P(None, "blk"),
        P("blk", None),
        P("req", "blk", None),
        P("req"),
        P("req"),
        P("req", "blk", None),
        P(),
    )
    return jax.shard_map(
        body,
        mesh=mesh,
        in_specs=placed,
        out_specs=(P("req", "blk"), P("req", None, None), P("req", "blk", None)),
        check_vma=False,
    )
```

```python
import math

import jax
import jax.numpy as jnp
import numpy as np
from jax import lax
from jax.experimental import pallas as pl
from jax.experimental.pallas import tpu as pltpu
from jax.sharding import PartitionSpec as P

HEADS = 8
HEAD_SIZE = 128
T = 5
R = 8
ROWS = R * T
BLK = 32
REQ = 8
WIDTH = 2048
STRIPS = WIDTH // 128
EXTENT = 512
CH = 96
STATE = 256
EPSILON = 1e-05
ROPE_THETA = 100000000000.0
NEGATIVE = -1e30
MESH = pl.DeviceIdType.MESH
F32 = jnp.float32
BF16 = jnp.bfloat16

NT = (((1,), (1,)), ((), ()))

FAR = sorted(
    [(dz, dx) for dz in range(8) for dx in range(4) if dz or dx],
    key=lambda o: -(min(o[0], 8 - o[0]) + min(o[1], 4 - o[1])),
)
FAR_EVEN = [o for o in FAR if (o[0] + o[1]) % 2 == 0]
FAR_ODD = [o for o in FAR if (o[0] + o[1]) % 2 == 1]


def iota(shape, dim):
    return lax.broadcasted_iota(jnp.int32, shape, dim)


def widen(values):
    return values.astype(F32)


def pack_pair(strip):
    lane = iota((24, 128), 1)
    top = strip[0:24]
    low = jnp.concatenate([strip[24:40], jnp.zeros((8, 128), F32)], axis=0)
    first = jnp.where(lane < 64, top, pltpu.roll(low, 64, 1))
    second = jnp.where(lane < 64, pltpu.roll(top, 64, 1), low)
    return first, second


def unpack_pair(first, second):
    lane = iota((24, 128), 1)
    top = jnp.where(lane < 64, first, pltpu.roll(second, 64, 1))
    low = jnp.where(lane < 64, pltpu.roll(first, 64, 1), second)
    return jnp.concatenate([top, low[0:16]], axis=0)


def kernel(
    hidden,
    attn_gain,
    ffn_gain,
    w_shared,
    w_dt,
    w_x,
    w_z,
    w_attn,
    w_ssm,
    w_gate,
    w_up,
    w_down,
    cache,
    parked,
    freq,
    dt_bias,
    a_log,
    d_skip,
    cache_len,
    accepted,
    slots,
    out_hidden,
    out_kv,
    out_state,
    hid_v,
    ag_v,
    fg_v,
    fr_v,
    wsh_v,
    wdt_v,
    wx_v,
    wz_v,
    wmix_v,
    wg_v,
    wu_v,
    wd_v,
    kv_v,
    pk_v,
    hp_v,
    pj_v,
    q_v,
    nk_v,
    b_v,
    c_v,
    both_v,
    s_v,
    p_v,
    o_v,
    l_v,
    g_v,
    wst_v,
    st_send,
    st_recv,
    at_send,
    at_recv,
    mx_send,
    mx_recv,
    rs_v,
    dn_send,
    dn_recv,
    in_sem,
    kv_sem,
    st_ss,
    st_rs,
    pj_ss,
    pj_rs,
    at_ss,
    at_rs,
    mx_ss,
    mx_rs,
    rs_ss,
    rs_rs,
    dn_ss,
    dn_rs,
):
    g = lax.axis_index("req")
    me = lax.axis_index("blk")
    core = lax.rem(g, 2)

    def owner_of(e):
        return 2 * e + lax.rem(lax.div(e, 2) + core, 2)

    my_z = lax.div(me, 4)
    my_x = lax.rem(me, 4)

    def at_offset(dz, dx):
        return lax.rem(my_z + dz, 8) * 4 + lax.rem(my_x + dx, 4)

    owns = 1 - lax.rem(my_z + my_x + core, 2)
    my_e = lax.div(me, 2)
    parity = lax.rem(me, 2)
    is_owner = owns == 1

    def load(i, src, dst):
        copy = pltpu.make_async_copy(src, dst, in_sem.at[i])
        copy.start()
        return copy

    barrier = pltpu.get_barrier_semaphore()

    for offset in FAR:
        pl.semaphore_signal(
            barrier, inc=1, device_id=(g, at_offset(*offset)), device_id_type=MESH
        )

    def greet_req(k, carry):
        pl.semaphore_signal(
            barrier, inc=1, device_id=(lax.rem(g + k, REQ), me), device_id_type=MESH
        )
        return carry

    lax.fori_loop(1, REQ, greet_req, 0)

    c_hid = load(0, hidden, hid_v)
    c_ag = load(1, attn_gain, ag_v)
    c_wsh = load(2, w_shared, wsh_v)
    c_pk = load(3, parked, pk_v)
    c_wx = load(4, w_x, wx_v.at[pl.ds(0, CH)])
    c_wz = load(5, w_z, wz_v.at[pl.ds(0, CH)])
    c_wdt = load(6, w_dt, wdt_v.at[pl.ds(0, 48)])
    c_fr = load(7, freq, fr_v)
    c_kv = []
    for r in range(R):
        copy = pltpu.make_async_copy(cache.at[r], kv_v.at[r], kv_sem.at[r])
        copy.start()
        c_kv.append(copy)
    c_ws = load(8, w_ssm, wmix_v.at[pl.ds(0, CH)])
    c_wa = load(9, w_attn, wmix_v.at[pl.ds(CH, 32)])
    c_fg = load(10, ffn_gain, fg_v)
    c_wg = load(11, w_gate, wg_v)
    c_wu = load(12, w_up, wu_v)
    c_wd = load(13, w_down, wd_v)

    c_hid.wait()
    c_ag.wait()
    row = iota((ROWS, ROWS), 0)
    col = iota((ROWS, ROWS), 1)
    place = (col == (row & 7) * T + (row >> 3)).astype(F32).astype(BF16)
    hid = jnp.dot(place, hid_v[...], preferred_element_type=F32)
    scaling = lax.rsqrt(jnp.sum(hid * hid, axis=1, keepdims=True) * (1.0 / WIDTH) + EPSILON)
    gain = widen(ag_v[...])
    hid_strips = [hid[:, 128 * e : 128 * (e + 1)] for e in range(STRIPS)]
    normed = jnp.concatenate(
        [(hid_strips[e] * scaling * gain[e : e + 1]).astype(BF16) for e in range(STRIPS)], axis=1
    )
    c_wsh.wait()
    part = lax.dot_general(normed, wsh_v[...], NT, preferred_element_type=F32)
    twice = jnp.concatenate([part, part], axis=1)
    low = jnp.concatenate([twice[24:40], jnp.zeros((8, 128), F32)], axis=0)
    pj_v[me] = jnp.where(iota((24, 128), 1) < 64, twice[0:24], low).astype(BF16)

    pl.semaphore_wait(barrier, BLK - 1 + REQ - 1)

    def blk_copy(src, dst, send, recv, target):
        return pltpu.make_async_remote_copy(
            src_ref=src,
            dst_ref=dst,
            send_sem=send,
            recv_sem=recv,
            device_id=(g, target),
            device_id_type=MESH,
        )

    def pj_copy(k):
        return blk_copy(
            pj_v.at[me], pj_v.at[me], pj_ss.at[k], pj_rs.at[me], at_offset(*FAR[k])
        )

    for k in range(BLK - 1):
        pj_copy(k).start()

    c_pk.wait()

    def st_copy(k):
        target = lax.rem(g + k, REQ)
        return pltpu.make_async_remote_copy(
            src_ref=st_send.at[k],
            dst_ref=st_recv.at[g],
            send_sem=st_ss.at[k],
            recv_sem=st_rs.at[g],
            device_id=(target, me),
            device_id_type=MESH,
        )

    def st_push(k, carry):
        target = lax.rem(g + k, REQ)
        found = jnp.int32(0)
        picks = [jnp.int32(0), jnp.int32(0)]
        for i in range(2, R):
            slot = slots[target * R + i]
            mine = (slot >> 3) == g
            picks[0] = jnp.where(mine & (found == 0), slot & 7, picks[0])
            picks[1] = jnp.where(mine & (found == 1), slot & 7, picks[1])
            found = found + mine.astype(jnp.int32)
        for c in range(2):
            st_send[k, c] = pk_v[picks[c]].astype(BF16)
        st_copy(k).start()
        return carry

    lax.fori_loop(1, REQ, st_push, 0)

    for e in range(STRIPS):
        hp_v[e] = hid_strips[e]
    wx_v[CH:128] = jnp.zeros((128 - CH, WIDTH), BF16)
    wz_v[CH:128] = jnp.zeros((128 - CH, WIDTH), BF16)
    wdt_v[48:128] = jnp.zeros((80, WIDTH), BF16)
    c_wx.wait()
    inner_x = lax.dot_general(normed, wx_v[...], NT, preferred_element_type=F32)
    c_wz.wait()
    inner_z = lax.dot_general(normed, wz_v[...], NT, preferred_element_type=F32)
    c_wdt.wait()
    dt = lax.dot_general(normed, wdt_v[...], NT, preferred_element_type=F32)

    head0 = lax.div(me * CH, 64)
    cut = 64 - lax.rem(me * CH, 64)
    lane1 = iota((1, 128), 1)
    lane = iota((ROWS, 128), 1)

    def by_head(ref):
        return jnp.where(lane1 < cut, ref[head0], ref[head0 + 1])

    dt0 = jnp.sum(jnp.where(lane == head0, dt, 0.0), axis=1, keepdims=True)
    dt1 = jnp.sum(jnp.where(lane == head0 + 1, dt, 0.0), axis=1, keepdims=True)
    raw = jnp.where(lane < cut, dt0, dt1) + by_head(dt_bias)
    steps = jnp.maximum(raw, 0.0) + jnp.log1p(jnp.exp(-jnp.abs(raw)))
    rate = -jnp.exp(by_head(a_log))
    skip = by_head(d_skip)

    c_fr.wait()
    sub24 = iota((24, 128), 0)
    lane24 = iota((24, 128), 1)
    base = jnp.zeros((24, 128), jnp.int32)
    for r in range(R):
        base = jnp.where((sub24 & 7) == r, cache_len[r], base)
    spot = base + (sub24 >> 3) + jnp.where(lane24 < 64, 0, 3)
    angle = spot.astype(F32) * fr_v[...]
    cosine = jnp.cos(angle)
    sine = jnp.sin(angle)

    nk_v[:, 40:128, :] = jnp.zeros((4, 88, 128), F32)
    b_v[:, 40:64, :] = jnp.zeros((2, 24, 128), F32)
    c_v[:, 40:64, :] = jnp.zeros((2, 24, 128), F32)

    def pj_wait(k, carry):
        source = lax.rem(me + BLK - k, BLK)
        blk_copy(
            pj_v.at[source], pj_v.at[source], pj_ss.at[k], pj_rs.at[source], source
        ).wait_recv()
        return carry

    lax.fori_loop(1, BLK, pj_wait, 0)

    def rotated(i):
        first = widen(pj_v[i])
        second = widen(pj_v[i + 1])
        return unpack_pair(
            first * cosine - second * sine, second * cosine + first * sine
        )

    def plain(i):
        return unpack_pair(widen(pj_v[i]), widen(pj_v[i + 1]))

    for h in range(HEADS):
        rows = rotated(2 * h)
        for t in range(T):
            q_v[pl.ds(t * 8 + h, R, stride=ROWS), :] = rows[8 * t : 8 * t + 8]
    for j in range(2):
        nk_v[j, 0:ROWS, :] = rotated(16 + 2 * j)
        nk_v[2 + j, 0:ROWS, :] = plain(20 + 2 * j)
        b_v[j, 0:ROWS, :] = plain(24 + 2 * j)
        c_v[j, 0:ROWS, :] = plain(28 + 2 * j)

    acc_col = jnp.zeros((8, 128), jnp.int32)
    sub8 = iota((8, 128), 0)
    for r in range(R):
        acc_col = jnp.where(sub8 == r, accepted[r], acc_col)
    for t in range(T):
        for j in range(4):
            rows = nk_v[j, 8 * t : 8 * t + 8, :]
            out_kv[t, :, 128 * j : 128 * (j + 1)] = jnp.where(acc_col > t, rows, 0.0).astype(BF16)

    sub40 = iota((ROWS, 128), 0)
    group0 = (sub40 & 7) < 4
    spots = iota((ROWS, EXTENT), 1)
    for r in range(R):
        query = q_v[ROWS * r : ROWS * (r + 1), :]
        both_v[ROWS * r : ROWS * (r + 1), :] = jnp.concatenate(
            [jnp.where(group0, query, 0.0), jnp.where(group0, 0.0, query)], axis=1
        ).astype(BF16)
    new_keys = jnp.concatenate([nk_v[0], nk_v[1]], axis=1).astype(BF16)
    new_scores = lax.dot_general(both_v[...], new_keys, NT, preferred_element_type=F32)
    lanes = iota((ROWS, 128), 1)
    in_order = ((lanes >> 3) <= (sub40 >> 3)) & (me == 0)
    for r in range(R):
        c_kv[r].wait()
        rows = slice(ROWS * r, ROWS * (r + 1))
        scores = lax.dot_general(
            both_v[rows, :], kv_v[r, :, 0:256], NT, preferred_element_type=F32
        )
        s_v[rows, 0:EXTENT] = jnp.where(spots < cache_len[r] - me * EXTENT, scores, NEGATIVE)
        s_v[rows, EXTENT : EXTENT + 128] = jnp.where(
            in_order & ((lanes & 7) == r), new_scores[rows, :], NEGATIVE
        )
    scale = HEAD_SIZE**-0.5
    totals = []
    peaks = []
    for r in range(R):
        rows = slice(ROWS * r, ROWS * (r + 1))
        scores = s_v[rows, :]
        peak = jnp.max(scores, axis=1, keepdims=True)
        weights = jnp.exp2((scores - peak) * (scale * math.log2(math.e)))
        totals.append(jnp.sum(weights, axis=1, keepdims=True))
        peaks.append(peak)
        p_v[rows, :] = weights.astype(BF16)
    new_values = jnp.concatenate([nk_v[2], nk_v[3]], axis=1).astype(BF16)
    new_mixed = jnp.dot(
        p_v[:, EXTENT : EXTENT + 128], new_values, preferred_element_type=F32
    )
    for r in range(R):
        rows = slice(ROWS * r, ROWS * (r + 1))
        mixed = new_mixed[rows, :] + jnp.dot(
            p_v[rows, 0:EXTENT], kv_v[r, :, 256:512], preferred_element_type=F32
        )
        mixed = jnp.where(group0, mixed[:, 0:128], mixed[:, 128:256])
        o_v[rows, :] = mixed / totals[r]
        level = jnp.where(
            peaks[r] > NEGATIVE, peaks[r] * scale + jnp.log(totals[r]), NEGATIVE
        )
        l_v[rows, :] = jnp.broadcast_to(level, (ROWS, 128))

    lane8 = iota((8, 128), 1)
    for h in range(HEADS):
        outs = [o_v[pl.ds(t * 8 + h, R, stride=ROWS), :] for t in range(T)]
        stats = jnp.zeros((8, 128), F32)
        for t in range(T):
            level = l_v[pl.ds(t * 8 + h, R, stride=ROWS), :]
            high = widen(level.astype(BF16))
            middle = widen((level - high).astype(BF16))
            rest = level - high - middle
            stats = jnp.where(lane8 == 32 + t, high, stats)
            stats = jnp.where(lane8 == 40 + t, middle, stats)
            stats = jnp.where(lane8 == 48 + t, rest, stats)
        for q in range(4):
            first = outs[0] if q == 0 else pltpu.roll(outs[0], 128 - 32 * q, 1)
            for j in range(1, 4):
                shift = (32 * (j - q)) % 128
                moved = pltpu.roll(outs[j], shift, 1) if shift else outs[j]
                first = jnp.where(lane8 >= 32 * j, moved, first)
            last = pltpu.roll(outs[4], 128 - 32 * q, 1) if q else outs[4]
            second = jnp.where(lane8 < 32, last, stats)
            at_send[4 * h + q] = jnp.concatenate([first, second], axis=0).astype(BF16)

    def at_copy(k):
        target = at_offset(*FAR[k])
        return blk_copy(at_send.at[target], at_recv.at[me], at_ss.at[k], at_rs.at[me], target)

    for k in range(BLK - 1):
        at_copy(k).start()
    at_recv[me] = at_send[me]

    def st_wait(k, carry):
        source = lax.rem(g + REQ - k, REQ)
        pltpu.make_async_remote_copy(
            src_ref=st_send.at[k],
            dst_ref=st_recv.at[source],
            send_sem=st_ss.at[k],
            recv_sem=st_rs.at[source],
            device_id=(source, me),
            device_id_type=MESH,
        ).wait_recv()
        return carry

    lax.fori_loop(1, REQ, st_wait, 0)

    step_t = [steps[8 * t : 8 * t + 8] for t in range(T)]
    x_t = [inner_x[8 * t : 8 * t + 8] for t in range(T)]
    dx_t = [step_t[t] * x_t[t] for t in range(T)]
    run_t = [step_t[0]]
    for t in range(1, T):
        run_t.append(run_t[-1] + step_t[t])
    at_accept = jnp.zeros((8, 128), F32)
    for t in range(T):
        at_accept = jnp.where(acc_col == t + 1, run_t[t], at_accept)
    wst_v[...] = jnp.zeros((128, 128), F32)
    for u in range(T):
        past = jnp.where(acc_col > u, rate * (at_accept - run_t[u]), NEGATIVE)
        weight = jnp.exp(past) * dx_t[u]
        wst_v[8 * u : 8 * u + 8, :] = weight
        wst_v[64 + 8 * u : 72 + 8 * u, :] = weight - widen(weight.astype(BF16))
    wst_v[40:48, :] = jnp.exp(rate * at_accept)
    turned = wst_v[...].T
    turned_low = turned[0:CH].astype(BF16)

    b_rows = jnp.concatenate([b_v[0], b_v[1]], axis=1)
    sub64 = iota((64, STATE), 0) & 7
    owners = []
    for r in range(2, R):
        slot = slots[g * R + r]
        own = slot >> 3
        rank = jnp.int32(0)
        for other in owners:
            rank = rank + (other == own).astype(jnp.int32)
        owners.append(own)
    for r in range(R):
        if r < 2:
            start = pk_v[slots[g * R + r] & 7]
        else:
            own = owners[r - 2]
            rank = jnp.int32(0)
            for other in owners[: r - 2]:
                rank = rank + (other == own).astype(jnp.int32)
            start = widen(st_recv[own, jnp.minimum(rank, 1)])
        c_rows = jnp.concatenate(
            [c_v[0, pl.ds(r, 8, stride=8), :], c_v[1, pl.ds(r, 8, stride=8), :]], axis=1
        )
        g_v[8 * r : 8 * r + 8, 0:CH] = lax.dot_general(
            c_rows.astype(BF16), start.astype(BF16), NT, preferred_element_type=F32
        )
        b_mine = jnp.where(sub64 == r, b_rows, 0.0)
        b_twice = jnp.concatenate([b_mine, b_mine], axis=0).astype(BF16)
        grown = jnp.dot(turned_low, b_twice, preferred_element_type=F32)
        out_state[r] = turned[0:CH, 40 + r : 41 + r] * start + grown

    gated_t = []
    for t in range(T):
        y = jnp.exp(rate * run_t[t]) * g_v[pl.ds(t, R, stride=8), :] + skip * x_t[t]
        for u in range(t + 1):
            match = jnp.zeros((8, 1), F32)
            for j in range(2):
                match = match + jnp.sum(
                    c_v[j, 8 * t : 8 * t + 8, :] * b_v[j, 8 * u : 8 * u + 8, :],
                    axis=1,
                    keepdims=True,
                )
            kept = dx_t[u] if u == t else jnp.exp(rate * (run_t[t] - run_t[u])) * dx_t[u]
            y = y + match * kept
        z = inner_z[8 * t : 8 * t + 8]
        gated_t.append(y * (z * (1.0 / (1.0 + jnp.exp(-z)))))

    def at_wait(k, carry):
        source = lax.rem(me + BLK - k, BLK)
        blk_copy(
            at_send.at[source], at_recv.at[source], at_ss.at[k], at_rs.at[source], source
        ).wait_recv()
        return carry

    lax.fori_loop(1, BLK, at_wait, 0)
    parts = widen(at_recv[...])
    stats = parts[:, 8:16, :].reshape(BLK * 8, 128).astype(BF16)
    from_lane = iota((128, 256), 0)
    to_time = iota((128, 256), 1) >> 5
    to_time = jnp.minimum(to_time, 4)
    spread = (
        (from_lane == 32 + to_time) | (from_lane == 40 + to_time) | (from_lane == 48 + to_time)
    )
    level = jnp.dot(
        stats, spread.astype(F32).astype(BF16), preferred_element_type=F32
    ).reshape(BLK, 8, 256)
    top = jnp.max(level, axis=0, keepdims=True)
    share = jnp.exp(level - top)
    values = jnp.concatenate([parts[:, 0:8, :], parts[:, 8:16, :]], axis=2)
    merged = jnp.sum(share * values, axis=0) / jnp.sum(share, axis=0)
    mix_t = []
    for t in range(T):
        piece = merged[:, 0:128] if t < 4 else merged[:, 128:256]
        shift = (96 - 32 * t) % 128 if t < 4 else 96
        moved = pltpu.roll(piece, shift, 1) if shift else piece
        mix_t.append(jnp.where(lane8 < CH, gated_t[t], moved))
    mix_in = jnp.concatenate(mix_t, axis=0).astype(BF16)

    c_ws.wait()
    c_wa.wait()
    for e in range(0, STRIPS, 2):
        pair = jnp.dot(
            mix_in, wmix_v[:, 128 * e : 128 * (e + 2)], preferred_element_type=F32
        ).astype(BF16)
        mx_send[e] = pair[:, 0:128]
        mx_send[e + 1] = pair[:, 128:256]

    def mx_copy(k):
        odd = FAR_ODD[k]
        even = FAR_EVEN[k] if k < STRIPS - 1 else odd
        target = at_offset(
            odd[0] + owns * (even[0] - odd[0]), odd[1] + owns * (even[1] - odd[1])
        )
        return blk_copy(
            mx_send.at[lax.div(target, 2)], mx_recv.at[me], mx_ss.at[k], mx_rs.at[me], target
        )

    for k in range(STRIPS - 1):
        mx_copy(k).start()

    @pl.when(jnp.logical_not(is_owner))
    def _():
        mx_copy(STRIPS - 1).start()

    def rs_copy(k):
        return blk_copy(
            rs_v.at[my_e], rs_v.at[my_e], rs_ss.at[k], rs_rs.at[my_e], at_offset(*FAR[k])
        )

    @pl.when(is_owner)
    def _():
        def mx_wait(k, carry):
            source = lax.rem(me + BLK - k, BLK)
            blk_copy(
                mx_send.at[0], mx_recv.at[source], mx_ss.at[0], mx_rs.at[source], source
            ).wait_recv()
            return carry

        mx_recv[me] = mx_send[my_e]
        lax.fori_loop(1, BLK, mx_wait, 0)
        total = jnp.sum(widen(mx_recv[...]), axis=0)
        rs_v[my_e] = (hp_v[my_e] + total).astype(BF16)

        for k in range(BLK - 1):
            rs_copy(k).start()

    c_fg.wait()
    c_wg.wait()
    c_wu.wait()
    c_wd.wait()

    def rs_wait(e, carry):
        @pl.when(owner_of(e) != me)
        def _():
            blk_copy(
                rs_v.at[e], rs_v.at[e], rs_ss.at[0], rs_rs.at[e], owner_of(e)
            ).wait_recv()

        return carry

    lax.fori_loop(0, STRIPS, rs_wait, 0)

    resid = [widen(rs_v[e]) for e in range(STRIPS)]
    squares = resid[0] * resid[0]
    for e in range(1, STRIPS):
        squares = squares + resid[e] * resid[e]
    scaling2 = lax.rsqrt(jnp.sum(squares, axis=1, keepdims=True) * (1.0 / WIDTH) + EPSILON)
    gain2 = widen(fg_v[...])
    normed2 = jnp.concatenate(
        [(resid[e] * scaling2 * gain2[e : e + 1]).astype(BF16) for e in range(STRIPS)], axis=1
    )
    gate = jnp.dot(normed2, wg_v[...], preferred_element_type=F32)
    up = jnp.dot(normed2, wu_v[...], preferred_element_type=F32)
    inner = (gate * (1.0 / (1.0 + jnp.exp(-gate))) * up).astype(BF16)
    for e in range(0, STRIPS, 2):
        pair = jnp.dot(inner, wd_v[:, 128 * e : 128 * (e + 2)], preferred_element_type=F32)
        for i in range(2):
            first, second = pack_pair(pair[:, 128 * i : 128 * (i + 1)])
            dn_send[2 * (e + i)] = first.astype(BF16)
            dn_send[2 * (e + i) + 1] = second.astype(BF16)

    def dn_copy(k):
        target = at_offset(*FAR[k])
        return blk_copy(dn_send.at[target], dn_recv.at[me], dn_ss.at[k], dn_rs.at[me], target)

    for k in range(BLK - 1):
        dn_copy(k).start()
    dn_recv[me] = dn_send[me]
    own_even, own_odd = pack_pair(widen(rs_v[my_e]))
    own = jnp.where(parity == 0, own_even, own_odd)

    def dn_wait(k, carry):
        source = lax.rem(me + BLK - k, BLK)
        blk_copy(
            dn_send.at[source], dn_recv.at[source], dn_ss.at[k], dn_rs.at[source], source
        ).wait_recv()
        return carry

    lax.fori_loop(1, BLK, dn_wait, 0)
    done = own + jnp.sum(widen(dn_recv[...]), axis=0)
    done = jnp.concatenate([done, pltpu.roll(done, 64, 1)[0:16]], axis=0).astype(BF16)
    back = (row == (col & 7) * T + (col >> 3)).astype(F32).astype(BF16)
    out_hidden[...] = jnp.dot(back, done, preferred_element_type=F32)[:, 0:64].astype(BF16)

    for k in range(BLK - 1):
        pj_copy(k).wait_send()
        at_copy(k).wait_send()
        dn_copy(k).wait_send()

    def st_sent(k, carry):
        st_copy(k).wait_send()
        return carry

    lax.fori_loop(1, REQ, st_sent, 0)
    for k in range(STRIPS - 1):
        mx_copy(k).wait_send()

    @pl.when(jnp.logical_not(is_owner))
    def _():
        mx_copy(STRIPS - 1).wait_send()

    @pl.when(is_owner)
    def _():
        for k in range(BLK - 1):
            rs_copy(k).wait_send()


def handoff(hidden, kv, state, hidden_out, kv_out, state_out, sem):
    copies = [
        pltpu.make_async_copy(state.at[r], state_out.at[r], sem.at[2 + r]) for r in range(R)
    ]
    copies.append(pltpu.make_async_copy(kv, kv_out, sem.at[1]))
    copies.append(pltpu.make_async_copy(hidden, hidden_out, sem.at[0]))
    for copy in copies:
        copy.start()
    for copy in copies:
        copy.wait()


def body(
    hidden,
    attn_gain,
    ffn_gain,
    shared_weight,
    w_dt,
    dt_bias,
    a_log,
    d_skip,
    w_inner_x,
    w_inner_z,
    w_attn_out,
    w_ssm_out,
    w_gate,
    w_up,
    w_down,
    key_value_cache,
    cache_len,
    accepted,
    parked,
    source_slot,
):
    half = HEAD_SIZE // 2
    exponent = np.arange(128) % half * 2.0 / HEAD_SIZE
    freq = jnp.asarray(np.power(ROPE_THETA, -exponent).astype(np.float32).reshape(1, 128))
    anywhere = pl.BlockSpec(memory_space=pltpu.HBM)
    scalars = pl.BlockSpec(memory_space=pltpu.SMEM)
    vm = pltpu.VMEM
    dma = pltpu.SemaphoreType.DMA
    shapes = (
        jax.ShapeDtypeStruct((ROWS, WIDTH // BLK), BF16),
        jax.ShapeDtypeStruct((T, R, 512), BF16),
        jax.ShapeDtypeStruct((R, CH, STATE), F32),
    )
    outs = pl.pallas_call(
        kernel,
        out_shape=tuple(vm(shape.shape, shape.dtype) for shape in shapes),
        in_specs=[anywhere] * 15 + [scalars] * 6,
        out_specs=(pl.BlockSpec(memory_space=vm),) * 3,
        scratch_shapes=[
            vm((ROWS, WIDTH), BF16),
            vm((STRIPS, 128), BF16),
            vm((STRIPS, 128), BF16),
            vm((1, 128), F32),
            vm((64, WIDTH), BF16),
            vm((128, WIDTH), BF16),
            vm((128, WIDTH), BF16),
            vm((128, WIDTH), BF16),
            vm((128, WIDTH), BF16),
            vm((WIDTH, 128), BF16),
            vm((WIDTH, 128), BF16),
            vm((128, WIDTH), BF16),
            vm((R, EXTENT, 512), BF16),
            vm((R, CH, STATE), F32),
            vm((STRIPS, ROWS, 128), F32),
            vm((BLK, 24, 128), BF16),
            vm((R * ROWS, 128), F32),
            vm((4, 128, 128), F32),
            vm((2, 64, 128), F32),
            vm((2, 64, 128), F32),
            vm((R * ROWS, 256), BF16),
            vm((R * ROWS, EXTENT + 128), F32),
            vm((R * ROWS, EXTENT + 128), BF16),
            vm((R * ROWS, 128), F32),
            vm((R * ROWS, 128), F32),
            vm((64, 128), F32),
            vm((128, 128), F32),
            vm((REQ, 2, CH, STATE), BF16),
            vm((REQ, 2, CH, STATE), BF16),
            vm((BLK, 16, 128), BF16),
            vm((BLK, 16, 128), BF16),
            vm((STRIPS, ROWS, 128), BF16),
            vm((BLK, ROWS, 128), BF16),
            vm((STRIPS, ROWS, 128), BF16),
            vm((BLK, 24, 128), BF16),
            vm((BLK, 24, 128), BF16),
            dma((14,)),
            dma((R,)),
            dma((REQ,)),
            dma((REQ,)),
            dma((BLK,)),
            dma((BLK,)),
            dma((BLK,)),
            dma((BLK,)),
            dma((STRIPS,)),
            dma((BLK,)),
            dma((BLK,)),
            dma((STRIPS,)),
            dma((BLK,)),
            dma((BLK,)),
        ],
        compiler_params=pltpu.CompilerParams(
            collective_id=0, has_side_effects=True, vmem_limit_bytes=63000000
        ),
        name="layer",
    )(
        hidden,
        attn_gain.reshape(STRIPS, 128),
        ffn_gain.reshape(STRIPS, 128),
        shared_weight.T,
        w_dt.T,
        w_inner_x.T,
        w_inner_z.T,
        w_attn_out,
        w_ssm_out,
        w_gate,
        w_up,
        w_down,
        key_value_cache,
        parked,
        freq,
        dt_bias,
        a_log,
        d_skip,
        cache_len,
        accepted,
        source_slot,
    )
    outs = pl.pallas_call(
        handoff,
        out_shape=shapes,
        in_specs=[pl.BlockSpec(memory_space=vm)] * 3,
        out_specs=(anywhere,) * 3,
        scratch_shapes=[dma((2 + R,))],
        compiler_params=pltpu.CompilerParams(vmem_limit_bytes=1000000),
        name="handoff",
    )(*outs)
    return outs[0], outs[1].transpose(1, 0, 2), outs[2]


def solution(mesh):
    placed = (
        P("req", None),
        P(),
        P(),
        P(None, "blk"),
        P(),
        P(),
        P(),
        P(),
        P(None, "blk"),
        P(None, "blk"),
        P("blk", None),
        P("blk", None),
        P(None, "blk"),
        P(None, "blk"),
        P("blk", None),
        P("req", "blk", None),
        P("req"),
        P("req"),
        P("req", "blk", None),
        P(),
    )
    return jax.shard_map(
        body,
        mesh=mesh,
        in_specs=placed,
        out_specs=(P("req", "blk"), P("req", None, None), P("req", "blk", None)),
        check_vma=False,
    )
```

```python
import math

import jax
import jax.numpy as jnp
import numpy as np
from jax import lax
from jax.experimental import pallas as pl
from jax.experimental.pallas import tpu as pltpu
from jax.sharding import PartitionSpec as P

HEADS = 8
HEAD_SIZE = 128
T = 5
R = 8
ROWS = R * T
BLK = 32
REQ = 8
WIDTH = 2048
STRIPS = WIDTH // 128
EXTENT = 512
CH = 96
STATE = 256
EPSILON = 1e-05
ROPE_THETA = 100000000000.0
NEGATIVE = -1e30
MESH = pl.DeviceIdType.MESH
F32 = jnp.float32
BF16 = jnp.bfloat16

NT = (((1,), (1,)), ((), ()))

FAR = sorted(
    [(dz, dx) for dz in range(8) for dx in range(4) if dz or dx],
    key=lambda o: -(min(o[0], 8 - o[0]) + min(o[1], 4 - o[1])),
)
FAR_EVEN = [o for o in FAR if (o[0] + o[1]) % 2 == 0]
FAR_ODD = [o for o in FAR if (o[0] + o[1]) % 2 == 1]


def iota(shape, dim):
    return lax.broadcasted_iota(jnp.int32, shape, dim)


def widen(values):
    return values.astype(F32)


def pack_pair(strip):
    lane = iota((24, 128), 1)
    top = strip[0:24]
    low = jnp.concatenate([strip[24:40], jnp.zeros((8, 128), F32)], axis=0)
    first = jnp.where(lane < 64, top, pltpu.roll(low, 64, 1))
    second = jnp.where(lane < 64, pltpu.roll(top, 64, 1), low)
    return first, second


def unpack_pair(first, second):
    lane = iota((24, 128), 1)
    top = jnp.where(lane < 64, first, pltpu.roll(second, 64, 1))
    low = jnp.where(lane < 64, pltpu.roll(first, 64, 1), second)
    return jnp.concatenate([top, low[0:16]], axis=0)


def kernel(
    hidden,
    attn_gain,
    ffn_gain,
    w_shared,
    w_dt,
    w_x,
    w_z,
    w_attn,
    w_ssm,
    w_gate,
    w_up,
    w_down,
    cache,
    parked,
    freq,
    dt_bias,
    a_log,
    d_skip,
    cache_len,
    accepted,
    slots,
    out_hidden,
    out_kv,
    out_state,
    hid_v,
    ag_v,
    fg_v,
    fr_v,
    wsh_v,
    wdt_v,
    wx_v,
    wz_v,
    wmix_v,
    wg_v,
    wu_v,
    wd_v,
    kv_v,
    pk_v,
    hp_v,
    pj_v,
    q_v,
    nk_v,
    b_v,
    c_v,
    both_v,
    s_v,
    p_v,
    o_v,
    l_v,
    g_v,
    wst_v,
    st_send,
    st_recv,
    at_send,
    at_recv,
    mx_send,
    mx_recv,
    rs_v,
    dn_send,
    dn_recv,
    in_sem,
    kv_sem,
    st_ss,
    st_rs,
    pj_ss,
    pj_rs,
    at_ss,
    at_rs,
    mx_ss,
    mx_rs,
    rs_ss,
    rs_rs,
    dn_ss,
    dn_rs,
):
    g = lax.axis_index("req")
    me = lax.axis_index("blk")
    core = lax.rem(g, 2)

    def owner_of(e):
        return 2 * e + lax.rem(lax.div(e, 2) + core, 2)

    my_z = lax.div(me, 4)
    my_x = lax.rem(me, 4)

    def at_offset(dz, dx):
        return lax.rem(my_z + dz, 8) * 4 + lax.rem(my_x + dx, 4)

    owns = 1 - lax.rem(my_z + my_x + core, 2)
    my_e = lax.div(me, 2)
    parity = lax.rem(me, 2)
    is_owner = owns == 1

    def load(i, src, dst):
        copy = pltpu.make_async_copy(src, dst, in_sem.at[i])
        copy.start()
        return copy

    barrier = pltpu.get_barrier_semaphore()

    for offset in FAR:
        pl.semaphore_signal(
            barrier, inc=1, device_id=(g, at_offset(*offset)), device_id_type=MESH
        )

    def greet_req(k, carry):
        pl.semaphore_signal(
            barrier, inc=1, device_id=(lax.rem(g + k, REQ), me), device_id_type=MESH
        )
        return carry

    lax.fori_loop(1, REQ, greet_req, 0)

    c_hid = load(0, hidden, hid_v)
    c_ag = load(1, attn_gain, ag_v)
    c_wsh = load(2, w_shared, wsh_v)
    c_pk = load(3, parked, pk_v)
    c_wx = load(4, w_x, wx_v.at[pl.ds(0, CH)])
    c_wz = load(5, w_z, wz_v.at[pl.ds(0, CH)])
    c_wdt = load(6, w_dt, wdt_v.at[pl.ds(0, 48)])
    c_fr = load(7, freq, fr_v)
    c_kv = []
    for r in range(R):
        copy = pltpu.make_async_copy(cache.at[r], kv_v.at[r], kv_sem.at[r])
        copy.start()
        c_kv.append(copy)
    c_ws = load(8, w_ssm, wmix_v.at[pl.ds(0, CH)])
    c_wa = load(9, w_attn, wmix_v.at[pl.ds(CH, 32)])
    c_fg = load(10, ffn_gain, fg_v)
    c_wg = load(11, w_gate, wg_v)
    c_wu = load(12, w_up, wu_v)
    c_wd = load(13, w_down, wd_v)

    c_hid.wait()
    c_ag.wait()
    row = iota((ROWS, ROWS), 0)
    col = iota((ROWS, ROWS), 1)
    place = (col == (row & 7) * T + (row >> 3)).astype(F32).astype(BF16)
    hid = jnp.dot(place, hid_v[...], preferred_element_type=F32)
    scaling = lax.rsqrt(jnp.sum(hid * hid, axis=1, keepdims=True) * (1.0 / WIDTH) + EPSILON)
    gain = widen(ag_v[...])
    hid_strips = [hid[:, 128 * e : 128 * (e + 1)] for e in range(STRIPS)]
    normed = jnp.concatenate(
        [(hid_strips[e] * scaling * gain[e : e + 1]).astype(BF16) for e in range(STRIPS)], axis=1
    )
    c_wsh.wait()
    part = lax.dot_general(normed, wsh_v[...], NT, preferred_element_type=F32)
    twice = jnp.concatenate([part, part], axis=1)
    low = jnp.concatenate([twice[24:40], jnp.zeros((8, 128), F32)], axis=0)
    pj_v[me] = jnp.where(iota((24, 128), 1) < 64, twice[0:24], low).astype(BF16)

    pl.semaphore_wait(barrier, BLK - 1 + REQ - 1)

    def blk_copy(src, dst, send, recv, target):
        return pltpu.make_async_remote_copy(
            src_ref=src,
            dst_ref=dst,
            send_sem=send,
            recv_sem=recv,
            device_id=(g, target),
            device_id_type=MESH,
        )

    def arrived(buffer, count, send, recv):
        blocks = buffer.at[pl.ds(0, count)]
        blk_copy(blocks, blocks, send.at[0], recv.at[0], at_offset(0, 1)).wait_recv()

    def left(buffer, count, send, recv):
        blocks = buffer.at[pl.ds(0, count)]
        blk_copy(blocks, blocks, send.at[0], recv.at[0], at_offset(0, 1)).wait_send()

    def pj_copy(k):
        return blk_copy(
            pj_v.at[me], pj_v.at[me], pj_ss.at[0], pj_rs.at[0], at_offset(*FAR[k])
        )

    for k in range(BLK - 1):
        pj_copy(k).start()

    c_pk.wait()

    def st_copy(k):
        target = lax.rem(g + k, REQ)
        return pltpu.make_async_remote_copy(
            src_ref=st_send.at[k],
            dst_ref=st_recv.at[g],
            send_sem=st_ss.at[0],
            recv_sem=st_rs.at[0],
            device_id=(target, me),
            device_id_type=MESH,
        )

    def st_push(k, carry):
        target = lax.rem(g + k, REQ)
        found = jnp.int32(0)
        picks = [jnp.int32(0), jnp.int32(0)]
        for i in range(2, R):
            slot = slots[target * R + i]
            mine = (slot >> 3) == g
            picks[0] = jnp.where(mine & (found == 0), slot & 7, picks[0])
            picks[1] = jnp.where(mine & (found == 1), slot & 7, picks[1])
            found = found + mine.astype(jnp.int32)
        for c in range(2):
            st_send[k, c] = pk_v[picks[c]].astype(BF16)
        st_copy(k).start()
        return carry

    lax.fori_loop(1, REQ, st_push, 0)

    for e in range(STRIPS):
        hp_v[e] = hid_strips[e]
    wx_v[CH:128] = jnp.zeros((128 - CH, WIDTH), BF16)
    wz_v[CH:128] = jnp.zeros((128 - CH, WIDTH), BF16)
    wdt_v[48:128] = jnp.zeros((80, WIDTH), BF16)
    c_wx.wait()
    inner_x = lax.dot_general(normed, wx_v[...], NT, preferred_element_type=F32)
    c_wz.wait()
    inner_z = lax.dot_general(normed, wz_v[...], NT, preferred_element_type=F32)
    c_wdt.wait()
    dt = lax.dot_general(normed, wdt_v[...], NT, preferred_element_type=F32)

    head0 = lax.div(me * CH, 64)
    cut = 64 - lax.rem(me * CH, 64)
    lane1 = iota((1, 128), 1)
    lane = iota((ROWS, 128), 1)

    def by_head(ref):
        return jnp.where(lane1 < cut, ref[head0], ref[head0 + 1])

    dt0 = jnp.sum(jnp.where(lane == head0, dt, 0.0), axis=1, keepdims=True)
    dt1 = jnp.sum(jnp.where(lane == head0 + 1, dt, 0.0), axis=1, keepdims=True)
    raw = jnp.where(lane < cut, dt0, dt1) + by_head(dt_bias)
    steps = jnp.maximum(raw, 0.0) + jnp.log1p(jnp.exp(-jnp.abs(raw)))
    rate = -jnp.exp(by_head(a_log))
    skip = by_head(d_skip)

    c_fr.wait()
    sub24 = iota((24, 128), 0)
    lane24 = iota((24, 128), 1)
    base = jnp.zeros((24, 128), jnp.int32)
    for r in range(R):
        base = jnp.where((sub24 & 7) == r, cache_len[r], base)
    spot = base + (sub24 >> 3) + jnp.where(lane24 < 64, 0, 3)
    angle = spot.astype(F32) * fr_v[...]
    cosine = jnp.cos(angle)
    sine = jnp.sin(angle)

    nk_v[:, 40:128, :] = jnp.zeros((4, 88, 128), F32)
    b_v[:, 40:64, :] = jnp.zeros((2, 24, 128), F32)
    c_v[:, 40:64, :] = jnp.zeros((2, 24, 128), F32)

    arrived(pj_v, BLK - 1, pj_ss, pj_rs)

    def rotated(i):
        first = widen(pj_v[i])
        second = widen(pj_v[i + 1])
        return unpack_pair(
            first * cosine - second * sine, second * cosine + first * sine
        )

    def plain(i):
        return unpack_pair(widen(pj_v[i]), widen(pj_v[i + 1]))

    for h in range(HEADS):
        rows = rotated(2 * h)
        for t in range(T):
            q_v[pl.ds(t * 8 + h, R, stride=ROWS), :] = rows[8 * t : 8 * t + 8]
    for j in range(2):
        nk_v[j, 0:ROWS, :] = rotated(16 + 2 * j)
        nk_v[2 + j, 0:ROWS, :] = plain(20 + 2 * j)
        b_v[j, 0:ROWS, :] = plain(24 + 2 * j)
        c_v[j, 0:ROWS, :] = plain(28 + 2 * j)

    acc_col = jnp.zeros((8, 128), jnp.int32)
    sub8 = iota((8, 128), 0)
    for r in range(R):
        acc_col = jnp.where(sub8 == r, accepted[r], acc_col)
    for t in range(T):
        for j in range(4):
            rows = nk_v[j, 8 * t : 8 * t + 8, :]
            out_kv[t, :, 128 * j : 128 * (j + 1)] = jnp.where(acc_col > t, rows, 0.0).astype(BF16)

    sub40 = iota((ROWS, 128), 0)
    group0 = (sub40 & 7) < 4
    spots = iota((ROWS, EXTENT), 1)
    for r in range(R):
        query = q_v[ROWS * r : ROWS * (r + 1), :]
        both_v[ROWS * r : ROWS * (r + 1), :] = jnp.concatenate(
            [jnp.where(group0, query, 0.0), jnp.where(group0, 0.0, query)], axis=1
        ).astype(BF16)
    new_keys = jnp.concatenate([nk_v[0], nk_v[1]], axis=1).astype(BF16)
    new_scores = lax.dot_general(both_v[...], new_keys, NT, preferred_element_type=F32)
    lanes = iota((ROWS, 128), 1)
    in_order = ((lanes >> 3) <= (sub40 >> 3)) & (me == 0)
    for r in range(R):
        c_kv[r].wait()
        rows = slice(ROWS * r, ROWS * (r + 1))
        scores = lax.dot_general(
            both_v[rows, :], kv_v[r, :, 0:256], NT, preferred_element_type=F32
        )
        s_v[rows, 0:EXTENT] = jnp.where(spots < cache_len[r] - me * EXTENT, scores, NEGATIVE)
        s_v[rows, EXTENT : EXTENT + 128] = jnp.where(
            in_order & ((lanes & 7) == r), new_scores[rows, :], NEGATIVE
        )
    scale = HEAD_SIZE**-0.5
    totals = []
    peaks = []
    for r in range(R):
        rows = slice(ROWS * r, ROWS * (r + 1))
        scores = s_v[rows, :]
        peak = jnp.max(scores, axis=1, keepdims=True)
        weights = jnp.exp2((scores - peak) * (scale * math.log2(math.e)))
        totals.append(jnp.sum(weights, axis=1, keepdims=True))
        peaks.append(peak)
        p_v[rows, :] = weights.astype(BF16)
    new_values = jnp.concatenate([nk_v[2], nk_v[3]], axis=1).astype(BF16)
    new_mixed = jnp.dot(
        p_v[:, EXTENT : EXTENT + 128], new_values, preferred_element_type=F32
    )
    for r in range(R):
        rows = slice(ROWS * r, ROWS * (r + 1))
        mixed = new_mixed[rows, :] + jnp.dot(
            p_v[rows, 0:EXTENT], kv_v[r, :, 256:512], preferred_element_type=F32
        )
        mixed = jnp.where(group0, mixed[:, 0:128], mixed[:, 128:256])
        o_v[rows, :] = mixed / totals[r]
        level = jnp.where(
            peaks[r] > NEGATIVE, peaks[r] * scale + jnp.log(totals[r]), NEGATIVE
        )
        l_v[rows, :] = jnp.broadcast_to(level, (ROWS, 128))

    lane8 = iota((8, 128), 1)
    for h in range(HEADS):
        outs = [o_v[pl.ds(t * 8 + h, R, stride=ROWS), :] for t in range(T)]
        stats = jnp.zeros((8, 128), F32)
        for t in range(T):
            level = l_v[pl.ds(t * 8 + h, R, stride=ROWS), :]
            high = widen(level.astype(BF16))
            middle = widen((level - high).astype(BF16))
            rest = level - high - middle
            stats = jnp.where(lane8 == 32 + t, high, stats)
            stats = jnp.where(lane8 == 40 + t, middle, stats)
            stats = jnp.where(lane8 == 48 + t, rest, stats)
        for q in range(4):
            first = outs[0] if q == 0 else pltpu.roll(outs[0], 128 - 32 * q, 1)
            for j in range(1, 4):
                shift = (32 * (j - q)) % 128
                moved = pltpu.roll(outs[j], shift, 1) if shift else outs[j]
                first = jnp.where(lane8 >= 32 * j, moved, first)
            last = pltpu.roll(outs[4], 128 - 32 * q, 1) if q else outs[4]
            second = jnp.where(lane8 < 32, last, stats)
            at_send[4 * h + q] = jnp.concatenate([first, second], axis=0).astype(BF16)

    def at_copy(k):
        target = at_offset(*FAR[k])
        return blk_copy(at_send.at[target], at_recv.at[me], at_ss.at[0], at_rs.at[0], target)

    for k in range(BLK - 1):
        at_copy(k).start()
    at_recv[me] = at_send[me]

    arrived(st_recv, REQ - 1, st_ss, st_rs)

    step_t = [steps[8 * t : 8 * t + 8] for t in range(T)]
    x_t = [inner_x[8 * t : 8 * t + 8] for t in range(T)]
    dx_t = [step_t[t] * x_t[t] for t in range(T)]
    run_t = [step_t[0]]
    for t in range(1, T):
        run_t.append(run_t[-1] + step_t[t])
    at_accept = jnp.zeros((8, 128), F32)
    for t in range(T):
        at_accept = jnp.where(acc_col == t + 1, run_t[t], at_accept)
    wst_v[...] = jnp.zeros((128, 128), F32)
    for u in range(T):
        past = jnp.where(acc_col > u, rate * (at_accept - run_t[u]), NEGATIVE)
        weight = jnp.exp(past) * dx_t[u]
        wst_v[8 * u : 8 * u + 8, :] = weight
        wst_v[64 + 8 * u : 72 + 8 * u, :] = weight - widen(weight.astype(BF16))
    wst_v[40:48, :] = jnp.exp(rate * at_accept)
    turned = wst_v[...].T
    turned_low = turned[0:CH].astype(BF16)

    b_rows = jnp.concatenate([b_v[0], b_v[1]], axis=1)
    sub64 = iota((64, STATE), 0) & 7
    owners = []
    for r in range(2, R):
        slot = slots[g * R + r]
        own = slot >> 3
        rank = jnp.int32(0)
        for other in owners:
            rank = rank + (other == own).astype(jnp.int32)
        owners.append(own)
    for r in range(R):
        if r < 2:
            start = pk_v[slots[g * R + r] & 7]
        else:
            own = owners[r - 2]
            rank = jnp.int32(0)
            for other in owners[: r - 2]:
                rank = rank + (other == own).astype(jnp.int32)
            start = widen(st_recv[own, jnp.minimum(rank, 1)])
        c_rows = jnp.concatenate(
            [c_v[0, pl.ds(r, 8, stride=8), :], c_v[1, pl.ds(r, 8, stride=8), :]], axis=1
        )
        g_v[8 * r : 8 * r + 8, 0:CH] = lax.dot_general(
            c_rows.astype(BF16), start.astype(BF16), NT, preferred_element_type=F32
        )
        b_mine = jnp.where(sub64 == r, b_rows, 0.0)
        b_twice = jnp.concatenate([b_mine, b_mine], axis=0).astype(BF16)
        grown = jnp.dot(turned_low, b_twice, preferred_element_type=F32)
        out_state[r] = turned[0:CH, 40 + r : 41 + r] * start + grown

    gated_t = []
    for t in range(T):
        y = jnp.exp(rate * run_t[t]) * g_v[pl.ds(t, R, stride=8), :] + skip * x_t[t]
        for u in range(t + 1):
            match = jnp.zeros((8, 1), F32)
            for j in range(2):
                match = match + jnp.sum(
                    c_v[j, 8 * t : 8 * t + 8, :] * b_v[j, 8 * u : 8 * u + 8, :],
                    axis=1,
                    keepdims=True,
                )
            kept = dx_t[u] if u == t else jnp.exp(rate * (run_t[t] - run_t[u])) * dx_t[u]
            y = y + match * kept
        z = inner_z[8 * t : 8 * t + 8]
        gated_t.append(y * (z * (1.0 / (1.0 + jnp.exp(-z)))))

    arrived(at_recv, BLK - 1, at_ss, at_rs)
    parts = widen(at_recv[...])
    stats = parts[:, 8:16, :].reshape(BLK * 8, 128).astype(BF16)
    from_lane = iota((128, 256), 0)
    to_time = iota((128, 256), 1) >> 5
    to_time = jnp.minimum(to_time, 4)
    spread = (
        (from_lane == 32 + to_time) | (from_lane == 40 + to_time) | (from_lane == 48 + to_time)
    )
    level = jnp.dot(
        stats, spread.astype(F32).astype(BF16), preferred_element_type=F32
    ).reshape(BLK, 8, 256)
    top = jnp.max(level, axis=0, keepdims=True)
    share = jnp.exp(level - top)
    values = jnp.concatenate([parts[:, 0:8, :], parts[:, 8:16, :]], axis=2)
    merged = jnp.sum(share * values, axis=0) / jnp.sum(share, axis=0)
    mix_t = []
    for t in range(T):
        piece = merged[:, 0:128] if t < 4 else merged[:, 128:256]
        shift = (96 - 32 * t) % 128 if t < 4 else 96
        moved = pltpu.roll(piece, shift, 1) if shift else piece
        mix_t.append(jnp.where(lane8 < CH, gated_t[t], moved))
    mix_in = jnp.concatenate(mix_t, axis=0).astype(BF16)

    c_ws.wait()
    c_wa.wait()
    for e in range(0, STRIPS, 2):
        pair = jnp.dot(
            mix_in, wmix_v[:, 128 * e : 128 * (e + 2)], preferred_element_type=F32
        ).astype(BF16)
        mx_send[e] = pair[:, 0:128]
        mx_send[e + 1] = pair[:, 128:256]

    def mx_copy(k):
        odd = FAR_ODD[k]
        even = FAR_EVEN[k] if k < STRIPS - 1 else odd
        target = at_offset(
            odd[0] + owns * (even[0] - odd[0]), odd[1] + owns * (even[1] - odd[1])
        )
        return blk_copy(
            mx_send.at[lax.div(target, 2)], mx_recv.at[me], mx_ss.at[0], mx_rs.at[0], target
        )

    for k in range(STRIPS - 1):
        mx_copy(k).start()

    @pl.when(jnp.logical_not(is_owner))
    def _():
        mx_copy(STRIPS - 1).start()

    def rs_copy(k):
        return blk_copy(
            rs_v.at[my_e], rs_v.at[my_e], rs_ss.at[0], rs_rs.at[0], at_offset(*FAR[k])
        )

    @pl.when(is_owner)
    def _():
        mx_recv[me] = mx_send[my_e]
        arrived(mx_recv, BLK - 1, mx_ss, mx_rs)
        total = jnp.sum(widen(mx_recv[...]), axis=0)
        rs_v[my_e] = (hp_v[my_e] + total).astype(BF16)

        for k in range(BLK - 1):
            rs_copy(k).start()

    c_fg.wait()
    c_wg.wait()
    c_wu.wait()
    c_wd.wait()

    @pl.when(is_owner)
    def _():
        arrived(rs_v, STRIPS - 1, rs_ss, rs_rs)

    @pl.when(jnp.logical_not(is_owner))
    def _():
        arrived(rs_v, STRIPS, rs_ss, rs_rs)


    resid = [widen(rs_v[e]) for e in range(STRIPS)]
    squares = resid[0] * resid[0]
    for e in range(1, STRIPS):
        squares = squares + resid[e] * resid[e]
    scaling2 = lax.rsqrt(jnp.sum(squares, axis=1, keepdims=True) * (1.0 / WIDTH) + EPSILON)
    gain2 = widen(fg_v[...])
    normed2 = jnp.concatenate(
        [(resid[e] * scaling2 * gain2[e : e + 1]).astype(BF16) for e in range(STRIPS)], axis=1
    )
    gate = jnp.dot(normed2, wg_v[...], preferred_element_type=F32)
    up = jnp.dot(normed2, wu_v[...], preferred_element_type=F32)
    inner = (gate * (1.0 / (1.0 + jnp.exp(-gate))) * up).astype(BF16)
    for e in range(0, STRIPS, 2):
        pair = jnp.dot(inner, wd_v[:, 128 * e : 128 * (e + 2)], preferred_element_type=F32)
        for i in range(2):
            first, second = pack_pair(pair[:, 128 * i : 128 * (i + 1)])
            dn_send[2 * (e + i)] = first.astype(BF16)
            dn_send[2 * (e + i) + 1] = second.astype(BF16)

    def dn_copy(k):
        target = at_offset(*FAR[k])
        return blk_copy(dn_send.at[target], dn_recv.at[me], dn_ss.at[0], dn_rs.at[0], target)

    for k in range(BLK - 1):
        dn_copy(k).start()
    dn_recv[me] = dn_send[me]
    own_even, own_odd = pack_pair(widen(rs_v[my_e]))
    own = jnp.where(parity == 0, own_even, own_odd)

    left(pj_v, BLK - 1, pj_ss, pj_rs)
    left(st_send, REQ - 1, st_ss, st_rs)
    left(at_send, BLK - 1, at_ss, at_rs)

    @pl.when(is_owner)
    def _():
        left(mx_send, STRIPS - 1, mx_ss, mx_rs)
        left(mx_recv, BLK - 1, rs_ss, rs_rs)

    @pl.when(jnp.logical_not(is_owner))
    def _():
        left(mx_send, STRIPS, mx_ss, mx_rs)

    arrived(dn_recv, BLK - 1, dn_ss, dn_rs)
    done = own + jnp.sum(widen(dn_recv[...]), axis=0)
    done = jnp.concatenate([done, pltpu.roll(done, 64, 1)[0:16]], axis=0).astype(BF16)
    back = (row == (col & 7) * T + (col >> 3)).astype(F32).astype(BF16)
    out_hidden[...] = jnp.dot(back, done, preferred_element_type=F32)[:, 0:64].astype(BF16)

    left(dn_send, BLK - 1, dn_ss, dn_rs)


def handoff(hidden, kv, state, hidden_out, kv_out, state_out, sem):
    copies = [
        pltpu.make_async_copy(state.at[r], state_out.at[r], sem.at[2 + r]) for r in range(R)
    ]
    copies.append(pltpu.make_async_copy(kv, kv_out, sem.at[1]))
    copies.append(pltpu.make_async_copy(hidden, hidden_out, sem.at[0]))
    for copy in copies:
        copy.start()
    for copy in copies:
        copy.wait()


def body(
    hidden,
    attn_gain,
    ffn_gain,
    shared_weight,
    w_dt,
    dt_bias,
    a_log,
    d_skip,
    w_inner_x,
    w_inner_z,
    w_attn_out,
    w_ssm_out,
    w_gate,
    w_up,
    w_down,
    key_value_cache,
    cache_len,
    accepted,
    parked,
    source_slot,
):
    half = HEAD_SIZE // 2
    exponent = np.arange(128) % half * 2.0 / HEAD_SIZE
    freq = jnp.asarray(np.power(ROPE_THETA, -exponent).astype(np.float32).reshape(1, 128))
    anywhere = pl.BlockSpec(memory_space=pltpu.HBM)
    scalars = pl.BlockSpec(memory_space=pltpu.SMEM)
    vm = pltpu.VMEM
    dma = pltpu.SemaphoreType.DMA
    shapes = (
        jax.ShapeDtypeStruct((ROWS, WIDTH // BLK), BF16),
        jax.ShapeDtypeStruct((T, R, 512), BF16),
        jax.ShapeDtypeStruct((R, CH, STATE), F32),
    )
    outs = pl.pallas_call(
        kernel,
        out_shape=tuple(vm(shape.shape, shape.dtype) for shape in shapes),
        in_specs=[anywhere] * 15 + [scalars] * 6,
        out_specs=(pl.BlockSpec(memory_space=vm),) * 3,
        scratch_shapes=[
            vm((ROWS, WIDTH), BF16),
            vm((STRIPS, 128), BF16),
            vm((STRIPS, 128), BF16),
            vm((1, 128), F32),
            vm((64, WIDTH), BF16),
            vm((128, WIDTH), BF16),
            vm((128, WIDTH), BF16),
            vm((128, WIDTH), BF16),
            vm((128, WIDTH), BF16),
            vm((WIDTH, 128), BF16),
            vm((WIDTH, 128), BF16),
            vm((128, WIDTH), BF16),
            vm((R, EXTENT, 512), BF16),
            vm((R, CH, STATE), F32),
            vm((STRIPS, ROWS, 128), F32),
            vm((BLK, 24, 128), BF16),
            vm((R * ROWS, 128), F32),
            vm((4, 128, 128), F32),
            vm((2, 64, 128), F32),
            vm((2, 64, 128), F32),
            vm((R * ROWS, 256), BF16),
            vm((R * ROWS, EXTENT + 128), F32),
            vm((R * ROWS, EXTENT + 128), BF16),
            vm((R * ROWS, 128), F32),
            vm((R * ROWS, 128), F32),
            vm((64, 128), F32),
            vm((128, 128), F32),
            vm((REQ, 2, CH, STATE), BF16),
            vm((REQ, 2, CH, STATE), BF16),
            vm((BLK, 16, 128), BF16),
            vm((BLK, 16, 128), BF16),
            vm((STRIPS, ROWS, 128), BF16),
            vm((BLK, ROWS, 128), BF16),
            vm((STRIPS, ROWS, 128), BF16),
            vm((BLK, 24, 128), BF16),
            vm((BLK, 24, 128), BF16),
            dma((14,)),
            dma((R,)),
            dma((1,)),
            dma((1,)),
            dma((1,)),
            dma((1,)),
            dma((1,)),
            dma((1,)),
            dma((1,)),
            dma((1,)),
            dma((1,)),
            dma((1,)),
            dma((1,)),
            dma((1,)),
        ],
        compiler_params=pltpu.CompilerParams(
            collective_id=0, has_side_effects=True, vmem_limit_bytes=63000000
        ),
        name="layer",
    )(
        hidden,
        attn_gain.reshape(STRIPS, 128),
        ffn_gain.reshape(STRIPS, 128),
        shared_weight.T,
        w_dt.T,
        w_inner_x.T,
        w_inner_z.T,
        w_attn_out,
        w_ssm_out,
        w_gate,
        w_up,
        w_down,
        key_value_cache,
        parked,
        freq,
        dt_bias,
        a_log,
        d_skip,
        cache_len,
        accepted,
        source_slot,
    )
    outs = pl.pallas_call(
        handoff,
        out_shape=shapes,
        in_specs=[pl.BlockSpec(memory_space=vm)] * 3,
        out_specs=(anywhere,) * 3,
        scratch_shapes=[dma((2 + R,))],
        compiler_params=pltpu.CompilerParams(vmem_limit_bytes=1000000),
        name="handoff",
    )(*outs)
    return outs[0], outs[1].transpose(1, 0, 2), outs[2]


def solution(mesh):
    placed = (
        P("req", None),
        P(),
        P(),
        P(None, "blk"),
        P(),
        P(),
        P(),
        P(),
        P(None, "blk"),
        P(None, "blk"),
        P("blk", None),
        P("blk", None),
        P(None, "blk"),
        P(None, "blk"),
        P("blk", None),
        P("req", "blk", None),
        P("req"),
        P("req"),
        P("req", "blk", None),
        P(),
    )
    return jax.shard_map(
        body,
        mesh=mesh,
        in_specs=placed,
        out_specs=(P("req", "blk"), P("req", None, None), P("req", "blk", None)),
        check_vma=False,
    )
```

```python
import math

import jax
import jax.numpy as jnp
import numpy as np
from jax import lax
from jax.experimental import pallas as pl
from jax.experimental.pallas import tpu as pltpu
from jax.sharding import PartitionSpec as P

HEADS = 8
HEAD_SIZE = 128
T = 5
R = 8
ROWS = R * T
BLK = 32
REQ = 8
WIDTH = 2048
STRIPS = WIDTH // 128
EXTENT = 512
CH = 96
STATE = 256
EPSILON = 1e-05
ROPE_THETA = 100000000000.0
NEGATIVE = -1e30
MESH = pl.DeviceIdType.MESH
F32 = jnp.float32
BF16 = jnp.bfloat16

NT = (((1,), (1,)), ((), ()))

FAR = sorted(
    [(dz, dx) for dz in range(8) for dx in range(4) if dz or dx],
    key=lambda o: -(min(o[0], 8 - o[0]) + min(o[1], 4 - o[1])),
)
FAR_EVEN = [o for o in FAR if (o[0] + o[1]) % 2 == 0]
FAR_ODD = [o for o in FAR if (o[0] + o[1]) % 2 == 1]


def iota(shape, dim):
    return lax.broadcasted_iota(jnp.int32, shape, dim)


def widen(values):
    return values.astype(F32)


def pack_pair(strip):
    lane = iota((24, 128), 1)
    top = strip[0:24]
    low = jnp.concatenate([strip[24:40], jnp.zeros((8, 128), F32)], axis=0)
    first = jnp.where(lane < 64, top, pltpu.roll(low, 64, 1))
    second = jnp.where(lane < 64, pltpu.roll(top, 64, 1), low)
    return first, second


def unpack_pair(first, second):
    lane = iota((24, 128), 1)
    top = jnp.where(lane < 64, first, pltpu.roll(second, 64, 1))
    low = jnp.where(lane < 64, pltpu.roll(first, 64, 1), second)
    return jnp.concatenate([top, low[0:16]], axis=0)


def kernel(
    hidden,
    attn_gain,
    ffn_gain,
    w_shared,
    w_dt,
    w_x,
    w_z,
    w_attn,
    w_ssm,
    w_gate,
    w_up,
    w_down,
    cache,
    parked,
    freq,
    dt_bias_h,
    a_log_h,
    d_skip_h,
    cache_len_h,
    accepted_h,
    slots_h,
    out_hidden,
    out_kv,
    out_state,
    hid_v,
    dt_bias,
    a_log,
    d_skip,
    cache_len,
    accepted,
    slots,
    ag_v,
    fg_v,
    fr_v,
    wsh_v,
    wdt_v,
    wx_v,
    wz_v,
    wmix_v,
    wg_v,
    wu_v,
    wd_v,
    kv_v,
    pk_v,
    hp_v,
    pj_v,
    q_v,
    nk_v,
    b_v,
    c_v,
    both_v,
    s_v,
    p_v,
    o_v,
    l_v,
    g_v,
    wst_v,
    st_send,
    st_recv,
    at_send,
    at_recv,
    mx_send,
    mx_recv,
    rs_v,
    dn_send,
    dn_recv,
    in_sem,
    kv_sem,
    st_ss,
    st_rs,
    pj_ss,
    pj_rs,
    at_ss,
    at_rs,
    mx_ss,
    mx_rs,
    rs_ss,
    rs_rs,
    dn_ss,
    dn_rs,
):
    g = lax.axis_index("req")
    me = lax.axis_index("blk")
    core = lax.rem(g, 2)

    def owner_of(e):
        return 2 * e + lax.rem(lax.div(e, 2) + core, 2)

    my_z = lax.div(me, 4)
    my_x = lax.rem(me, 4)

    def at_offset(dz, dx):
        return lax.rem(my_z + dz, 8) * 4 + lax.rem(my_x + dx, 4)

    owns = 1 - lax.rem(my_z + my_x + core, 2)
    my_e = lax.div(me, 2)
    parity = lax.rem(me, 2)
    is_owner = owns == 1

    def load(i, src, dst):
        copy = pltpu.make_async_copy(src, dst, in_sem.at[i])
        copy.start()
        return copy

    barrier = pltpu.get_barrier_semaphore()

    for offset in FAR:
        pl.semaphore_signal(
            barrier, inc=1, device_id=(g, at_offset(*offset)), device_id_type=MESH
        )

    def greet_req(k, carry):
        pl.semaphore_signal(
            barrier, inc=1, device_id=(lax.rem(g + k, REQ), me), device_id_type=MESH
        )
        return carry

    lax.fori_loop(1, REQ, greet_req, 0)

    c_hid = load(0, hidden, hid_v)
    c_ag = load(1, attn_gain, ag_v)
    c_wsh = load(2, w_shared, wsh_v)
    c_small = [
        load(14, slots_h, slots),
        load(15, cache_len_h, cache_len),
        load(16, accepted_h, accepted),
        load(17, dt_bias_h, dt_bias),
        load(18, a_log_h, a_log),
        load(19, d_skip_h, d_skip),
    ]
    c_pk = load(3, parked, pk_v)
    c_wx = load(4, w_x, wx_v.at[pl.ds(0, CH)])
    c_wz = load(5, w_z, wz_v.at[pl.ds(0, CH)])
    c_wdt = load(6, w_dt, wdt_v.at[pl.ds(0, 48)])
    c_fr = load(7, freq, fr_v)
    c_kv = []
    for r in range(R):
        copy = pltpu.make_async_copy(cache.at[r], kv_v.at[r], kv_sem.at[r])
        copy.start()
        c_kv.append(copy)
    c_ws = load(8, w_ssm, wmix_v.at[pl.ds(0, CH)])
    c_wa = load(9, w_attn, wmix_v.at[pl.ds(CH, 32)])
    c_fg = load(10, ffn_gain, fg_v)
    c_wg = load(11, w_gate, wg_v)
    c_wu = load(12, w_up, wu_v)
    c_wd = load(13, w_down, wd_v)

    c_hid.wait()
    c_ag.wait()
    row = iota((ROWS, ROWS), 0)
    col = iota((ROWS, ROWS), 1)
    place = (col == (row & 7) * T + (row >> 3)).astype(F32).astype(BF16)
    hid = jnp.dot(place, hid_v[...], preferred_element_type=F32)
    scaling = lax.rsqrt(jnp.sum(hid * hid, axis=1, keepdims=True) * (1.0 / WIDTH) + EPSILON)
    gain = widen(ag_v[...])
    hid_strips = [hid[:, 128 * e : 128 * (e + 1)] for e in range(STRIPS)]
    normed = jnp.concatenate(
        [(hid_strips[e] * scaling * gain[e : e + 1]).astype(BF16) for e in range(STRIPS)], axis=1
    )
    c_wsh.wait()
    part = lax.dot_general(normed, wsh_v[...], NT, preferred_element_type=F32)
    twice = jnp.concatenate([part, part], axis=1)
    low = jnp.concatenate([twice[24:40], jnp.zeros((8, 128), F32)], axis=0)
    pj_v[me] = jnp.where(iota((24, 128), 1) < 64, twice[0:24], low).astype(BF16)

    pl.semaphore_wait(barrier, BLK - 1 + REQ - 1)

    def blk_copy(src, dst, send, recv, target):
        return pltpu.make_async_remote_copy(
            src_ref=src,
            dst_ref=dst,
            send_sem=send,
            recv_sem=recv,
            device_id=(g, target),
            device_id_type=MESH,
        )

    def arrived(buffer, count, send, recv):
        blocks = buffer.at[pl.ds(0, count)]
        blk_copy(blocks, blocks, send.at[0], recv.at[0], at_offset(0, 1)).wait_recv()

    def left(buffer, count, send, recv):
        blocks = buffer.at[pl.ds(0, count)]
        blk_copy(blocks, blocks, send.at[0], recv.at[0], at_offset(0, 1)).wait_send()

    def pj_copy(k):
        return blk_copy(
            pj_v.at[me], pj_v.at[me], pj_ss.at[0], pj_rs.at[0], at_offset(*FAR[k])
        )

    for k in range(BLK - 1):
        pj_copy(k).start()

    for copy in c_small:
        copy.wait()
    c_pk.wait()

    def st_copy(k):
        target = lax.rem(g + k, REQ)
        return pltpu.make_async_remote_copy(
            src_ref=st_send.at[k],
            dst_ref=st_recv.at[g],
            send_sem=st_ss.at[0],
            recv_sem=st_rs.at[0],
            device_id=(target, me),
            device_id_type=MESH,
        )

    def st_push(k, carry):
        target = lax.rem(g + k, REQ)
        found = jnp.int32(0)
        picks = [jnp.int32(0), jnp.int32(0)]
        for i in range(2, R):
            slot = slots[target * R + i]
            mine = (slot >> 3) == g
            picks[0] = jnp.where(mine & (found == 0), slot & 7, picks[0])
            picks[1] = jnp.where(mine & (found == 1), slot & 7, picks[1])
            found = found + mine.astype(jnp.int32)
        for c in range(2):
            st_send[k, c] = pk_v[picks[c]].astype(BF16)
        st_copy(k).start()
        return carry

    lax.fori_loop(1, REQ, st_push, 0)

    for e in range(STRIPS):
        hp_v[e] = hid_strips[e]
    wx_v[CH:128] = jnp.zeros((128 - CH, WIDTH), BF16)
    wz_v[CH:128] = jnp.zeros((128 - CH, WIDTH), BF16)
    wdt_v[48:128] = jnp.zeros((80, WIDTH), BF16)
    c_wx.wait()
    inner_x = lax.dot_general(normed, wx_v[...], NT, preferred_element_type=F32)
    c_wz.wait()
    inner_z = lax.dot_general(normed, wz_v[...], NT, preferred_element_type=F32)
    c_wdt.wait()
    dt = lax.dot_general(normed, wdt_v[...], NT, preferred_element_type=F32)

    head0 = lax.div(me * CH, 64)
    cut = 64 - lax.rem(me * CH, 64)
    lane1 = iota((1, 128), 1)
    lane = iota((ROWS, 128), 1)

    def by_head(ref):
        return jnp.where(lane1 < cut, ref[head0], ref[head0 + 1])

    dt0 = jnp.sum(jnp.where(lane == head0, dt, 0.0), axis=1, keepdims=True)
    dt1 = jnp.sum(jnp.where(lane == head0 + 1, dt, 0.0), axis=1, keepdims=True)
    raw = jnp.where(lane < cut, dt0, dt1) + by_head(dt_bias)
    steps = jnp.maximum(raw, 0.0) + jnp.log1p(jnp.exp(-jnp.abs(raw)))
    rate = -jnp.exp(by_head(a_log))
    skip = by_head(d_skip)

    c_fr.wait()
    sub24 = iota((24, 128), 0)
    lane24 = iota((24, 128), 1)
    base = jnp.zeros((24, 128), jnp.int32)
    for r in range(R):
        base = jnp.where((sub24 & 7) == r, cache_len[r], base)
    spot = base + (sub24 >> 3) + jnp.where(lane24 < 64, 0, 3)
    angle = spot.astype(F32) * fr_v[...]
    cosine = jnp.cos(angle)
    sine = jnp.sin(angle)

    nk_v[:, 40:128, :] = jnp.zeros((4, 88, 128), F32)
    b_v[:, 40:64, :] = jnp.zeros((2, 24, 128), F32)
    c_v[:, 40:64, :] = jnp.zeros((2, 24, 128), F32)

    arrived(pj_v, BLK - 1, pj_ss, pj_rs)

    def rotated(i):
        first = widen(pj_v[i])
        second = widen(pj_v[i + 1])
        return unpack_pair(
            first * cosine - second * sine, second * cosine + first * sine
        )

    def plain(i):
        return unpack_pair(widen(pj_v[i]), widen(pj_v[i + 1]))

    for h in range(HEADS):
        rows = rotated(2 * h)
        for t in range(T):
            q_v[pl.ds(t * 8 + h, R, stride=ROWS), :] = rows[8 * t : 8 * t + 8]
    for j in range(2):
        nk_v[j, 0:ROWS, :] = rotated(16 + 2 * j)
        nk_v[2 + j, 0:ROWS, :] = plain(20 + 2 * j)
        b_v[j, 0:ROWS, :] = plain(24 + 2 * j)
        c_v[j, 0:ROWS, :] = plain(28 + 2 * j)

    acc_col = jnp.zeros((8, 128), jnp.int32)
    sub8 = iota((8, 128), 0)
    for r in range(R):
        acc_col = jnp.where(sub8 == r, accepted[r], acc_col)
    for t in range(T):
        for j in range(4):
            rows = nk_v[j, 8 * t : 8 * t + 8, :]
            out_kv[t, :, 128 * j : 128 * (j + 1)] = jnp.where(acc_col > t, rows, 0.0).astype(BF16)

    sub40 = iota((ROWS, 128), 0)
    group0 = (sub40 & 7) < 4
    spots = iota((ROWS, EXTENT), 1)
    for r in range(R):
        query = q_v[ROWS * r : ROWS * (r + 1), :]
        both_v[ROWS * r : ROWS * (r + 1), :] = jnp.concatenate(
            [jnp.where(group0, query, 0.0), jnp.where(group0, 0.0, query)], axis=1
        ).astype(BF16)
    new_keys = jnp.concatenate([nk_v[0], nk_v[1]], axis=1).astype(BF16)
    new_scores = lax.dot_general(both_v[...], new_keys, NT, preferred_element_type=F32)
    lanes = iota((ROWS, 128), 1)
    in_order = ((lanes >> 3) <= (sub40 >> 3)) & (me == 0)
    for r in range(R):
        c_kv[r].wait()
        rows = slice(ROWS * r, ROWS * (r + 1))
        scores = lax.dot_general(
            both_v[rows, :], kv_v[r, :, 0:256], NT, preferred_element_type=F32
        )
        s_v[rows, 0:EXTENT] = jnp.where(spots < cache_len[r] - me * EXTENT, scores, NEGATIVE)
        s_v[rows, EXTENT : EXTENT + 128] = jnp.where(
            in_order & ((lanes & 7) == r), new_scores[rows, :], NEGATIVE
        )
    scale = HEAD_SIZE**-0.5
    totals = []
    peaks = []
    for r in range(R):
        rows = slice(ROWS * r, ROWS * (r + 1))
        scores = s_v[rows, :]
        peak = jnp.max(scores, axis=1, keepdims=True)
        weights = jnp.exp2((scores - peak) * (scale * math.log2(math.e)))
        totals.append(jnp.sum(weights, axis=1, keepdims=True))
        peaks.append(peak)
        p_v[rows, :] = weights.astype(BF16)
    new_values = jnp.concatenate([nk_v[2], nk_v[3]], axis=1).astype(BF16)
    new_mixed = jnp.dot(
        p_v[:, EXTENT : EXTENT + 128], new_values, preferred_element_type=F32
    )
    for r in range(R):
        rows = slice(ROWS * r, ROWS * (r + 1))
        mixed = new_mixed[rows, :] + jnp.dot(
            p_v[rows, 0:EXTENT], kv_v[r, :, 256:512], preferred_element_type=F32
        )
        mixed = jnp.where(group0, mixed[:, 0:128], mixed[:, 128:256])
        o_v[rows, :] = mixed / totals[r]
        level = jnp.where(
            peaks[r] > NEGATIVE, peaks[r] * scale + jnp.log(totals[r]), NEGATIVE
        )
        l_v[rows, :] = jnp.broadcast_to(level, (ROWS, 128))

    lane8 = iota((8, 128), 1)
    for h in range(HEADS):
        outs = [o_v[pl.ds(t * 8 + h, R, stride=ROWS), :] for t in range(T)]
        stats = jnp.zeros((8, 128), F32)
        for t in range(T):
            level = l_v[pl.ds(t * 8 + h, R, stride=ROWS), :]
            high = widen(level.astype(BF16))
            middle = widen((level - high).astype(BF16))
            rest = level - high - middle
            stats = jnp.where(lane8 == 32 + t, high, stats)
            stats = jnp.where(lane8 == 40 + t, middle, stats)
            stats = jnp.where(lane8 == 48 + t, rest, stats)
        for q in range(4):
            first = outs[0] if q == 0 else pltpu.roll(outs[0], 128 - 32 * q, 1)
            for j in range(1, 4):
                shift = (32 * (j - q)) % 128
                moved = pltpu.roll(outs[j], shift, 1) if shift else outs[j]
                first = jnp.where(lane8 >= 32 * j, moved, first)
            last = pltpu.roll(outs[4], 128 - 32 * q, 1) if q else outs[4]
            second = jnp.where(lane8 < 32, last, stats)
            at_send[4 * h + q] = jnp.concatenate([first, second], axis=0).astype(BF16)

    def at_copy(k):
        target = at_offset(*FAR[k])
        return blk_copy(at_send.at[target], at_recv.at[me], at_ss.at[0], at_rs.at[0], target)

    for k in range(BLK - 1):
        at_copy(k).start()
    at_recv[me] = at_send[me]

    arrived(st_recv, REQ - 1, st_ss, st_rs)

    step_t = [steps[8 * t : 8 * t + 8] for t in range(T)]
    x_t = [inner_x[8 * t : 8 * t + 8] for t in range(T)]
    dx_t = [step_t[t] * x_t[t] for t in range(T)]
    run_t = [step_t[0]]
    for t in range(1, T):
        run_t.append(run_t[-1] + step_t[t])
    at_accept = jnp.zeros((8, 128), F32)
    for t in range(T):
        at_accept = jnp.where(acc_col == t + 1, run_t[t], at_accept)
    wst_v[...] = jnp.zeros((128, 128), F32)
    for u in range(T):
        past = jnp.where(acc_col > u, rate * (at_accept - run_t[u]), NEGATIVE)
        weight = jnp.exp(past) * dx_t[u]
        wst_v[8 * u : 8 * u + 8, :] = weight
        wst_v[64 + 8 * u : 72 + 8 * u, :] = weight - widen(weight.astype(BF16))
    wst_v[40:48, :] = jnp.exp(rate * at_accept)
    turned = wst_v[...].T
    turned_low = turned[0:CH].astype(BF16)

    b_rows = jnp.concatenate([b_v[0], b_v[1]], axis=1)
    sub64 = iota((64, STATE), 0) & 7
    owners = []
    for r in range(2, R):
        slot = slots[g * R + r]
        own = slot >> 3
        rank = jnp.int32(0)
        for other in owners:
            rank = rank + (other == own).astype(jnp.int32)
        owners.append(own)
    for r in range(R):
        if r < 2:
            start = pk_v[slots[g * R + r] & 7]
        else:
            own = owners[r - 2]
            rank = jnp.int32(0)
            for other in owners[: r - 2]:
                rank = rank + (other == own).astype(jnp.int32)
            start = widen(st_recv[own, jnp.minimum(rank, 1)])
        c_rows = jnp.concatenate(
            [c_v[0, pl.ds(r, 8, stride=8), :], c_v[1, pl.ds(r, 8, stride=8), :]], axis=1
        )
        g_v[8 * r : 8 * r + 8, 0:CH] = lax.dot_general(
            c_rows.astype(BF16), start.astype(BF16), NT, preferred_element_type=F32
        )
        b_mine = jnp.where(sub64 == r, b_rows, 0.0)
        b_twice = jnp.concatenate([b_mine, b_mine], axis=0).astype(BF16)
        grown = jnp.dot(turned_low, b_twice, preferred_element_type=F32)
        out_state[r] = turned[0:CH, 40 + r : 41 + r] * start + grown

    gated_t = []
    for t in range(T):
        y = jnp.exp(rate * run_t[t]) * g_v[pl.ds(t, R, stride=8), :] + skip * x_t[t]
        for u in range(t + 1):
            match = jnp.zeros((8, 1), F32)
            for j in range(2):
                match = match + jnp.sum(
                    c_v[j, 8 * t : 8 * t + 8, :] * b_v[j, 8 * u : 8 * u + 8, :],
                    axis=1,
                    keepdims=True,
                )
            kept = dx_t[u] if u == t else jnp.exp(rate * (run_t[t] - run_t[u])) * dx_t[u]
            y = y + match * kept
        z = inner_z[8 * t : 8 * t + 8]
        gated_t.append(y * (z * (1.0 / (1.0 + jnp.exp(-z)))))

    arrived(at_recv, BLK - 1, at_ss, at_rs)
    parts = widen(at_recv[...])
    stats = parts[:, 8:16, :].reshape(BLK * 8, 128).astype(BF16)
    from_lane = iota((128, 256), 0)
    to_time = iota((128, 256), 1) >> 5
    to_time = jnp.minimum(to_time, 4)
    spread = (
        (from_lane == 32 + to_time) | (from_lane == 40 + to_time) | (from_lane == 48 + to_time)
    )
    level = jnp.dot(
        stats, spread.astype(F32).astype(BF16), preferred_element_type=F32
    ).reshape(BLK, 8, 256)
    top = jnp.max(level, axis=0, keepdims=True)
    share = jnp.exp(level - top)
    values = jnp.concatenate([parts[:, 0:8, :], parts[:, 8:16, :]], axis=2)
    merged = jnp.sum(share * values, axis=0) / jnp.sum(share, axis=0)
    mix_t = []
    for t in range(T):
        piece = merged[:, 0:128] if t < 4 else merged[:, 128:256]
        shift = (96 - 32 * t) % 128 if t < 4 else 96
        moved = pltpu.roll(piece, shift, 1) if shift else piece
        mix_t.append(jnp.where(lane8 < CH, gated_t[t], moved))
    mix_in = jnp.concatenate(mix_t, axis=0).astype(BF16)

    c_ws.wait()
    c_wa.wait()
    for e in range(0, STRIPS, 2):
        pair = jnp.dot(
            mix_in, wmix_v[:, 128 * e : 128 * (e + 2)], preferred_element_type=F32
        ).astype(BF16)
        mx_send[e] = pair[:, 0:128]
        mx_send[e + 1] = pair[:, 128:256]

    def mx_copy(k):
        odd = FAR_ODD[k]
        even = FAR_EVEN[k] if k < STRIPS - 1 else odd
        target = at_offset(
            odd[0] + owns * (even[0] - odd[0]), odd[1] + owns * (even[1] - odd[1])
        )
        return blk_copy(
            mx_send.at[lax.div(target, 2)], mx_recv.at[me], mx_ss.at[0], mx_rs.at[0], target
        )

    for k in range(STRIPS - 1):
        mx_copy(k).start()

    @pl.when(jnp.logical_not(is_owner))
    def _():
        mx_copy(STRIPS - 1).start()

    def rs_copy(k):
        return blk_copy(
            rs_v.at[my_e], rs_v.at[my_e], rs_ss.at[0], rs_rs.at[0], at_offset(*FAR[k])
        )

    @pl.when(is_owner)
    def _():
        mx_recv[me] = mx_send[my_e]
        arrived(mx_recv, BLK - 1, mx_ss, mx_rs)
        total = jnp.sum(widen(mx_recv[...]), axis=0)
        rs_v[my_e] = (hp_v[my_e] + total).astype(BF16)

        for k in range(BLK - 1):
            rs_copy(k).start()

    c_fg.wait()
    c_wg.wait()
    c_wu.wait()
    c_wd.wait()

    @pl.when(is_owner)
    def _():
        arrived(rs_v, STRIPS - 1, rs_ss, rs_rs)

    @pl.when(jnp.logical_not(is_owner))
    def _():
        arrived(rs_v, STRIPS, rs_ss, rs_rs)


    resid = [widen(rs_v[e]) for e in range(STRIPS)]
    squares = resid[0] * resid[0]
    for e in range(1, STRIPS):
        squares = squares + resid[e] * resid[e]
    scaling2 = lax.rsqrt(jnp.sum(squares, axis=1, keepdims=True) * (1.0 / WIDTH) + EPSILON)
    gain2 = widen(fg_v[...])
    normed2 = jnp.concatenate(
        [(resid[e] * scaling2 * gain2[e : e + 1]).astype(BF16) for e in range(STRIPS)], axis=1
    )
    gate = jnp.dot(normed2, wg_v[...], preferred_element_type=F32)
    up = jnp.dot(normed2, wu_v[...], preferred_element_type=F32)
    inner = (gate * (1.0 / (1.0 + jnp.exp(-gate))) * up).astype(BF16)
    for e in range(0, STRIPS, 2):
        pair = jnp.dot(inner, wd_v[:, 128 * e : 128 * (e + 2)], preferred_element_type=F32)
        for i in range(2):
            first, second = pack_pair(pair[:, 128 * i : 128 * (i + 1)])
            dn_send[2 * (e + i)] = first.astype(BF16)
            dn_send[2 * (e + i) + 1] = second.astype(BF16)

    def dn_copy(k):
        target = at_offset(*FAR[k])
        return blk_copy(dn_send.at[target], dn_recv.at[me], dn_ss.at[0], dn_rs.at[0], target)

    for k in range(BLK - 1):
        dn_copy(k).start()
    dn_recv[me] = dn_send[me]
    own_even, own_odd = pack_pair(widen(rs_v[my_e]))
    own = jnp.where(parity == 0, own_even, own_odd)

    left(pj_v, BLK - 1, pj_ss, pj_rs)
    left(st_send, REQ - 1, st_ss, st_rs)
    left(at_send, BLK - 1, at_ss, at_rs)

    @pl.when(is_owner)
    def _():
        left(mx_send, STRIPS - 1, mx_ss, mx_rs)
        left(mx_recv, BLK - 1, rs_ss, rs_rs)

    @pl.when(jnp.logical_not(is_owner))
    def _():
        left(mx_send, STRIPS, mx_ss, mx_rs)

    arrived(dn_recv, BLK - 1, dn_ss, dn_rs)
    done = own + jnp.sum(widen(dn_recv[...]), axis=0)
    done = jnp.concatenate([done, pltpu.roll(done, 64, 1)[0:16]], axis=0).astype(BF16)
    back = (row == (col & 7) * T + (col >> 3)).astype(F32).astype(BF16)
    out_hidden[...] = jnp.dot(back, done, preferred_element_type=F32)[:, 0:64].astype(BF16)

    left(dn_send, BLK - 1, dn_ss, dn_rs)


def handoff(hidden, kv, state, hidden_out, kv_out, state_out, sem):
    copies = [
        pltpu.make_async_copy(state.at[r], state_out.at[r], sem.at[2 + r]) for r in range(R)
    ]
    copies.append(pltpu.make_async_copy(kv, kv_out, sem.at[1]))
    copies.append(pltpu.make_async_copy(hidden, hidden_out, sem.at[0]))
    for copy in copies:
        copy.start()
    for copy in copies:
        copy.wait()


def body(
    hidden,
    attn_gain,
    ffn_gain,
    shared_weight,
    w_dt,
    dt_bias,
    a_log,
    d_skip,
    w_inner_x,
    w_inner_z,
    w_attn_out,
    w_ssm_out,
    w_gate,
    w_up,
    w_down,
    key_value_cache,
    cache_len,
    accepted,
    parked,
    source_slot,
):
    half = HEAD_SIZE // 2
    exponent = np.arange(128) % half * 2.0 / HEAD_SIZE
    freq = jnp.asarray(np.power(ROPE_THETA, -exponent).astype(np.float32).reshape(1, 128))
    anywhere = pl.BlockSpec(memory_space=pltpu.HBM)
    vm = pltpu.VMEM
    dma = pltpu.SemaphoreType.DMA
    shapes = (
        jax.ShapeDtypeStruct((ROWS, WIDTH // BLK), BF16),
        jax.ShapeDtypeStruct((T, R, 512), BF16),
        jax.ShapeDtypeStruct((R, CH, STATE), F32),
    )
    outs = pl.pallas_call(
        kernel,
        out_shape=tuple(vm(shape.shape, shape.dtype) for shape in shapes),
        in_specs=[anywhere] * 21,
        out_specs=(pl.BlockSpec(memory_space=vm),) * 3,
        scratch_shapes=[
            vm((ROWS, WIDTH), BF16),
            pltpu.SMEM((48,), F32),
            pltpu.SMEM((48,), F32),
            pltpu.SMEM((48,), F32),
            pltpu.SMEM((R,), jnp.int32),
            pltpu.SMEM((R,), jnp.int32),
            pltpu.SMEM((R * REQ,), jnp.int32),
            vm((STRIPS, 128), BF16),
            vm((STRIPS, 128), BF16),
            vm((1, 128), F32),
            vm((64, WIDTH), BF16),
            vm((128, WIDTH), BF16),
            vm((128, WIDTH), BF16),
            vm((128, WIDTH), BF16),
            vm((128, WIDTH), BF16),
            vm((WIDTH, 128), BF16),
            vm((WIDTH, 128), BF16),
            vm((128, WIDTH), BF16),
            vm((R, EXTENT, 512), BF16),
            vm((R, CH, STATE), F32),
            vm((STRIPS, ROWS, 128), F32),
            vm((BLK, 24, 128), BF16),
            vm((R * ROWS, 128), F32),
            vm((4, 128, 128), F32),
            vm((2, 64, 128), F32),
            vm((2, 64, 128), F32),
            vm((R * ROWS, 256), BF16),
            vm((R * ROWS, EXTENT + 128), F32),
            vm((R * ROWS, EXTENT + 128), BF16),
            vm((R * ROWS, 128), F32),
            vm((R * ROWS, 128), F32),
            vm((64, 128), F32),
            vm((128, 128), F32),
            vm((REQ, 2, CH, STATE), BF16),
            vm((REQ, 2, CH, STATE), BF16),
            vm((BLK, 16, 128), BF16),
            vm((BLK, 16, 128), BF16),
            vm((STRIPS, ROWS, 128), BF16),
            vm((BLK, ROWS, 128), BF16),
            vm((STRIPS, ROWS, 128), BF16),
            vm((BLK, 24, 128), BF16),
            vm((BLK, 24, 128), BF16),
            dma((20,)),
            dma((R,)),
            dma((1,)),
            dma((1,)),
            dma((1,)),
            dma((1,)),
            dma((1,)),
            dma((1,)),
            dma((1,)),
            dma((1,)),
            dma((1,)),
            dma((1,)),
            dma((1,)),
            dma((1,)),
        ],
        compiler_params=pltpu.CompilerParams(
            collective_id=0, has_side_effects=True, vmem_limit_bytes=63000000
        ),
        name="layer",
    )(
        hidden,
        attn_gain.reshape(STRIPS, 128),
        ffn_gain.reshape(STRIPS, 128),
        shared_weight.T,
        w_dt.T,
        w_inner_x.T,
        w_inner_z.T,
        w_attn_out,
        w_ssm_out,
        w_gate,
        w_up,
        w_down,
        key_value_cache,
        parked,
        freq,
        dt_bias,
        a_log,
        d_skip,
        cache_len,
        accepted,
        source_slot,
    )
    outs = pl.pallas_call(
        handoff,
        out_shape=shapes,
        in_specs=[pl.BlockSpec(memory_space=vm)] * 3,
        out_specs=(anywhere,) * 3,
        scratch_shapes=[dma((2 + R,))],
        compiler_params=pltpu.CompilerParams(vmem_limit_bytes=1000000),
        name="handoff",
    )(*outs)
    return outs[0], outs[1].transpose(1, 0, 2), outs[2]


def solution(mesh):
    placed = (
        P("req", None),
        P(),
        P(),
        P(None, "blk"),
        P(),
        P(),
        P(),
        P(),
        P(None, "blk"),
        P(None, "blk"),
        P("blk", None),
        P("blk", None),
        P(None, "blk"),
        P(None, "blk"),
        P("blk", None),
        P("req", "blk", None),
        P("req"),
        P("req"),
        P("req", "blk", None),
        P(),
    )
    return jax.shard_map(
        body,
        mesh=mesh,
        in_specs=placed,
        out_specs=(P("req", "blk"), P("req", None, None), P("req", "blk", None)),
        check_vma=False,
    )
```

```python
import math

import jax
import jax.numpy as jnp
import numpy as np
from jax import lax
from jax.experimental import pallas as pl
from jax.experimental.pallas import tpu as pltpu
from jax.sharding import PartitionSpec as P

HEADS = 8
HEAD_SIZE = 128
T = 5
R = 8
ROWS = R * T
BLK = 32
REQ = 8
WIDTH = 2048
STRIPS = WIDTH // 128
EXTENT = 512
CH = 96
STATE = 256
EPSILON = 1e-05
ROPE_THETA = 100000000000.0
NEGATIVE = -1e30
MESH = pl.DeviceIdType.MESH
F32 = jnp.float32
BF16 = jnp.bfloat16

NT = (((1,), (1,)), ((), ()))

FAR = sorted(
    [(dz, dx) for dz in range(8) for dx in range(4) if dz or dx],
    key=lambda o: -(min(o[0], 8 - o[0]) + min(o[1], 4 - o[1])),
)
FAR_EVEN = [o for o in FAR if (o[0] + o[1]) % 2 == 0]
FAR_ODD = [o for o in FAR if (o[0] + o[1]) % 2 == 1]


def iota(shape, dim):
    return lax.broadcasted_iota(jnp.int32, shape, dim)


def widen(values):
    return values.astype(F32)


def pack_pair(strip):
    lane = iota((24, 128), 1)
    top = strip[0:24]
    low = jnp.concatenate([strip[24:40], jnp.zeros((8, 128), F32)], axis=0)
    first = jnp.where(lane < 64, top, pltpu.roll(low, 64, 1))
    second = jnp.where(lane < 64, pltpu.roll(top, 64, 1), low)
    return first, second


def unpack_pair(first, second):
    lane = iota((24, 128), 1)
    top = jnp.where(lane < 64, first, pltpu.roll(second, 64, 1))
    low = jnp.where(lane < 64, pltpu.roll(first, 64, 1), second)
    return jnp.concatenate([top, low[0:16]], axis=0)


def kernel(
    hidden,
    attn_gain,
    ffn_gain,
    w_shared,
    w_dt,
    w_x,
    w_z,
    w_attn,
    w_ssm,
    w_gate,
    w_up,
    w_down,
    cache,
    parked,
    freq,
    dt_bias_h,
    a_log_h,
    d_skip_h,
    cache_len_h,
    accepted_h,
    slots_h,
    out_hidden,
    out_kv,
    out_state,
    hid_v,
    dt_bias,
    a_log,
    d_skip,
    cache_len,
    accepted,
    slots,
    ag_v,
    fg_v,
    fr_v,
    wsh_v,
    wdt_v,
    wx_v,
    wz_v,
    wmix_v,
    wg_v,
    wu_v,
    wd_v,
    kv_v,
    pk_v,
    hp_v,
    pj_v,
    q_v,
    nk_v,
    b_v,
    c_v,
    both_v,
    s_v,
    p_v,
    o_v,
    l_v,
    g_v,
    wst_v,
    st_send,
    st_recv,
    at_send,
    at_recv,
    mx_send,
    mx_recv,
    rs_v,
    dn_send,
    dn_recv,
    in_sem,
    kv_sem,
    st_ss,
    st_rs,
    pj_ss,
    pj_rs,
    at_ss,
    at_rs,
    mx_ss,
    mx_rs,
    rs_ss,
    rs_rs,
    dn_ss,
    dn_rs,
):
    g = lax.axis_index("req")
    me = lax.axis_index("blk")
    core = lax.rem(g, 2)

    def owner_of(e):
        return 2 * e + lax.rem(lax.div(e, 2) + core, 2)

    my_z = lax.div(me, 4)
    my_x = lax.rem(me, 4)

    planes = [lax.rem(my_z + dz, 8) * 4 for dz in range(8)]
    places = [lax.rem(my_x + dx, 4) for dx in range(4)]

    def at_offset(dz, dx):
        return planes[dz] + places[dx]

    owns = 1 - lax.rem(my_z + my_x + core, 2)
    my_e = lax.div(me, 2)
    parity = lax.rem(me, 2)
    is_owner = owns == 1

    def load(i, src, dst):
        copy = pltpu.make_async_copy(src, dst, in_sem.at[i])
        copy.start()
        return copy

    barrier = pltpu.get_barrier_semaphore()

    for offset in FAR:
        pl.semaphore_signal(
            barrier, inc=1, device_id=(g, at_offset(*offset)), device_id_type=MESH
        )

    def greet_req(k, carry):
        pl.semaphore_signal(
            barrier, inc=1, device_id=(lax.rem(g + k, REQ), me), device_id_type=MESH
        )
        return carry

    lax.fori_loop(1, REQ, greet_req, 0)

    c_hid = load(0, hidden, hid_v)
    c_ag = load(1, attn_gain, ag_v)
    c_wsh = load(2, w_shared, wsh_v)
    c_small = [
        load(14, slots_h, slots),
        load(15, cache_len_h, cache_len),
        load(16, accepted_h, accepted),
        load(17, dt_bias_h, dt_bias),
        load(18, a_log_h, a_log),
        load(19, d_skip_h, d_skip),
    ]
    c_pk = load(3, parked, pk_v)
    c_wx = load(4, w_x, wx_v.at[pl.ds(0, CH)])
    c_wz = load(5, w_z, wz_v.at[pl.ds(0, CH)])
    c_wdt = load(6, w_dt, wdt_v.at[pl.ds(0, 48)])
    c_fr = load(7, freq, fr_v)
    c_kv = []
    for r in range(R):
        copy = pltpu.make_async_copy(cache.at[r], kv_v.at[r], kv_sem.at[r])
        copy.start()
        c_kv.append(copy)
    c_ws = load(8, w_ssm, wmix_v.at[pl.ds(0, CH)])
    c_wa = load(9, w_attn, wmix_v.at[pl.ds(CH, 32)])
    c_fg = load(10, ffn_gain, fg_v)
    c_wg = load(11, w_gate, wg_v)
    c_wu = load(12, w_up, wu_v)
    c_wd = load(13, w_down, wd_v)

    c_hid.wait()
    c_ag.wait()
    row = iota((ROWS, ROWS), 0)
    col = iota((ROWS, ROWS), 1)
    place = (col == (row & 7) * T + (row >> 3)).astype(F32).astype(BF16)
    hid = jnp.dot(place, hid_v[...], preferred_element_type=F32)
    scaling = lax.rsqrt(jnp.sum(hid * hid, axis=1, keepdims=True) * (1.0 / WIDTH) + EPSILON)
    gain = widen(ag_v[...])
    hid_strips = [hid[:, 128 * e : 128 * (e + 1)] for e in range(STRIPS)]
    normed = jnp.concatenate(
        [(hid_strips[e] * scaling * gain[e : e + 1]).astype(BF16) for e in range(STRIPS)], axis=1
    )
    c_wsh.wait()
    part = lax.dot_general(normed, wsh_v[...], NT, preferred_element_type=F32)
    twice = jnp.concatenate([part, part], axis=1)
    low = jnp.concatenate([twice[24:40], jnp.zeros((8, 128), F32)], axis=0)
    pj_v[me] = jnp.where(iota((24, 128), 1) < 64, twice[0:24], low).astype(BF16)

    pl.semaphore_wait(barrier, BLK - 1 + REQ - 1)

    def blk_copy(src, dst, send, recv, target):
        return pltpu.make_async_remote_copy(
            src_ref=src,
            dst_ref=dst,
            send_sem=send,
            recv_sem=recv,
            device_id=(g, target),
            device_id_type=MESH,
        )

    def arrived(buffer, count, send, recv):
        blocks = buffer.at[pl.ds(0, count)]
        blk_copy(blocks, blocks, send.at[0], recv.at[0], at_offset(0, 1)).wait_recv()

    def left(buffer, count, send, recv):
        blocks = buffer.at[pl.ds(0, count)]
        blk_copy(blocks, blocks, send.at[0], recv.at[0], at_offset(0, 1)).wait_send()

    def pj_copy(k):
        return blk_copy(
            pj_v.at[me], pj_v.at[me], pj_ss.at[0], pj_rs.at[0], at_offset(*FAR[k])
        )

    for k in range(BLK - 1):
        pj_copy(k).start()

    for copy in c_small:
        copy.wait()
    c_pk.wait()

    def st_copy(k):
        target = lax.rem(g + k, REQ)
        return pltpu.make_async_remote_copy(
            src_ref=st_send.at[k],
            dst_ref=st_recv.at[g],
            send_sem=st_ss.at[0],
            recv_sem=st_rs.at[0],
            device_id=(target, me),
            device_id_type=MESH,
        )

    def st_push(k, carry):
        target = lax.rem(g + k, REQ)
        found = jnp.int32(0)
        picks = [jnp.int32(0), jnp.int32(0)]
        for i in range(2, R):
            slot = slots[target * R + i]
            mine = (slot >> 3) == g
            picks[0] = jnp.where(mine & (found == 0), slot & 7, picks[0])
            picks[1] = jnp.where(mine & (found == 1), slot & 7, picks[1])
            found = found + mine.astype(jnp.int32)
        for c in range(2):
            st_send[k, c] = pk_v[picks[c]].astype(BF16)
        st_copy(k).start()
        return carry

    lax.fori_loop(1, REQ, st_push, 0)

    for e in range(STRIPS):
        hp_v[e] = hid_strips[e]
    wx_v[CH:128] = jnp.zeros((128 - CH, WIDTH), BF16)
    wz_v[CH:128] = jnp.zeros((128 - CH, WIDTH), BF16)
    wdt_v[48:128] = jnp.zeros((80, WIDTH), BF16)
    c_wx.wait()
    inner_x = lax.dot_general(normed, wx_v[...], NT, preferred_element_type=F32)
    c_wz.wait()
    inner_z = lax.dot_general(normed, wz_v[...], NT, preferred_element_type=F32)
    c_wdt.wait()
    dt = lax.dot_general(normed, wdt_v[...], NT, preferred_element_type=F32)

    head0 = lax.div(me * CH, 64)
    cut = 64 - lax.rem(me * CH, 64)
    lane1 = iota((1, 128), 1)
    lane = iota((ROWS, 128), 1)

    def by_head(ref):
        return jnp.where(lane1 < cut, ref[head0], ref[head0 + 1])

    dt0 = jnp.sum(jnp.where(lane == head0, dt, 0.0), axis=1, keepdims=True)
    dt1 = jnp.sum(jnp.where(lane == head0 + 1, dt, 0.0), axis=1, keepdims=True)
    raw = jnp.where(lane < cut, dt0, dt1) + by_head(dt_bias)
    steps = jnp.maximum(raw, 0.0) + jnp.log1p(jnp.exp(-jnp.abs(raw)))
    rate = -jnp.exp(by_head(a_log))
    skip = by_head(d_skip)

    c_fr.wait()
    sub24 = iota((24, 128), 0)
    lane24 = iota((24, 128), 1)
    base = jnp.zeros((24, 128), jnp.int32)
    for r in range(R):
        base = jnp.where((sub24 & 7) == r, cache_len[r], base)
    spot = base + (sub24 >> 3) + jnp.where(lane24 < 64, 0, 3)
    angle = spot.astype(F32) * fr_v[...]
    cosine = jnp.cos(angle)
    sine = jnp.sin(angle)

    nk_v[:, 40:128, :] = jnp.zeros((4, 88, 128), F32)
    b_v[:, 40:64, :] = jnp.zeros((2, 24, 128), F32)
    c_v[:, 40:64, :] = jnp.zeros((2, 24, 128), F32)

    arrived(pj_v, BLK - 1, pj_ss, pj_rs)

    def rotated(i):
        first = widen(pj_v[i])
        second = widen(pj_v[i + 1])
        return unpack_pair(
            first * cosine - second * sine, second * cosine + first * sine
        )

    def plain(i):
        return unpack_pair(widen(pj_v[i]), widen(pj_v[i + 1]))

    for h in range(HEADS):
        rows = rotated(2 * h)
        for t in range(T):
            q_v[pl.ds(t * 8 + h, R, stride=ROWS), :] = rows[8 * t : 8 * t + 8]
    for j in range(2):
        nk_v[j, 0:ROWS, :] = rotated(16 + 2 * j)
        nk_v[2 + j, 0:ROWS, :] = plain(20 + 2 * j)
        b_v[j, 0:ROWS, :] = plain(24 + 2 * j)
        c_v[j, 0:ROWS, :] = plain(28 + 2 * j)

    acc_col = jnp.zeros((8, 128), jnp.int32)
    sub8 = iota((8, 128), 0)
    for r in range(R):
        acc_col = jnp.where(sub8 == r, accepted[r], acc_col)
    for t in range(T):
        for j in range(4):
            rows = nk_v[j, 8 * t : 8 * t + 8, :]
            out_kv[t, :, 128 * j : 128 * (j + 1)] = jnp.where(acc_col > t, rows, 0.0).astype(BF16)

    sub40 = iota((ROWS, 128), 0)
    group0 = (sub40 & 7) < 4
    spots = iota((ROWS, EXTENT), 1)
    for r in range(R):
        query = q_v[ROWS * r : ROWS * (r + 1), :]
        both_v[ROWS * r : ROWS * (r + 1), :] = jnp.concatenate(
            [jnp.where(group0, query, 0.0), jnp.where(group0, 0.0, query)], axis=1
        ).astype(BF16)
    new_keys = jnp.concatenate([nk_v[0], nk_v[1]], axis=1).astype(BF16)
    new_scores = lax.dot_general(both_v[...], new_keys, NT, preferred_element_type=F32)
    lanes = iota((ROWS, 128), 1)
    in_order = ((lanes >> 3) <= (sub40 >> 3)) & (me == 0)
    for r in range(R):
        c_kv[r].wait()
        rows = slice(ROWS * r, ROWS * (r + 1))
        scores = lax.dot_general(
            both_v[rows, :], kv_v[r, :, 0:256], NT, preferred_element_type=F32
        )
        s_v[rows, 0:EXTENT] = jnp.where(spots < cache_len[r] - me * EXTENT, scores, NEGATIVE)
        s_v[rows, EXTENT : EXTENT + 128] = jnp.where(
            in_order & ((lanes & 7) == r), new_scores[rows, :], NEGATIVE
        )
    scale = HEAD_SIZE**-0.5
    totals = []
    peaks = []
    for r in range(R):
        rows = slice(ROWS * r, ROWS * (r + 1))
        scores = s_v[rows, :]
        peak = jnp.max(scores, axis=1, keepdims=True)
        weights = jnp.exp2((scores - peak) * (scale * math.log2(math.e)))
        totals.append(jnp.sum(weights, axis=1, keepdims=True))
        peaks.append(peak)
        p_v[rows, :] = weights.astype(BF16)
    new_values = jnp.concatenate([nk_v[2], nk_v[3]], axis=1).astype(BF16)
    new_mixed = jnp.dot(
        p_v[:, EXTENT : EXTENT + 128], new_values, preferred_element_type=F32
    )
    for r in range(R):
        rows = slice(ROWS * r, ROWS * (r + 1))
        mixed = new_mixed[rows, :] + jnp.dot(
            p_v[rows, 0:EXTENT], kv_v[r, :, 256:512], preferred_element_type=F32
        )
        mixed = jnp.where(group0, mixed[:, 0:128], mixed[:, 128:256])
        o_v[rows, :] = mixed / totals[r]
        level = jnp.where(
            peaks[r] > NEGATIVE, peaks[r] * scale + jnp.log(totals[r]), NEGATIVE
        )
        l_v[rows, :] = jnp.broadcast_to(level, (ROWS, 128))

    lane8 = iota((8, 128), 1)
    for h in range(HEADS):
        outs = [o_v[pl.ds(t * 8 + h, R, stride=ROWS), :] for t in range(T)]
        stats = jnp.zeros((8, 128), F32)
        for t in range(T):
            level = l_v[pl.ds(t * 8 + h, R, stride=ROWS), :]
            high = widen(level.astype(BF16))
            middle = widen((level - high).astype(BF16))
            rest = level - high - middle
            stats = jnp.where(lane8 == 32 + t, high, stats)
            stats = jnp.where(lane8 == 40 + t, middle, stats)
            stats = jnp.where(lane8 == 48 + t, rest, stats)
        for q in range(4):
            first = outs[0] if q == 0 else pltpu.roll(outs[0], 128 - 32 * q, 1)
            for j in range(1, 4):
                shift = (32 * (j - q)) % 128
                moved = pltpu.roll(outs[j], shift, 1) if shift else outs[j]
                first = jnp.where(lane8 >= 32 * j, moved, first)
            last = pltpu.roll(outs[4], 128 - 32 * q, 1) if q else outs[4]
            second = jnp.where(lane8 < 32, last, stats)
            at_send[4 * h + q] = jnp.concatenate([first, second], axis=0).astype(BF16)

    def at_copy(k):
        target = at_offset(*FAR[k])
        return blk_copy(at_send.at[target], at_recv.at[me], at_ss.at[0], at_rs.at[0], target)

    for k in range(BLK - 1):
        at_copy(k).start()
    at_recv[me] = at_send[me]

    arrived(st_recv, REQ - 1, st_ss, st_rs)

    step_t = [steps[8 * t : 8 * t + 8] for t in range(T)]
    x_t = [inner_x[8 * t : 8 * t + 8] for t in range(T)]
    dx_t = [step_t[t] * x_t[t] for t in range(T)]
    run_t = [step_t[0]]
    for t in range(1, T):
        run_t.append(run_t[-1] + step_t[t])
    at_accept = jnp.zeros((8, 128), F32)
    for t in range(T):
        at_accept = jnp.where(acc_col == t + 1, run_t[t], at_accept)
    wst_v[...] = jnp.zeros((128, 128), F32)
    for u in range(T):
        past = jnp.where(acc_col > u, rate * (at_accept - run_t[u]), NEGATIVE)
        weight = jnp.exp(past) * dx_t[u]
        wst_v[8 * u : 8 * u + 8, :] = weight
        wst_v[64 + 8 * u : 72 + 8 * u, :] = weight - widen(weight.astype(BF16))
    wst_v[40:48, :] = jnp.exp(rate * at_accept)
    turned = wst_v[...].T
    turned_low = turned[0:CH].astype(BF16)

    b_rows = jnp.concatenate([b_v[0], b_v[1]], axis=1)
    sub64 = iota((64, STATE), 0) & 7
    owners = []
    for r in range(2, R):
        slot = slots[g * R + r]
        own = slot >> 3
        rank = jnp.int32(0)
        for other in owners:
            rank = rank + (other == own).astype(jnp.int32)
        owners.append(own)
    for r in range(R):
        if r < 2:
            start = pk_v[slots[g * R + r] & 7]
        else:
            own = owners[r - 2]
            rank = jnp.int32(0)
            for other in owners[: r - 2]:
                rank = rank + (other == own).astype(jnp.int32)
            start = widen(st_recv[own, jnp.minimum(rank, 1)])
        c_rows = jnp.concatenate(
            [c_v[0, pl.ds(r, 8, stride=8), :], c_v[1, pl.ds(r, 8, stride=8), :]], axis=1
        )
        g_v[8 * r : 8 * r + 8, 0:CH] = lax.dot_general(
            c_rows.astype(BF16), start.astype(BF16), NT, preferred_element_type=F32
        )
        b_mine = jnp.where(sub64 == r, b_rows, 0.0)
        b_twice = jnp.concatenate([b_mine, b_mine], axis=0).astype(BF16)
        grown = jnp.dot(turned_low, b_twice, preferred_element_type=F32)
        out_state[r] = turned[0:CH, 40 + r : 41 + r] * start + grown

    gated_t = []
    for t in range(T):
        y = jnp.exp(rate * run_t[t]) * g_v[pl.ds(t, R, stride=8), :] + skip * x_t[t]
        for u in range(t + 1):
            match = jnp.zeros((8, 1), F32)
            for j in range(2):
                match = match + jnp.sum(
                    c_v[j, 8 * t : 8 * t + 8, :] * b_v[j, 8 * u : 8 * u + 8, :],
                    axis=1,
                    keepdims=True,
                )
            kept = dx_t[u] if u == t else jnp.exp(rate * (run_t[t] - run_t[u])) * dx_t[u]
            y = y + match * kept
        z = inner_z[8 * t : 8 * t + 8]
        gated_t.append(y * (z * (1.0 / (1.0 + jnp.exp(-z)))))

    arrived(at_recv, BLK - 1, at_ss, at_rs)
    parts = widen(at_recv[...])
    stats = parts[:, 8:16, :].reshape(BLK * 8, 128).astype(BF16)
    from_lane = iota((128, 256), 0)
    to_time = iota((128, 256), 1) >> 5
    to_time = jnp.minimum(to_time, 4)
    spread = (
        (from_lane == 32 + to_time) | (from_lane == 40 + to_time) | (from_lane == 48 + to_time)
    )
    level = jnp.dot(
        stats, spread.astype(F32).astype(BF16), preferred_element_type=F32
    ).reshape(BLK, 8, 256)
    top = jnp.max(level, axis=0, keepdims=True)
    share = jnp.exp(level - top)
    values = jnp.concatenate([parts[:, 0:8, :], parts[:, 8:16, :]], axis=2)
    merged = jnp.sum(share * values, axis=0) / jnp.sum(share, axis=0)
    mix_t = []
    for t in range(T):
        piece = merged[:, 0:128] if t < 4 else merged[:, 128:256]
        shift = (96 - 32 * t) % 128 if t < 4 else 96
        moved = pltpu.roll(piece, shift, 1) if shift else piece
        mix_t.append(jnp.where(lane8 < CH, gated_t[t], moved))
    mix_in = jnp.concatenate(mix_t, axis=0).astype(BF16)

    c_ws.wait()
    c_wa.wait()
    for e in range(0, STRIPS, 2):
        pair = jnp.dot(
            mix_in, wmix_v[:, 128 * e : 128 * (e + 2)], preferred_element_type=F32
        ).astype(BF16)
        mx_send[e] = pair[:, 0:128]
        mx_send[e + 1] = pair[:, 128:256]

    def mx_copy(k):
        odd = FAR_ODD[k]
        even = FAR_EVEN[k] if k < STRIPS - 1 else odd
        target = at_offset(*odd) + owns * (at_offset(*even) - at_offset(*odd))
        return blk_copy(
            mx_send.at[lax.div(target, 2)], mx_recv.at[me], mx_ss.at[0], mx_rs.at[0], target
        )

    for k in range(STRIPS - 1):
        mx_copy(k).start()

    @pl.when(jnp.logical_not(is_owner))
    def _():
        mx_copy(STRIPS - 1).start()

    def rs_copy(k):
        return blk_copy(
            rs_v.at[my_e], rs_v.at[my_e], rs_ss.at[0], rs_rs.at[0], at_offset(*FAR[k])
        )

    @pl.when(is_owner)
    def _():
        mx_recv[me] = mx_send[my_e]
        arrived(mx_recv, BLK - 1, mx_ss, mx_rs)
        total = jnp.sum(widen(mx_recv[...]), axis=0)
        rs_v[my_e] = (hp_v[my_e] + total).astype(BF16)

        for k in range(BLK - 1):
            rs_copy(k).start()

    c_fg.wait()
    c_wg.wait()
    c_wu.wait()
    c_wd.wait()

    @pl.when(is_owner)
    def _():
        arrived(rs_v, STRIPS - 1, rs_ss, rs_rs)

    @pl.when(jnp.logical_not(is_owner))
    def _():
        arrived(rs_v, STRIPS, rs_ss, rs_rs)


    resid = [widen(rs_v[e]) for e in range(STRIPS)]
    squares = resid[0] * resid[0]
    for e in range(1, STRIPS):
        squares = squares + resid[e] * resid[e]
    scaling2 = lax.rsqrt(jnp.sum(squares, axis=1, keepdims=True) * (1.0 / WIDTH) + EPSILON)
    gain2 = widen(fg_v[...])
    normed2 = jnp.concatenate(
        [(resid[e] * scaling2 * gain2[e : e + 1]).astype(BF16) for e in range(STRIPS)], axis=1
    )
    gate = jnp.dot(normed2, wg_v[...], preferred_element_type=F32)
    up = jnp.dot(normed2, wu_v[...], preferred_element_type=F32)
    inner = (gate * (1.0 / (1.0 + jnp.exp(-gate))) * up).astype(BF16)
    for e in range(0, STRIPS, 2):
        pair = jnp.dot(inner, wd_v[:, 128 * e : 128 * (e + 2)], preferred_element_type=F32)
        for i in range(2):
            first, second = pack_pair(pair[:, 128 * i : 128 * (i + 1)])
            dn_send[2 * (e + i)] = first.astype(BF16)
            dn_send[2 * (e + i) + 1] = second.astype(BF16)

    def dn_copy(k):
        target = at_offset(*FAR[k])
        return blk_copy(dn_send.at[target], dn_recv.at[me], dn_ss.at[0], dn_rs.at[0], target)

    for k in range(BLK - 1):
        dn_copy(k).start()
    dn_recv[me] = dn_send[me]
    own_even, own_odd = pack_pair(widen(rs_v[my_e]))
    own = jnp.where(parity == 0, own_even, own_odd)

    left(pj_v, BLK - 1, pj_ss, pj_rs)
    left(st_send, REQ - 1, st_ss, st_rs)
    left(at_send, BLK - 1, at_ss, at_rs)

    @pl.when(is_owner)
    def _():
        left(mx_send, STRIPS - 1, mx_ss, mx_rs)
        left(mx_recv, BLK - 1, rs_ss, rs_rs)

    @pl.when(jnp.logical_not(is_owner))
    def _():
        left(mx_send, STRIPS, mx_ss, mx_rs)

    arrived(dn_recv, BLK - 1, dn_ss, dn_rs)
    done = own + jnp.sum(widen(dn_recv[...]), axis=0)
    done = jnp.concatenate([done, pltpu.roll(done, 64, 1)[0:16]], axis=0).astype(BF16)
    back = (row == (col & 7) * T + (col >> 3)).astype(F32).astype(BF16)
    out_hidden[...] = jnp.dot(back, done, preferred_element_type=F32)[:, 0:64].astype(BF16)

    left(dn_send, BLK - 1, dn_ss, dn_rs)


def handoff(hidden, kv, state, hidden_out, kv_out, state_out, sem):
    copies = [
        pltpu.make_async_copy(state.at[r], state_out.at[r], sem.at[2 + r]) for r in range(R)
    ]
    copies.append(pltpu.make_async_copy(kv, kv_out, sem.at[1]))
    copies.append(pltpu.make_async_copy(hidden, hidden_out, sem.at[0]))
    for copy in copies:
        copy.start()
    for copy in copies:
        copy.wait()


def body(
    hidden,
    attn_gain,
    ffn_gain,
    shared_weight,
    w_dt,
    dt_bias,
    a_log,
    d_skip,
    w_inner_x,
    w_inner_z,
    w_attn_out,
    w_ssm_out,
    w_gate,
    w_up,
    w_down,
    key_value_cache,
    cache_len,
    accepted,
    parked,
    source_slot,
):
    half = HEAD_SIZE // 2
    exponent = np.arange(128) % half * 2.0 / HEAD_SIZE
    freq = jnp.asarray(np.power(ROPE_THETA, -exponent).astype(np.float32).reshape(1, 128))
    anywhere = pl.BlockSpec(memory_space=pltpu.HBM)
    vm = pltpu.VMEM
    dma = pltpu.SemaphoreType.DMA
    shapes = (
        jax.ShapeDtypeStruct((ROWS, WIDTH // BLK), BF16),
        jax.ShapeDtypeStruct((T, R, 512), BF16),
        jax.ShapeDtypeStruct((R, CH, STATE), F32),
    )
    outs = pl.pallas_call(
        kernel,
        out_shape=tuple(vm(shape.shape, shape.dtype) for shape in shapes),
        in_specs=[anywhere] * 21,
        out_specs=(pl.BlockSpec(memory_space=vm),) * 3,
        scratch_shapes=[
            vm((ROWS, WIDTH), BF16),
            pltpu.SMEM((48,), F32),
            pltpu.SMEM((48,), F32),
            pltpu.SMEM((48,), F32),
            pltpu.SMEM((R,), jnp.int32),
            pltpu.SMEM((R,), jnp.int32),
            pltpu.SMEM((R * REQ,), jnp.int32),
            vm((STRIPS, 128), BF16),
            vm((STRIPS, 128), BF16),
            vm((1, 128), F32),
            vm((64, WIDTH), BF16),
            vm((128, WIDTH), BF16),
            vm((128, WIDTH), BF16),
            vm((128, WIDTH), BF16),
            vm((128, WIDTH), BF16),
            vm((WIDTH, 128), BF16),
            vm((WIDTH, 128), BF16),
            vm((128, WIDTH), BF16),
            vm((R, EXTENT, 512), BF16),
            vm((R, CH, STATE), F32),
            vm((STRIPS, ROWS, 128), F32),
            vm((BLK, 24, 128), BF16),
            vm((R * ROWS, 128), F32),
            vm((4, 128, 128), F32),
            vm((2, 64, 128), F32),
            vm((2, 64, 128), F32),
            vm((R * ROWS, 256), BF16),
            vm((R * ROWS, EXTENT + 128), F32),
            vm((R * ROWS, EXTENT + 128), BF16),
            vm((R * ROWS, 128), F32),
            vm((R * ROWS, 128), F32),
            vm((64, 128), F32),
            vm((128, 128), F32),
            vm((REQ, 2, CH, STATE), BF16),
            vm((REQ, 2, CH, STATE), BF16),
            vm((BLK, 16, 128), BF16),
            vm((BLK, 16, 128), BF16),
            vm((STRIPS, ROWS, 128), BF16),
            vm((BLK, ROWS, 128), BF16),
            vm((STRIPS, ROWS, 128), BF16),
            vm((BLK, 24, 128), BF16),
            vm((BLK, 24, 128), BF16),
            dma((20,)),
            dma((R,)),
            dma((1,)),
            dma((1,)),
            dma((1,)),
            dma((1,)),
            dma((1,)),
            dma((1,)),
            dma((1,)),
            dma((1,)),
            dma((1,)),
            dma((1,)),
            dma((1,)),
            dma((1,)),
        ],
        compiler_params=pltpu.CompilerParams(
            collective_id=0, has_side_effects=True, vmem_limit_bytes=63000000
        ),
        name="layer",
    )(
        hidden,
        attn_gain.reshape(STRIPS, 128),
        ffn_gain.reshape(STRIPS, 128),
        shared_weight.T,
        w_dt.T,
        w_inner_x.T,
        w_inner_z.T,
        w_attn_out,
        w_ssm_out,
        w_gate,
        w_up,
        w_down,
        key_value_cache,
        parked,
        freq,
        dt_bias,
        a_log,
        d_skip,
        cache_len,
        accepted,
        source_slot,
    )
    outs = pl.pallas_call(
        handoff,
        out_shape=shapes,
        in_specs=[pl.BlockSpec(memory_space=vm)] * 3,
        out_specs=(anywhere,) * 3,
        scratch_shapes=[dma((2 + R,))],
        compiler_params=pltpu.CompilerParams(vmem_limit_bytes=1000000),
        name="handoff",
    )(*outs)
    return outs[0], outs[1].transpose(1, 0, 2), outs[2]


def solution(mesh):
    placed = (
        P("req", None),
        P(),
        P(),
        P(None, "blk"),
        P(),
        P(),
        P(),
        P(),
        P(None, "blk"),
        P(None, "blk"),
        P("blk", None),
        P("blk", None),
        P(None, "blk"),
        P(None, "blk"),
        P("blk", None),
        P("req", "blk", None),
        P("req"),
        P("req"),
        P("req", "blk", None),
        P(),
    )
    return jax.shard_map(
        body,
        mesh=mesh,
        in_specs=placed,
        out_specs=(P("req", "blk"), P("req", None, None), P("req", "blk", None)),
        check_vma=False,
    )
```
